32 devices in a mesh: scen: 8 (over z, y), rows: 2 (over x), section: 2 (over core).
Axes of the slice: x: 2, y: 2, z: 4, core: 2. Of those that a mesh axis runs over, the one named last changes fastest.
Arguments:
- lp_blocks: bfloat16 [192, 2, 4, 2, 128, 128], P('scen', 'rows', 'section'), may hold values from -0.1875 to 0.1875
- block_columns: int32 [192, 2, 4, 2], P('scen', None, 'section'), may hold values from 0 to 175
- scenario_nodes: int32 [3, 192], P(None, 'scen'), may hold values from 0 to 511, as said below
- scenario_weights: float32 [192], P('scen'), may hold values from 0.5 to 4.5
- cost: bfloat16 [192, 4, 22528], P('scen', 'section'), may hold values from -6 to 6
- bounds_rhs: float32 [192, 256], P('scen', 'rows'), may hold values from -6 to 6
- primal_start: bfloat16 [192, 4, 22528], P('scen', 'section'), may hold values from 0 to 2
- dual_start: float32 [192, 256], P('scen', 'rows'), may hold values from 0 to 1
- multiplier_start: float32 [192, 4, 512], P('scen', 'section'), may hold values from -3 to 3
- consensus_start: float32 [585, 512], replicated, may hold values from 0 to 2
Outputs:
- primal: float32 [192, 4, 22528], P('scen', 'section')
- dual: float32 [192, 256], P('scen', 'rows')
- multiplier: float32 [192, 4, 512], P('scen', 'section')
- penalty: float32 [], replicated
The draws below stay inside these ranges and needn't reach their ends.
Inputs may be any that keep to these rules, and one draw needn't show every extreme that they name: `scenario_nodes`: node ids never fall from one scenario to the next at any section; the section-three node is the section-four node // 8 and the section-two node the section-three node // 8; the first scenario lies in node 0 and the last in node 511 of section four.
All inputs are finite; a program needn't handle non-finite values.
Results may differ from the reference program's by a relative error of at most 0.0018.
Values sent between devices are 32-bit elements; how exact they have to be, the bound alone decides.
No kernel may reach another device: no remote copies, remote signals or barrier semaphores. Data moves between devices by JAX's collectives and lax.ppermute only.
A program may use at most 128 MiB of HBM per device.

```python
import jax
import jax.numpy as jnp
from jax import lax

S_DEV = 24
BLK = 128
CPS = 176
NZ = 2
SECTIONS = 4
N1 = 8
BR = 8
SWEEPS = 2
SCEN = 192
RB = 2
ROWS = 256
COLS = 22528
HCOLS = 512
N2 = 64
N3 = 512
NODES = 585
N_SCEN = 8


def draw_scenario_nodes(key, part):
    first = jax.random.randint(jax.random.fold_in(key, 11), (SCEN,), 0, N3)
    second = jax.random.randint(jax.random.fold_in(key, 12), (SCEN,), 0, N3)
    leaves = jnp.sort(jnp.minimum(first, second))
    leaves = leaves.at[0].set(0).at[SCEN - 1].set(N3 - 1)
    middle = leaves // BR
    upper = middle // BR
    return jnp.stack([upper, middle, leaves]).astype(jnp.int32)


def draw_scenario_weights(key, part):
    ramp = jnp.arange(SCEN, dtype=jnp.float32) / max(SCEN - 1, 1)
    factor = jax.random.uniform(jax.random.fold_in(key, 22), (SCEN,), jnp.float32, 0.5, 1.5)
    return ((1.0 + 2.0 * ramp) * factor).astype(jnp.float32)


def with_ends(drawn, own_key, least, top_value):
    place = [jax.random.randint(jax.random.fold_in(own_key, axis), (), 0, length) for axis, length in enumerate(drawn.shape)]
    main_axis = drawn.shape.index(max(drawn.shape))
    neighbour = place[:main_axis] + [(place[main_axis] + 1) % drawn.shape[main_axis]] + place[main_axis + 1:]
    return drawn.at[tuple(place)].set(least).at[tuple(neighbour)].set(top_value)


def block_scale(stream_key, dims, shards, smallest, top_value):
    loudness, own = 1.0, jax.random.fold_in(stream_key, 6)
    for position, blocks in shards:
        heights = jnp.exp(jax.random.uniform(jax.random.fold_in(own, position), (blocks,), jnp.float32, smallest / len(shards), top_value / len(shards)))
        loudness = loudness * jnp.repeat(heights, dims[position] // blocks).reshape([-1 if axis == position else 1 for axis in range(len(dims))])
    return loudness


def bell_draw(own_key, dims, deviation, limit, cuts=(), kind=jnp.bfloat16):
    values = deviation * jax.random.normal(own_key, dims, jnp.float32)
    if cuts:
        values = values * block_scale(own_key, dims, cuts, -0.22, 0.18)
    return jnp.clip(values, -limit, limit).astype(kind)


def setup_inputs(seed: int = 0) -> dict:
    seeds = jax.random.split(jax.random.key(seed), 11)
    lp_blocks = bell_draw(seeds[0], (SCEN, RB, SECTIONS, NZ, BLK, BLK), (SECTIONS * NZ * BLK) ** -0.5, 0.1875, ((0, 8), (1, 2), (2, 2)))
    block_columns = with_ends(jax.random.randint(seeds[1], (SCEN, RB, SECTIONS, NZ), 0, CPS), jax.random.fold_in(seeds[1], 1), 0, CPS - 1).astype(jnp.int32)
    scenario_nodes = draw_scenario_nodes(jax.random.fold_in(seeds[10], 71), 0)
    scenario_weights = draw_scenario_weights(jax.random.fold_in(seeds[10], 71), 0)
    cost = bell_draw(seeds[4], (SCEN, SECTIONS, COLS), 1.0, 6.0, ((0, 8), (1, 2)))
    bounds_rhs = bell_draw(seeds[5], (SCEN, ROWS), 1.0, 6.0, ((0, 8), (1, 2)), jnp.float32)
    primal_start = jnp.clip(2.0 * jax.random.uniform(seeds[6], (SCEN, SECTIONS, COLS), jnp.float32) ** block_scale(seeds[6], (SCEN, SECTIONS, COLS), ((0, 8), (1, 2)), -0.2, 0.2), 0.0, 2.0).astype(jnp.bfloat16)
    dual_start = jnp.clip(1.0 * jax.random.uniform(seeds[7], (SCEN, ROWS), jnp.float32) ** block_scale(seeds[7], (SCEN, ROWS), ((0, 8), (1, 2)), -0.2, 0.2), 0.0, 1.0)
    multiplier_start = bell_draw(seeds[8], (SCEN, SECTIONS, HCOLS), 0.5, 3.0, ((0, 8), (1, 2)), jnp.float32)
    consensus_start = jnp.clip(jax.random.uniform(seeds[9], (NODES, HCOLS), jnp.float32, 0.0, 2.0), 0.0, 2.0)
    return {"lp_blocks": lp_blocks, "block_columns": block_columns, "scenario_nodes": scenario_nodes, "scenario_weights": scenario_weights, "cost": cost, "bounds_rhs": bounds_rhs, "primal_start": primal_start, "dual_start": dual_start, "multiplier_start": multiplier_start, "consensus_start": consensus_start}


TAU_STEP = 0.4
SIGMA_STEP = 0.4
RHO_START = 1.0
EPSILON = 1e-06

def averaged(node_table, node_mass):
    positive = node_mass > 0
    safe_mass = jnp.where(positive, node_mass, 1.0)
    return jnp.where(positive[:, None], node_table / safe_mass[:, None], 0.0)

def selector_of(block_columns):
    return (block_columns[..., None] == jnp.arange(CPS, dtype=jnp.int32)).astype(jnp.float32)

def group_forward(pieces):
    matrices, columns, vector = pieces
    picked = jnp.einsum('srjnc,sjcb->srjnb', selector_of(columns), vector.astype(jnp.float32), precision=lax.Precision.HIGHEST)
    return jnp.einsum('srjnab,srjnb->sra', matrices.astype(jnp.float32), picked, precision=lax.Precision.HIGHEST)

def group_adjoint(pieces):
    matrices, columns, vector = pieces
    parts = jnp.einsum('srjnab,sra->srjnb', matrices.astype(jnp.float32), vector.astype(jnp.float32), precision=lax.Precision.HIGHEST)
    return jnp.einsum('srjnc,srjnb->sjcb', selector_of(columns), parts, precision=lax.Precision.HIGHEST)

def reference(lp_blocks, block_columns, scenario_nodes, scenario_weights, cost, bounds_rhs, primal_start, dual_start, multiplier_start, consensus_start):
    offsets = jnp.array([1, 1 + N1, 1 + N1 + N2], jnp.int32)
    node_rows = jnp.concatenate([jnp.zeros((1, SCEN), jnp.int32), (scenario_nodes + offsets[:, None]).astype(jnp.int32)], axis=0)
    matrix_groups = lp_blocks.reshape((N_SCEN, S_DEV) + lp_blocks.shape[1:])
    column_groups = block_columns.reshape((N_SCEN, S_DEV) + block_columns.shape[1:])
    cost_full = cost.astype(jnp.float32)

    def spread_nodes(table):
        return jnp.stack([table[node_rows[section_id]] for section_id in range(SECTIONS)], axis=1)

    def node_sums(values):
        total = jnp.zeros((NODES,) + values.shape[2:], jnp.float32)
        for section_id in range(SECTIONS):
            total = total + jax.ops.segment_sum(values[:, section_id], node_rows[section_id], num_segments=NODES)
        return total
    node_mass = node_sums(scenario_weights[:, None] * jnp.ones((SCEN, SECTIONS), jnp.float32))
    penalty = jnp.asarray(RHO_START, jnp.float32)
    primal = primal_start.astype(jnp.float32)
    dual, multiplier, previous = (dual_start, multiplier_start, consensus_start)
    for sweep_index in range(SWEEPS):
        anchors = spread_nodes(previous)
        dual_half = dual.astype(jnp.bfloat16).reshape(N_SCEN, S_DEV, RB, BLK)
        adjoint = lax.map(group_adjoint, (matrix_groups, column_groups, dual_half)).reshape(SCEN, SECTIONS, COLS)
        hedge_term = multiplier + penalty * (primal[:, :, :HCOLS] - anchors)
        hedge_full = jnp.pad(hedge_term, ((0, 0), (0, 0), (0, COLS - HCOLS)))
        primal_next = jnp.maximum(primal - TAU_STEP * (cost_full + adjoint + hedge_full), 0.0)
        step_half = (2.0 * primal_next - primal).astype(jnp.bfloat16).reshape(N_SCEN, S_DEV, SECTIONS, CPS, BLK)
        image = lax.map(group_forward, (matrix_groups, column_groups, step_half)).reshape(SCEN, ROWS)
        dual_next = jnp.maximum(dual + SIGMA_STEP * (image - bounds_rhs), 0.0)
        hedged_next = primal_next[:, :, :HCOLS]
        node_table = node_sums(scenario_weights[:, None, None] * hedged_next)
        consensus = averaged(node_table, node_mass)
        new_anchors = spread_nodes(consensus)
        multiplier = multiplier + penalty * (hedged_next - new_anchors)
        primal_gap = jnp.sum(scenario_weights[:, None, None] * (hedged_next - new_anchors) ** 2)
        drift_gap = jnp.sum(scenario_weights[:, None, None] * (new_anchors - anchors) ** 2)
        penalty = penalty * jnp.sqrt(primal_gap / (drift_gap + EPSILON))
        primal, dual, previous = (primal_next, dual_next, consensus)
    return (primal, dual, multiplier, penalty)
```

```python
import functools

import jax
import jax.numpy as jnp
from jax import lax
from jax.experimental import pallas as pl
from jax.experimental.pallas import tpu as pltpu
from jax.sharding import PartitionSpec as P

BLK = 128
N1 = 8
N2 = 64
SWEEPS = 2
TAU_STEP = 0.4
SIGMA_STEP = 0.4
RHO_START = 1.0
EPSILON = 1e-06
MIB = 1 << 20
F32 = jnp.float32
BF16 = jnp.bfloat16
HIGHEST = lax.Precision.HIGHEST

VMEM = pl.BlockSpec(memory_space=pltpu.VMEM)
SMEM = pl.BlockSpec(memory_space=pltpu.SMEM)


def params(mib):
    return pltpu.CompilerParams(vmem_limit_bytes=mib * MIB)


def shape(*dims, dtype=F32):
    return jax.ShapeDtypeStruct(dims, dtype)


def write_pieces(lp_ref, dual, out_ref, S, J, NZ):
    for s in range(S):
        row = dual[s : s + 1, :].astype(BF16)
        for j in range(J):
            for n in range(NZ):
                y = jnp.dot(row, lp_ref[s, j * NZ + n], preferred_element_type=F32)
                out_ref[pl.ds((n * J + j) * S + s, 1), :] = y


def write_image(lp_ref, step_ref, own, image_ref, S, J, NZ):
    Q = J * S
    for s in range(S):
        total = None
        for j in range(J):
            for n in range(NZ):
                x = step_ref[pl.ds((own * NZ + n) * Q + j * S + s, 1), :].astype(BF16)
                y = lax.dot_general(
                    x,
                    lp_ref[s, j * NZ + n],
                    (((1,), (1,)), ((), ())),
                    preferred_element_type=F32,
                )
                total = y if total is None else total + y
        image_ref[pl.ds(s, 1), :] = total


def pieces_kernel(S, J, NZ, lp_ref, dual_ref, out_ref):
    write_pieces(lp_ref, dual_ref[...], out_ref, S, J, NZ)


def dual_kernel(S, J, NZ, lp_ref, dual_ref, rhs_ref, image_ref, image2_ref, next_ref, out_ref):
    image = image_ref[...] + image2_ref[...]
    dual = jnp.maximum(dual_ref[...] + SIGMA_STEP * (image - rhs_ref[...]), 0.0)
    next_ref[...] = dual
    write_pieces(lp_ref, dual, out_ref, S, J, NZ)


def setup_kernel(
    S,
    J,
    R,
    NZ,
    HB,
    cols_ref,
    nodes_ref,
    weights_ref,
    primal_ref,
    cost_ref,
    mult_ref,
    table_ref,
    pp_ref,
    pc_ref,
    hp_ref,
    hc_ref,
    cb_ref,
    ml_ref,
    an_ref,
    id_ref,
    wb_ref,
    ts_ref,
    idx_sc,
    pp_sc,
    pc_sc,
    hp_sc,
    hc_sc,
):
    K, Q = R * NZ, J * S
    section = lax.axis_index("section")
    rows = primal_ref.shape[1]
    nodes = table_ref.shape[0]
    for s in range(S):
        for j in range(J):
            for k in range(K):
                c = cols_ref[s, k // NZ, j, k % NZ]
                idx_sc[pl.ds((s * K + k) * J + j, 1), :] = jnp.full(
                    (1, BLK), c * J + j, jnp.int32
                )
    for j in range(J):
        g = section * J + j
        level = jnp.maximum(g - 1, 0)
        off = jnp.where(g == 0, 0, jnp.where(g == 1, 1, jnp.where(g == 2, 1 + N1, 1 + N1 + N2)))
        keep = jnp.where(g == 0, 0, 1)
        for s in range(S):
            node = nodes_ref[level, s] * keep + off
            q = j * S + s
            id_ref[pl.ds(q, 1), :] = jnp.full((1, BLK), node, jnp.int32).astype(F32)
            wb_ref[pl.ds(q, 1), :] = jnp.full((1, BLK), weights_ref[s], F32)
            line = table_ref[pl.ds(node, 1), :]
            for h in range(HB):
                an_ref[pl.ds(h * Q + q, 1), :] = line[:, h * BLK : (h + 1) * BLK]
    tiles = -(-rows // BLK)
    lane = lax.broadcasted_iota(jnp.int32, (K * J, BLK), 1)
    for s in range(S):
        want = idx_sc[pl.ds(s * K * J, K * J), :]
        pick = jnp.concatenate(
            [(want == lane + t * BLK).astype(F32).astype(BF16) for t in range(tiles)], axis=1
        )[:, :rows]
        pp_sc[pl.ds(s * K * J, K * J), :] = jnp.dot(pick, primal_ref[s], preferred_element_type=F32)
        pc_sc[pl.ds(s * K * J, K * J), :] = jnp.dot(pick, cost_ref[s], preferred_element_type=F32)
        hp_sc[pl.ds(s * HB * J, HB * J), :] = primal_ref[s, : HB * J, :].astype(F32)
        hc_sc[pl.ds(s * HB * J, HB * J), :] = cost_ref[s, : HB * J, :].astype(F32)
    for j in range(J):
        for k in range(K):
            src, dst = pl.ds(k * J + j, S, stride=K * J), pl.ds(k * Q + j * S, S)
            pp_ref[dst, :] = pp_sc[src, :]
            pc_ref[dst, :] = pc_sc[src, :]
            cb_ref[dst, :] = (idx_sc[src, :] - j).astype(F32)
        for h in range(HB):
            src, dst = pl.ds(h * J + j, S, stride=HB * J), pl.ds(h * Q + j * S, S)
            hp_ref[dst, :] = hp_sc[src, :]
            hc_ref[dst, :] = hc_sc[src, :]
            ml_ref[dst, :] = mult_ref[src, :]
    rest = table_ref[...]
    for part in range(3):
        high = rest.astype(BF16)
        ts_ref[part, :nodes, :] = high
        rest = rest - high.astype(F32)
    ts_ref[:, nodes:, :] = jnp.zeros_like(ts_ref[:, nodes:, :])


def total(x):
    return jnp.sum(x, axis=(0, 1), keepdims=True)


def primal_step(
    S, J, R, NZ, HB, own, pieces_ref, other_refs, p_ref, pc_ref, h_ref, hc_ref, cb_ref, hedge, all_sc
):
    K, Q = R * NZ, J * S
    for shift in range(R):
        src = pieces_ref if shift == 0 else other_refs[shift - 1]
        at = lax.rem(own + shift, R) * (NZ * Q)
        all_sc[pl.ds(pl.multiple_of(at, 8), NZ * Q), :] = src[...]
    slot = lambda ref, k: ref[k * Q : (k + 1) * Q, :]
    cols = [slot(cb_ref, k) for k in range(K)]
    parts = [slot(all_sc, k) for k in range(K)]
    placed, hedged = [], []
    for k in range(K):
        add = None
        for m in range(K):
            term = parts[m] if m == k else jnp.where(cols[m] == cols[k], parts[m], 0.0)
            add = term if add is None else add + term
        for h in range(HB):
            add = add + jnp.where(cols[k] == float(h * J), hedge[h], 0.0)
        placed.append(
            jnp.maximum(slot(p_ref, k) - TAU_STEP * (slot(pc_ref, k) + add), 0.0)
        )
    for h in range(HB):
        add = None
        for m in range(K):
            term = jnp.where(cols[m] == float(h * J), parts[m], 0.0)
            add = term if add is None else add + term
        add = add + hedge[h]
        hedged.append(jnp.maximum(slot(h_ref, h) - TAU_STEP * (slot(hc_ref, h) + add), 0.0))
    return placed, hedged


def finish_step(
    S, J, R, NZ, HB, own, lp_ref, p_ref, placed, hedged, anchors, ids, wb, p_out, h_out, mu_ref, image_ref, send_ref, step_sc, send_sc
):
    K, Q = R * NZ, J * S
    for k in range(K):
        p_out[k * Q : (k + 1) * Q, :] = placed[k]
        step_sc[k * Q : (k + 1) * Q, :] = 2.0 * placed[k] - p_ref[k * Q : (k + 1) * Q, :]
    for h in range(HB):
        h_out[h * Q : (h + 1) * Q, :] = hedged[h]
    across = jnp.transpose(ids)[0:1, :Q]
    same = (jnp.broadcast_to(ids[:, :1], (Q, Q)) == across).astype(F32)
    sums = jnp.dot(
        same,
        jnp.concatenate([wb * x for x in hedged] + [wb], axis=1),
        precision=HIGHEST,
        preferred_element_type=F32,
    )
    mass = sums[:, HB * BLK :]
    inner = []
    for j in range(J):
        mine = ids[j * S : (j + 1) * S]
        inner.append((mine != mine[:1]) & (mine != mine[S - 1 :]))
    inner = jnp.concatenate([x.astype(F32) for x in inner], axis=0)
    gap, drift = jnp.zeros((Q, BLK), F32), jnp.zeros((Q, BLK), F32)
    for h in range(HB):
        mu = sums[:, h * BLK : (h + 1) * BLK] / mass
        mu_ref[h * Q : (h + 1) * Q, :] = mu
        gap = gap + wb * (hedged[h] - mu) ** 2
        drift = drift + (wb * inner) * (mu - anchors[h]) ** 2
    lane = lax.broadcasted_iota(jnp.int32, (1, BLK), 1)
    note = jnp.zeros((1, BLK), F32)
    for j in range(J):
        a, b = j * S, j * S + S - 1
        fresh = ids[b : b + 1] != ids[a : a + 1]
        for f in range(2):
            e = f * J + j
            at = b if f else a
            for h in range(HB):
                line = sums[at : at + 1, h * BLK : (h + 1) * BLK]
                send_sc[pl.ds(e * HB + h, 1), :] = jnp.where(fresh, line, 0.0) if f else line
            name, weight = ids[at : at + 1], mass[at : at + 1]
            if f:
                name, weight = jnp.where(fresh, name, -1.0), jnp.where(fresh, weight, 0.0)
            note = jnp.where(lane == e, name, note)
            note = jnp.where(lane == 2 * J + e, weight, note)
    note = jnp.where(lane == 4 * J, total(gap), note)
    note = jnp.where(lane == 4 * J + 1, total(drift), note)
    at = 2 * J * HB
    send_sc[pl.ds(at, 1), :] = note
    send_sc[pl.ds(at + 1, send_sc.shape[0] - at - 1), :] = jnp.zeros(
        (send_sc.shape[0] - at - 1, BLK), F32
    )
    message = send_sc[...]
    for d in range(send_ref.shape[0]):
        send_ref[d] = message
    write_image(lp_ref, step_sc, own, image_ref, S, J, NZ)


def first_kernel(
    S, J, R, NZ, HB, lp_ref, pp_ref, pc_ref, hp_ref, hc_ref, cb_ref, ml_ref, an_ref, id_ref, wb_ref, pieces_ref, *rest
):
    other_refs = rest[: R - 1]
    p_out, h_out, mu_ref, image_ref, send_ref, all_sc, step_sc, send_sc = rest[R - 1 :]
    Q = J * S
    own = lax.axis_index("rows")
    slot = lambda ref, k: ref[k * Q : (k + 1) * Q, :]
    anchors = [slot(an_ref, h) for h in range(HB)]
    hedge = [
        slot(ml_ref, h) + RHO_START * (slot(hp_ref, h) - anchors[h]) for h in range(HB)
    ]
    placed, hedged = primal_step(
        S, J, R, NZ, HB, own, pieces_ref, other_refs, pp_ref, pc_ref, hp_ref, hc_ref, cb_ref, hedge, all_sc
    )
    finish_step(
        S, J, R, NZ, HB, own, lp_ref, pp_ref, placed, hedged, anchors, id_ref[...], wb_ref[...], p_out, h_out, mu_ref, image_ref, send_ref, step_sc, send_sc
    )


def read_nodes(J, HB, got_ref, ids, devices):
    step = got_ref.shape[0] // devices
    E = 2 * J
    sums = [
        jnp.concatenate(
            [got_ref[pl.ds(e * HB + h, devices, stride=step), :] for e in range(E)], axis=0
        )
        for h in range(HB)
    ]
    notes = got_ref[pl.ds(E * HB, devices, stride=step), :]
    wide = lambda at: jnp.broadcast_to(notes[:, at : at + 1], (devices, BLK))
    names = jnp.concatenate([wide(e) for e in range(E)], axis=0)
    weight = jnp.concatenate([wide(E + e) for e in range(E)], axis=0)
    every = jnp.concatenate([ids, names], axis=0)
    across = jnp.transpose(names)[0:1, :]
    count = E * devices
    same = (jnp.broadcast_to(every[:, :1], (every.shape[0], count)) == across).astype(F32)
    totals = jnp.dot(
        same,
        jnp.concatenate(sums + [weight], axis=1),
        precision=HIGHEST,
        preferred_element_type=F32,
    )
    mass = totals[:, HB * BLK :]
    positive = mass > 0
    safe = jnp.where(positive, mass, 1.0)
    means = [
        jnp.where(positive, totals[:, h * BLK : (h + 1) * BLK] / safe, 0.0) for h in range(HB)
    ]
    own_safe = jnp.where(weight > 0, weight, 1.0)
    gap = total(notes[:, 2 * E : 2 * E + 1])
    drift = total(notes[:, 2 * E + 1 : 2 * E + 2])
    rows = ids.shape[0]
    spread = jnp.zeros((count, BLK), F32)
    for h in range(HB):
        spread = spread + weight * (sums[h] / own_safe - means[h][rows:]) ** 2
    gap = gap + total(spread)
    return positive[:rows], [m[:rows] for m in means], [m[rows:] for m in means], names, weight, gap, drift


def moved(weight, means, before):
    change = jnp.zeros_like(weight)
    for mean, old in zip(means, before):
        change = change + weight * (mean - old) ** 2
    return total(change)


def second_kernel(
    S, J, R, NZ, HB, devices, lp_ref, pp_ref, pc_ref, hp_ref, hc_ref, cb_ref, ml_ref, mu_ref, id_ref, wb_ref, ts_ref, got_ref, pieces_ref, *rest
):
    other_refs = rest[: R - 1]
    p_out, h_out, mu_out, image_ref, send_ref, ml_out, pen_ref, ent_ref, all_sc, step_sc, send_sc = rest[R - 1 :]
    Q = J * S
    own = lax.axis_index("rows")
    slot = lambda ref, k: ref[k * Q : (k + 1) * Q, :]
    ids = id_ref[...]
    shared, means, entry_means, names, weight, gap, drift = read_nodes(J, HB, got_ref, ids, devices)
    nodes = ts_ref.shape[1]
    where = lax.broadcasted_iota(jnp.int32, (names.shape[0], nodes), 1).astype(F32)
    pick = (jnp.broadcast_to(names[:, :1], where.shape) == where).astype(F32).astype(BF16)
    old = None
    for part in range(3):
        y = jnp.dot(pick, ts_ref[part], preferred_element_type=F32)
        old = y if old is None else old + y
    drift = drift + moved(weight, entry_means, [old[:, h * BLK : (h + 1) * BLK] for h in range(HB)])
    penalty = RHO_START * jnp.sqrt(gap / (drift + EPSILON))
    pen_ref[...] = jnp.broadcast_to(penalty, pen_ref.shape)
    anchors, hedge = [], []
    for h in range(HB):
        ent_ref[h] = entry_means[h]
        anchor = jnp.where(shared, means[h], slot(mu_ref, h))
        left = slot(hp_ref, h) - anchor
        mult = slot(ml_ref, h) + RHO_START * left
        ml_out[h * Q : (h + 1) * Q, :] = mult
        anchors.append(anchor)
        hedge.append(mult + penalty * left)
    placed, hedged = primal_step(
        S, J, R, NZ, HB, own, pieces_ref, other_refs, pp_ref, pc_ref, hp_ref, hc_ref, cb_ref, hedge, all_sc
    )
    finish_step(
        S, J, R, NZ, HB, own, lp_ref, pp_ref, placed, hedged, anchors, ids, wb_ref[...], p_out, h_out, mu_out, image_ref, send_ref, step_sc, send_sc
    )


def last_kernel(
    S, J, HB, devices, got_ref, id_ref, ent_ref, mu_ref, h_ref, ml_ref, pen_ref, dual_ref, rhs_ref, image_ref, image2_ref, dual_out, ml_out, pen_out
):
    Q = J * S
    image = image_ref[...] + image2_ref[...]
    dual_out[...] = jnp.maximum(dual_ref[...] + SIGMA_STEP * (image - rhs_ref[...]), 0.0)
    shared, means, entry_means, names, weight, gap, drift = read_nodes(
        J, HB, got_ref, id_ref[...], devices
    )
    drift = drift + moved(weight, entry_means, [ent_ref[h] for h in range(HB)])
    penalty = pen_ref[0:1, 0:1]
    pen_out[...] = penalty * jnp.sqrt(gap / (drift + EPSILON))
    for h in range(HB):
        anchor = jnp.where(shared, means[h], mu_ref[h * Q : (h + 1) * Q, :])
        mult = ml_ref[h * Q : (h + 1) * Q, :] + penalty * (h_ref[h * Q : (h + 1) * Q, :] - anchor)
        for j in range(J):
            ml_out[pl.ds(h * J + j, S, stride=HB * J), :] = mult[j * S : (j + 1) * S]


def bulk_kernel(S, J, R, NZ, HB, SB, cols_ref, primal_ref, cost_ref, p_ref, h_ref, out_ref):
    K, Q = R * NZ, J * S
    first = pl.program_id(0) * SB
    for i in range(SB):
        move = TAU_STEP * cost_ref[i].astype(F32)
        x = primal_ref[i].astype(F32)
        for _ in range(SWEEPS):
            x = jnp.maximum(x - move, 0.0)
        out_ref[i] = x
        s = first + i
        for j in range(J):
            for k in range(K):
                c = cols_ref[s, k // NZ, j, k % NZ]
                out_ref[i, pl.ds(c * J + j, 1), :] = p_ref[pl.ds(k * Q + j * S + s, 1), :]
            for h in range(HB):
                out_ref[i, pl.ds(h * J + j, 1), :] = h_ref[pl.ds(h * Q + j * S + s, 1), :]


def local(
    sizes,
    lp_blocks,
    block_columns,
    scenario_nodes,
    scenario_weights,
    cost,
    bounds_rhs,
    primal_start,
    dual_start,
    multiplier_start,
    consensus_start,
):
    scens, R, sections = sizes
    S, J, columns = cost.shape
    NZ = lp_blocks.shape[3]
    hedged = multiplier_start.shape[2]
    HB, C = hedged // BLK, columns // BLK
    K, Q = R * NZ, J * S
    nodes = consensus_start.shape[0]
    devices = scens * sections
    padded = -(-nodes // 16) * 16
    message = -(-(2 * J * HB + 1) // 8) * 8
    static = (S, J, R, NZ, HB)

    def interleave(x):
        return x.reshape(S, J, -1, BLK).transpose(0, 2, 1, 3).reshape(S, -1, BLK)

    def uninterleave(x):
        return x.reshape(S, -1, J, BLK).transpose(0, 2, 1, 3).reshape(S, J, -1)

    lp = lp_blocks.reshape(S, J * NZ, BLK, BLK)
    primal, price = interleave(primal_start), interleave(cost)
    mult = interleave(multiplier_start).reshape(S * HB * J, BLK)

    def from_rows(x):
        return [
            lax.ppermute(x, "rows", [((i + q) % R, i) for i in range(R)]) for q in range(1, R)
        ]

    def from_section(x):
        return lax.ppermute(x, "section", [(i, (i + 1) % sections) for i in range(sections)])

    def exchange(x):
        return lax.all_to_all(x, ("scen", "section"), 0, 0).reshape(-1, BLK)

    pieces = pl.pallas_call(
        functools.partial(pieces_kernel, S, J, NZ),
        out_shape=shape(NZ * Q, BLK),
        in_specs=[VMEM] * 2,
        out_specs=VMEM,
        compiler_params=params(16),
        name="pieces",
    )(lp, dual_start)
    others = from_rows(pieces)

    pp, pc, hp, hc, cb, ml, an, ids, wb, ts = pl.pallas_call(
        functools.partial(setup_kernel, *static),
        out_shape=[shape(K * Q, BLK)] * 2
        + [shape(HB * Q, BLK)] * 2
        + [shape(K * Q, BLK)]
        + [shape(HB * Q, BLK)] * 2
        + [shape(Q, BLK)] * 2
        + [shape(3, padded, hedged, dtype=BF16)],
        in_specs=[SMEM] * 3 + [VMEM] * 4,
        out_specs=[VMEM] * 10,
        scratch_shapes=[pltpu.VMEM((S * K * J, BLK), jnp.int32)]
        + [pltpu.VMEM((S * K * J, BLK), F32)] * 2
        + [pltpu.VMEM((S * HB * J, BLK), F32)] * 2,
        compiler_params=params(24),
        name="setup",
    )(block_columns, scenario_nodes, scenario_weights, primal, price, mult, consensus_start)

    step_out = [
        shape(K * Q, BLK),
        shape(HB * Q, BLK),
        shape(HB * Q, BLK),
        shape(S, BLK),
        shape(devices, message, BLK),
    ]
    step_scratch = [
        pltpu.VMEM((K * Q, BLK), F32),
        pltpu.VMEM((K * Q, BLK), F32),
        pltpu.VMEM((message, BLK), F32),
    ]
    p1, h1, mu1, image1, send1 = pl.pallas_call(
        functools.partial(first_kernel, *static),
        out_shape=step_out,
        in_specs=[VMEM] * (11 + R - 1),
        out_specs=[VMEM] * 5,
        scratch_shapes=step_scratch,
        compiler_params=params(16),
        name="first",
    )(lp, pp, pc, hp, hc, cb, ml, an, ids, wb, pieces, *others)
    got1 = exchange(send1)
    image1b = from_section(image1)

    dual1, pieces2 = pl.pallas_call(
        functools.partial(dual_kernel, S, J, NZ),
        out_shape=[shape(S, BLK), shape(NZ * Q, BLK)],
        in_specs=[VMEM] * 5,
        out_specs=[VMEM] * 2,
        compiler_params=params(16),
        name="dual",
    )(lp, dual_start, bounds_rhs, image1, image1b)
    others2 = from_rows(pieces2)

    p2, h2, mu2, image2, send2, ml1, pen1, ent1 = pl.pallas_call(
        functools.partial(second_kernel, *static, devices),
        out_shape=step_out
        + [shape(HB * Q, BLK), shape(8, BLK), shape(HB, 2 * J * devices, BLK)],
        in_specs=[VMEM] * (13 + R - 1),
        out_specs=[VMEM] * 8,
        scratch_shapes=step_scratch,
        compiler_params=params(20),
        name="second",
    )(lp, p1, pc, h1, hc, cb, ml, mu1, ids, wb, ts, got1, pieces2, *others2)
    got2 = exchange(send2)
    image2b = from_section(image2)

    SB = 4 if S % 4 == 0 else 1
    block = lambda rows: pl.BlockSpec((SB, rows, BLK), lambda i: (i, 0, 0))
    out = pl.pallas_call(
        functools.partial(bulk_kernel, *static, SB),
        out_shape=shape(S, C * J, BLK),
        grid=(S // SB,),
        in_specs=[SMEM, block(C * J), block(C * J), VMEM, VMEM],
        out_specs=block(C * J),
        compiler_params=params(16),
        name="bulk",
    )(block_columns, primal, price, p2, h2)

    dual2, ml2, pen2 = pl.pallas_call(
        functools.partial(last_kernel, S, J, HB, devices),
        out_shape=[shape(S, BLK), shape(S * HB * J, BLK), shape(1, 1)],
        in_specs=[VMEM] * 11,
        out_specs=[VMEM] * 3,
        compiler_params=params(16),
        name="last",
    )(got2, ids, ent1, mu2, h2, ml1, pen1, dual1, bounds_rhs, image2, image2b)

    return (
        uninterleave(out),
        dual2,
        uninterleave(ml2.reshape(S, HB * J, BLK)),
        pen2.reshape(()),
    )


def solution(mesh):
    sizes = tuple(mesh.shape[a] for a in ("scen", "rows", "section"))
    in_specs = (
        P("scen", "rows", "section", None, None, None),
        P("scen", None, "section", None),
        P(None, "scen"),
        P("scen"),
        P("scen", "section", None),
        P("scen", "rows"),
        P("scen", "section", None),
        P("scen", "rows"),
        P("scen", "section", None),
        P(),
    )
    out_specs = (P("scen", "section", None), P("scen", "rows"), P("scen", "section", None), P())
    return jax.shard_map(
        functools.partial(local, sizes),
        mesh=mesh,
        in_specs=in_specs,
        out_specs=out_specs,
        check_vma=False,
    )
```

```python
import functools

import jax
import jax.numpy as jnp
from jax import lax
from jax.experimental import pallas as pl
from jax.experimental.pallas import tpu as pltpu
from jax.sharding import PartitionSpec as P

BLK = 128
N1 = 8
N2 = 64
SWEEPS = 2
TAU_STEP = 0.4
SIGMA_STEP = 0.4
RHO_START = 1.0
EPSILON = 1e-06
F32 = jnp.float32
BF16 = jnp.bfloat16
HIGHEST = lax.Precision.HIGHEST

VMEM = pl.BlockSpec(memory_space=pltpu.VMEM)
SMEM = pl.BlockSpec(memory_space=pltpu.SMEM)
HBM = pl.BlockSpec(memory_space=pltpu.HBM)


def params(mib=16):
    return pltpu.CompilerParams(vmem_limit_bytes=mib << 20)


def in_vmem(x):
    return pltpu.with_memory_space_constraint(x, pltpu.VMEM)


def in_hbm(x):
    return pltpu.with_memory_space_constraint(x, pltpu.HBM)


def shape(*dims):
    return jax.ShapeDtypeStruct(dims, F32)


def near(*dims):
    return pltpu.VMEM(dims, F32)


def cut(src_ref, dst_ref, sems, parts):
    step = src_ref.shape[0] // parts
    at = [pl.ds(i * step, step) for i in range(parts)]
    return [
        pltpu.make_async_copy(src_ref.at[a], dst_ref.at[a], sems.at[i]) for i, a in enumerate(at)
    ]


def write_pieces(lp_ref, dual, out_ref, S, J, NZ, before=lambda s: None):
    for s in range(S):
        before(s)
        row = dual[s : s + 1, :].astype(BF16)
        for j in range(J):
            for n in range(NZ):
                y = jnp.dot(row, lp_ref[s, j * NZ + n], preferred_element_type=F32)
                out_ref[pl.ds((n * J + j) * S + s, 1), :] = y


def image_kernel(S, J, NZ, lp_ref, step_ref, image_ref):
    for s in range(S):
        total = None
        for j in range(J):
            for n in range(NZ):
                x = step_ref[pl.ds((n * J + j) * S + s, 1), :].astype(BF16)
                y = lax.dot_general(
                    x,
                    lp_ref[s, j * NZ + n],
                    (((1,), (1,)), ((), ())),
                    preferred_element_type=F32,
                )
                total = y if total is None else total + y
        image_ref[pl.ds(s, 1), :] = total


def pieces_kernel(
    S, J, NZ, lp_hbm, dual_hbm, primal_hbm, out_ref, lp_ref, primal_ref, sems, dual_ref, sem, primal_sem
):
    parts = sems.shape[0]
    dual_copy = pltpu.make_async_copy(dual_hbm, dual_ref, sem)
    dual_copy.start()
    copies = cut(lp_hbm, lp_ref, sems, parts)
    for copy in copies:
        copy.start()
    primal_copy = pltpu.make_async_copy(primal_hbm, primal_ref, primal_sem)
    primal_copy.start()
    dual_copy.wait()

    def before(s):
        if s % (S // parts) == 0:
            copies[s // (S // parts)].wait()

    write_pieces(lp_ref, dual_ref[...], out_ref, S, J, NZ, before)
    primal_copy.wait()


def dual_kernel(S, J, NZ, lp_ref, dual_ref, rhs_ref, image_ref, image2_ref, next_ref, out_ref):
    image = image_ref[...] + image2_ref[...]
    dual = jnp.maximum(dual_ref[...] + SIGMA_STEP * (image - rhs_ref[...]), 0.0)
    next_ref[...] = dual
    write_pieces(lp_ref, dual, out_ref, S, J, NZ)


def setup_kernel(
    S,
    J,
    R,
    NZ,
    HB,
    cols_ref,
    nodes_ref,
    weights_ref,
    primal_ref,
    cost_hbm,
    mult_ref,
    table_hbm,
    pp_ref,
    pc_ref,
    hp_ref,
    hc_ref,
    cb_ref,
    ml_ref,
    an_ref,
    id_ref,
    wb_ref,
    cost_ref,
    idx_sc,
    pp_sc,
    pc_sc,
    hp_sc,
    hc_sc,
    table_ref,
    cost_sem,
    table_sem,
):
    K, Q = R * NZ, J * S
    cost_copy = pltpu.make_async_copy(cost_hbm, cost_ref, cost_sem)
    cost_copy.start()
    table_copy = pltpu.make_async_copy(table_hbm, table_ref, table_sem)
    table_copy.start()
    section = lax.axis_index("section")
    rows = primal_ref.shape[1]
    for s in range(S):
        for j in range(J):
            for k in range(K):
                c = cols_ref[k // NZ, j, k % NZ, s]
                idx_sc[pl.ds((s * K + k) * J + j, 1), :] = jnp.full(
                    (1, BLK), c * J + j, jnp.int32
                )
    nodes_of = []
    for j in range(J):
        g = section * J + j
        level = jnp.maximum(g - 1, 0)
        off = jnp.where(g == 0, 0, jnp.where(g == 1, 1, jnp.where(g == 2, 1 + N1, 1 + N1 + N2)))
        keep = jnp.where(g == 0, 0, 1)
        for s in range(S):
            node = nodes_ref[level, s] * keep + off
            q = j * S + s
            id_ref[pl.ds(q, 1), :] = jnp.full((1, BLK), node, jnp.int32).astype(F32)
            wb_ref[pl.ds(q, 1), :] = jnp.full((1, BLK), weights_ref[s], F32)
            nodes_of.append(node)
    tiles = -(-rows // BLK)
    lane = lax.broadcasted_iota(jnp.int32, (K * J, BLK), 1)

    def gather(source_ref, placed_ref, hedged_ref):
        for s in range(S):
            want = idx_sc[pl.ds(s * K * J, K * J), :]
            pick = jnp.concatenate(
                [(want == lane + t * BLK).astype(F32).astype(BF16) for t in range(tiles)], axis=1
            )[:, :rows]
            placed_ref[pl.ds(s * K * J, K * J), :] = jnp.dot(
                pick, source_ref[s], preferred_element_type=F32
            )
            hedged_ref[pl.ds(s * HB * J, HB * J), :] = source_ref[s, : HB * J, :].astype(F32)

    gather(primal_ref, pp_sc, hp_sc)
    for j in range(J):
        for k in range(K):
            src, dst = pl.ds(k * J + j, S, stride=K * J), pl.ds(k * Q + j * S, S)
            pp_ref[dst, :] = pp_sc[src, :]
            cb_ref[dst, :] = (idx_sc[src, :] - j).astype(F32)
        for h in range(HB):
            src, dst = pl.ds(h * J + j, S, stride=HB * J), pl.ds(h * Q + j * S, S)
            hp_ref[dst, :] = hp_sc[src, :]
            ml_ref[dst, :] = mult_ref[src, :]
    cost_copy.wait()
    gather(cost_ref, pc_sc, hc_sc)
    for j in range(J):
        for k in range(K):
            src, dst = pl.ds(k * J + j, S, stride=K * J), pl.ds(k * Q + j * S, S)
            pc_ref[dst, :] = pc_sc[src, :]
        for h in range(HB):
            src, dst = pl.ds(h * J + j, S, stride=HB * J), pl.ds(h * Q + j * S, S)
            hc_ref[dst, :] = hc_sc[src, :]
    table_copy.wait()
    for q, node in enumerate(nodes_of):
        line = table_ref[pl.ds(node, 1), :]
        for h in range(HB):
            an_ref[pl.ds(h * Q + q, 1), :] = line[:, h * BLK : (h + 1) * BLK]


def total(x):
    return jnp.sum(x, axis=(0, 1), keepdims=True)


def primal_step(
    S, J, R, NZ, HB, own, pieces_ref, other_refs, p_ref, pc_ref, h_ref, hc_ref, cb_ref, hedge, all_sc
):
    K, Q = R * NZ, J * S
    for shift in range(R):
        src = pieces_ref if shift == 0 else other_refs[shift - 1]
        at = lax.rem(own + shift, R) * (NZ * Q)
        all_sc[pl.ds(pl.multiple_of(at, 8), NZ * Q), :] = src[...]
    slot = lambda ref, k: ref[k * Q : (k + 1) * Q, :]
    cols = [slot(cb_ref, k) for k in range(K)]
    parts = [slot(all_sc, k) for k in range(K)]
    placed, hedged = [], []
    for k in range(K):
        add = None
        for m in range(K):
            term = parts[m] if m == k else jnp.where(cols[m] == cols[k], parts[m], 0.0)
            add = term if add is None else add + term
        for h in range(HB):
            add = add + jnp.where(cols[k] == float(h * J), hedge[h], 0.0)
        placed.append(
            jnp.maximum(slot(p_ref, k) - TAU_STEP * (slot(pc_ref, k) + add), 0.0)
        )
    for h in range(HB):
        add = None
        for m in range(K):
            term = jnp.where(cols[m] == float(h * J), parts[m], 0.0)
            add = term if add is None else add + term
        add = add + hedge[h]
        hedged.append(jnp.maximum(slot(h_ref, h) - TAU_STEP * (slot(hc_ref, h) + add), 0.0))
    return placed, hedged


def finish_step(
    S, J, R, NZ, HB, own, p_ref, placed, hedged, anchors, with_anchors, ids, wb, p_out, h_out, mu_ref, send_ref, step_ref
):
    K, Q = R * NZ, J * S
    for k in range(K):
        p_out[k * Q : (k + 1) * Q, :] = placed[k]
    mine = pl.ds(pl.multiple_of(own * (NZ * Q), 8), NZ * Q)
    step_ref[...] = 2.0 * p_out[mine, :] - p_ref[mine, :]
    for h in range(HB):
        h_out[h * Q : (h + 1) * Q, :] = hedged[h]
    across = jnp.transpose(ids)[0:1, :Q]
    same = (jnp.broadcast_to(ids[:, :1], (Q, Q)) == across).astype(F32)
    sums = jnp.dot(
        same,
        jnp.concatenate([wb * x for x in hedged] + [wb], axis=1),
        precision=HIGHEST,
        preferred_element_type=F32,
    )
    mass = sums[:, HB * BLK :]
    inner = []
    for j in range(J):
        mine = ids[j * S : (j + 1) * S]
        inner.append((mine != mine[:1]) & (mine != mine[S - 1 :]))
    inner = jnp.concatenate([x.astype(F32) for x in inner], axis=0)
    gap, drift = jnp.zeros((Q, BLK), F32), jnp.zeros((Q, BLK), F32)
    for h in range(HB):
        mu = sums[:, h * BLK : (h + 1) * BLK] / mass
        mu_ref[h * Q : (h + 1) * Q, :] = mu
        gap = gap + wb * (hedged[h] - mu) ** 2
        drift = drift + (wb * inner) * (mu - anchors[h]) ** 2
    lane = lax.broadcasted_iota(jnp.int32, (1, BLK), 1)
    note = jnp.zeros((1, BLK), F32)
    for j in range(J):
        a, b = j * S, j * S + S - 1
        fresh = ids[b : b + 1] != ids[a : a + 1]
        for f in range(2):
            e = f * J + j
            at = b if f else a
            for h in range(HB):
                line = sums[at : at + 1, h * BLK : (h + 1) * BLK]
                send_ref[pl.ds(e * HB + h, 1), :] = jnp.where(fresh, line, 0.0) if f else line
            name, weight = ids[at : at + 1], mass[at : at + 1]
            if f:
                name, weight = jnp.where(fresh, name, -1.0), jnp.where(fresh, weight, 0.0)
            note = jnp.where(lane == e, name, note)
            note = jnp.where(lane == 2 * J + e, weight, note)
    note = jnp.where(lane == 4 * J, total(gap), note)
    note = jnp.where(lane == 4 * J + 1, total(drift), note)
    if with_anchors:
        for j in range(J):
            for f in range(2):
                at = j * S + (S - 1) * f
                for h in range(HB):
                    send_ref[pl.ds(2 * J * HB + 1 + (f * J + j) * HB + h, 1), :] = anchors[h][at : at + 1]
    at = 2 * J * HB * (2 if with_anchors else 1)
    send_ref[pl.ds(2 * J * HB, 1), :] = note
    send_ref[pl.ds(at + 1, send_ref.shape[0] - at - 1), :] = jnp.zeros(
        (send_ref.shape[0] - at - 1, BLK), F32
    )


def first_kernel(
    S, J, R, NZ, HB, pp_ref, pc_ref, hp_ref, hc_ref, cb_ref, ml_ref, an_ref, id_ref, wb_ref, pieces_ref, *rest
):
    other_refs = rest[: R - 1]
    p_out, h_out, mu_ref, send_ref, step_ref, all_sc = rest[R - 1 :]
    Q = J * S
    own = lax.axis_index("rows")
    slot = lambda ref, k: ref[k * Q : (k + 1) * Q, :]
    anchors = [slot(an_ref, h) for h in range(HB)]
    hedge = [
        slot(ml_ref, h) + RHO_START * (slot(hp_ref, h) - anchors[h]) for h in range(HB)
    ]
    placed, hedged = primal_step(
        S, J, R, NZ, HB, own, pieces_ref, other_refs, pp_ref, pc_ref, hp_ref, hc_ref, cb_ref, hedge, all_sc
    )
    finish_step(
        S, J, R, NZ, HB, own, pp_ref, placed, hedged, anchors, True, id_ref[...], wb_ref[...], p_out, h_out, mu_ref, send_ref, step_ref
    )


def read_nodes(J, HB, got_ref, ids, devices):
    step = got_ref.shape[0] // devices
    E = 2 * J
    sums = [
        jnp.concatenate(
            [got_ref[pl.ds(e * HB + h, devices, stride=step), :] for e in range(E)], axis=0
        )
        for h in range(HB)
    ]
    notes = got_ref[pl.ds(E * HB, devices, stride=step), :]
    wide = lambda at: jnp.broadcast_to(notes[:, at : at + 1], (devices, BLK))
    names = jnp.concatenate([wide(e) for e in range(E)], axis=0)
    weight = jnp.concatenate([wide(E + e) for e in range(E)], axis=0)
    every = jnp.concatenate([ids, names], axis=0)
    across = jnp.transpose(names)[0:1, :]
    count = E * devices
    same = (jnp.broadcast_to(every[:, :1], (every.shape[0], count)) == across).astype(F32)
    totals = jnp.dot(
        same,
        jnp.concatenate(sums + [weight], axis=1),
        precision=HIGHEST,
        preferred_element_type=F32,
    )
    mass = totals[:, HB * BLK :]
    positive = mass > 0
    safe = jnp.where(positive, mass, 1.0)
    means = [
        jnp.where(positive, totals[:, h * BLK : (h + 1) * BLK] / safe, 0.0) for h in range(HB)
    ]
    own_safe = jnp.where(weight > 0, weight, 1.0)
    gap = total(notes[:, 2 * E : 2 * E + 1])
    drift = total(notes[:, 2 * E + 1 : 2 * E + 2])
    before = [
        jnp.concatenate(
            [
                got_ref[pl.ds(E * HB + 1 + e * HB + h, devices, stride=step), :]
                for e in range(E)
            ],
            axis=0,
        )
        for h in range(HB)
    ] if step > 2 * E * HB else None
    rows = ids.shape[0]
    spread = jnp.zeros((count, BLK), F32)
    for h in range(HB):
        spread = spread + weight * (sums[h] / own_safe - means[h][rows:]) ** 2
    gap = gap + total(spread)
    return positive[:rows], [m[:rows] for m in means], [m[rows:] for m in means], before, weight, gap, drift


def moved(weight, means, before):
    change = jnp.zeros_like(weight)
    for mean, old in zip(means, before):
        change = change + weight * (mean - old) ** 2
    return total(change)


def put_sums(gap, drift, out_ref):
    lane = lax.broadcasted_iota(jnp.int32, out_ref.shape, 1)
    out_ref[...] = jnp.where(lane == 0, gap, drift)


def scaled(penalty, own_ref, other_refs):
    sums = own_ref[...]
    for ref in other_refs:
        sums = sums + ref[...]
    return penalty * jnp.sqrt(sums[0:1, 0:1] / (sums[0:1, 1:2] + EPSILON))


def nodes_kernel(
    S, J, HB, devices, got_ref, id_ref, mu_ref, h_ref, ml_ref, an_out, ml_out, ent_ref, sums_ref
):
    Q = J * S
    shared, means, entry_means, before, weight, gap, drift = read_nodes(
        J, HB, got_ref, id_ref[...], devices
    )
    put_sums(gap, drift + moved(weight, entry_means, before), sums_ref)
    for h in range(HB):
        at = pl.ds(h * Q, Q)
        ent_ref[h] = entry_means[h]
        anchor = jnp.where(shared, means[h], mu_ref[at, :])
        an_out[at, :] = anchor
        ml_out[at, :] = ml_ref[at, :] + RHO_START * (h_ref[at, :] - anchor)


def second_kernel(
    S, J, R, NZ, HB, pp_ref, pc_ref, hp_ref, hc_ref, cb_ref, ml_ref, an_ref, id_ref, wb_ref, sums_ref, sums2_ref, pieces_ref, *rest
):
    other_refs = rest[: R - 1]
    p_out, h_out, mu_out, send_ref, step_ref, pen_ref, all_sc = rest[R - 1 :]
    Q = J * S
    own = lax.axis_index("rows")
    slot = lambda ref, k: ref[k * Q : (k + 1) * Q, :]
    penalty = scaled(RHO_START, sums_ref, [sums2_ref])
    pen_ref[...] = jnp.broadcast_to(penalty, pen_ref.shape)
    anchors = [slot(an_ref, h) for h in range(HB)]
    hedge = [slot(ml_ref, h) + penalty * (slot(hp_ref, h) - anchors[h]) for h in range(HB)]
    placed, hedged = primal_step(
        S, J, R, NZ, HB, own, pieces_ref, other_refs, pp_ref, pc_ref, hp_ref, hc_ref, cb_ref, hedge, all_sc
    )
    finish_step(
        S, J, R, NZ, HB, own, pp_ref, placed, hedged, anchors, False, id_ref[...], wb_ref[...], p_out, h_out, mu_out, send_ref, step_ref
    )


def last_kernel(
    S, J, HB, devices, got_ref, id_ref, ent_ref, mu_ref, h_ref, ml_ref, pen_ref, ml_out, sums_ref
):
    Q = J * S
    shared, means, entry_means, before, weight, gap, drift = read_nodes(
        J, HB, got_ref, id_ref[...], devices
    )
    drift = drift + moved(weight, entry_means, [ent_ref[h] for h in range(HB)])
    put_sums(gap, drift, sums_ref)
    penalty = pen_ref[0:1, 0:1]
    for h in range(HB):
        at = pl.ds(h * Q, Q)
        anchor = jnp.where(shared, means[h], mu_ref[at, :])
        ml_out[at, :] = ml_ref[at, :] + penalty * (h_ref[at, :] - anchor)


def order_kernel(S, J, HB, ml_ref, out_ref):
    for h in range(HB):
        for j in range(J):
            src = pl.ds(h * J * S + j * S, S)
            out_ref[pl.ds(h * J + j, S, stride=HB * J), :] = ml_ref[src, :]


def last_dual_kernel(dual_ref, rhs_ref, image_ref, image2_ref, out_ref):
    image = image_ref[...] + image2_ref[...]
    out_ref[...] = jnp.maximum(dual_ref[...] + SIGMA_STEP * (image - rhs_ref[...]), 0.0)


def penalty_kernel(pen_ref, sums_ref, sums2_ref, out_ref):
    out_ref[...] = scaled(pen_ref[0:1, 0:1], sums_ref, [sums2_ref])


def bulk_kernel(S, J, R, NZ, HB, first, count, parts, cols_ref, primal_ref, cost_ref, p_ref, h_ref, *rest):
    out_hbm, out_ref, sems = rest[-3:]
    K, Q = R * NZ, J * S
    step = count // parts
    copies = [
        pltpu.make_async_copy(
            out_ref.at[pl.ds(i * step, step)], out_hbm.at[pl.ds(first + i * step, step)], sems.at[i]
        )
        for i in range(parts)
    ]
    for i in range(count):
        s = first + i
        move = TAU_STEP * cost_ref[s].astype(F32)
        x = primal_ref[s].astype(F32)
        for _ in range(SWEEPS):
            x = jnp.maximum(x - move, 0.0)
        out_ref[i] = x
        for j in range(J):
            for k in range(K):
                c = cols_ref[k // NZ, j, k % NZ, s]
                out_ref[i, pl.ds(c * J + j, 1), :] = p_ref[pl.ds(k * Q + j * S + s, 1), :]
            for h in range(HB):
                out_ref[i, pl.ds(h * J + j, 1), :] = h_ref[pl.ds(h * Q + j * S + s, 1), :]
        if (i + 1) % step == 0:
            copies[i // step].start()
    for copy in copies:
        copy.wait()


def merge_kernel(apart, x_ref, y_ref, *rest):
    out_ref = rest[-1]
    rows = x_ref.shape[0]
    high = lax.rem(lax.axis_index("scen") // apart, 2)
    out_ref[pl.ds(pl.multiple_of(high * rows, 8), rows), :] = x_ref[...]
    out_ref[pl.ds(pl.multiple_of((1 - high) * rows, 8), rows), :] = y_ref[...]


def local(
    sizes,
    lp_blocks,
    block_columns,
    scenario_nodes,
    scenario_weights,
    cost,
    bounds_rhs,
    primal_start,
    dual_start,
    multiplier_start,
    consensus_start,
):
    scens, R, sections = sizes
    S, J, columns = cost.shape
    NZ = lp_blocks.shape[3]
    hedged = multiplier_start.shape[2]
    HB, C = hedged // BLK, columns // BLK
    K, Q = R * NZ, J * S
    devices = scens
    message = -(-(2 * J * HB + 1) // 8) * 8
    message1 = -(-(4 * J * HB + 1) // 8) * 8
    static = (S, J, R, NZ, HB)

    def interleave(x):
        return x.reshape(S, J, -1, BLK).transpose(0, 2, 1, 3).reshape(S, -1, BLK)

    def uninterleave(x):
        return x.reshape(S, -1, J, BLK).transpose(0, 2, 1, 3).reshape(S, J, -1)

    columns_of = block_columns.transpose(1, 2, 3, 0)
    lp = in_hbm(lp_blocks.reshape(S, J * NZ, BLK, BLK))
    primal, price = in_hbm(interleave(primal_start)), in_hbm(interleave(cost))
    mult = interleave(multiplier_start).reshape(S * HB * J, BLK)

    def from_rows(x):
        return [
            lax.ppermute(x, "rows", [((i + q) % R, i) for i in range(R)]) for q in range(1, R)
        ]

    def from_section(x):
        return lax.ppermute(x, "section", [(i, (i + 1) % sections) for i in range(sections)])

    def partner(x, apart):
        return lax.ppermute(x, "scen", [(i, i ^ apart) for i in range(scens)])

    def merge(x, y, apart, *after):
        return pl.pallas_call(
            functools.partial(merge_kernel, apart),
            out_shape=near(2 * x.shape[0], BLK),
            in_specs=[VMEM] * 2 + [HBM if far else VMEM for far, _ in after],
            out_specs=VMEM,
            compiler_params=params(4),
            name="merge",
        )(x, y, *[in_hbm(z) if far else z for far, z in after])

    def exchange(x, *work):
        if scens & (scens - 1):
            return lax.all_gather(x, "scen", axis=0, tiled=True)
        apart, turn = scens // 2, 0
        while apart:
            y = partner(x, apart)
            x = merge(x, y, apart, *(work[turn]() if turn < len(work) else ()))
            apart, turn = apart // 2, turn + 1
        return x

    def near_like(x):
        return pltpu.VMEM(x.shape, x.dtype)

    parts = max(p for p in (4, 3, 2, 1) if S % p == 0)
    pieces, lp, primal = pl.pallas_call(
        functools.partial(pieces_kernel, S, J, NZ),
        out_shape=[near(NZ * Q, BLK), near_like(lp), near_like(primal)],
        in_specs=[HBM] * 3,
        out_specs=[VMEM] * 3,
        scratch_shapes=[
            pltpu.SemaphoreType.DMA((parts,)),
            pltpu.VMEM(dual_start.shape, F32),
            pltpu.SemaphoreType.DMA,
            pltpu.SemaphoreType.DMA,
        ],
        compiler_params=params(16),
        name="pieces",
    )(lp, in_hbm(dual_start), primal)
    others = from_rows(pieces)

    pp, pc, hp, hc, cb, ml, an, ids, wb, price = pl.pallas_call(
        functools.partial(setup_kernel, *static),
        out_shape=[near(K * Q, BLK)] * 2
        + [near(HB * Q, BLK)] * 2
        + [near(K * Q, BLK)]
        + [near(HB * Q, BLK)] * 2
        + [near(Q, BLK)] * 2
        + [near_like(price)],
        in_specs=[SMEM] * 3 + [VMEM, HBM, VMEM, HBM],
        out_specs=[VMEM] * 10,
        scratch_shapes=[pltpu.VMEM((S * K * J, BLK), jnp.int32)]
        + [pltpu.VMEM((S * K * J, BLK), F32)] * 2
        + [pltpu.VMEM((S * HB * J, BLK), F32)] * 2
        + [pltpu.VMEM(consensus_start.shape, F32)]
        + [pltpu.SemaphoreType.DMA] * 2,
        compiler_params=params(16),
        name="setup",
    )(columns_of, scenario_nodes, scenario_weights, in_vmem(primal), price, mult, in_hbm(consensus_start))
    primal = in_vmem(primal)

    def step_out(rows):
        return [
            near(K * Q, BLK),
            near(HB * Q, BLK),
            near(HB * Q, BLK),
            near(rows, BLK),
            near(NZ * Q, BLK),
        ]

    def image_of(step):
        return pl.pallas_call(
            functools.partial(image_kernel, S, J, NZ),
            out_shape=near(S, BLK),
            in_specs=[VMEM] * 2,
            out_specs=VMEM,
            compiler_params=params(8),
            name="image",
        )(lp, step)

    scratch = [pltpu.VMEM((K * Q, BLK), F32)]
    p1, h1, mu1, send1, step1 = pl.pallas_call(
        functools.partial(first_kernel, *static),
        out_shape=step_out(message1),
        in_specs=[VMEM] * (10 + R - 1),
        out_specs=[VMEM] * 5,
        scratch_shapes=scratch,
        compiler_params=params(8),
        name="first",
    )(pp, pc, hp, hc, cb, ml, an, ids, wb, pieces, *others)
    made = {}

    def image_work():
        made["image"] = image_of(step1)
        return ((False, made["image"]),)

    def dual_work():
        made["dual"], made["pieces"] = pl.pallas_call(
            functools.partial(dual_kernel, S, J, NZ),
            out_shape=[near(S, BLK), near(NZ * Q, BLK)],
            in_specs=[VMEM] * 5,
            out_specs=[VMEM] * 2,
            compiler_params=params(8),
            name="dual",
        )(lp, dual_start, bounds_rhs, made["image"], from_section(made["image"]))
        return ((False, made["pieces"]),)

    got1 = exchange(send1, image_work, dual_work)
    dual1, pieces2 = made["dual"], made["pieces"]
    others2 = from_rows(pieces2)

    an1, ml1, ent1, sums1 = pl.pallas_call(
        functools.partial(nodes_kernel, S, J, HB, devices),
        out_shape=[near(HB * Q, BLK)] * 2 + [near(HB, 2 * J * devices, BLK), near(8, BLK)],
        in_specs=[VMEM] * 5,
        out_specs=[VMEM] * 4,
        compiler_params=params(8),
        name="nodes",
    )(got1, ids, mu1, h1, ml)
    sums1b = from_section(sums1)

    p2, h2, mu2, send2, step2, pen1 = pl.pallas_call(
        functools.partial(second_kernel, *static),
        out_shape=step_out(message) + [near(8, BLK)],
        in_specs=[VMEM] * (12 + R - 1),
        out_specs=[VMEM] * 6,
        scratch_shapes=scratch,
        compiler_params=params(8),
        name="second",
    )(p1, pc, h1, hc, cb, ml1, an1, ids, wb, sums1, sums1b, pieces2, *others2)
    half = S // 2

    def bulk(first, count, *into):
        cuts = max(p for p in (3, 2, 1) if count % p == 0)
        return pl.pallas_call(
            functools.partial(bulk_kernel, *static, first, count, cuts),
            out_shape=shape(S, C * J, BLK),
            in_specs=[SMEM] + [VMEM] * 4 + [HBM] * len(into),
            out_specs=HBM,
            scratch_shapes=[pltpu.VMEM((count, C * J, BLK), F32), pltpu.SemaphoreType.DMA((cuts,))],
            input_output_aliases={5: 0} if into else {},
            compiler_params=params(8),
            name="bulk",
        )(columns_of, primal, price, p2, h2, *into)

    def last_image_work():
        made["image"] = image_of(step2)
        return ((False, made["image"]),)

    def bulk_work():
        made["out"] = bulk(0, half)
        made["image2"] = from_section(made["image"])
        return ((True, made["out"]),)

    def rest_work():
        made["out"] = bulk(half, S - half, made["out"])
        made["dual"] = pl.pallas_call(
            last_dual_kernel,
            out_shape=shape(S, BLK),
            in_specs=[VMEM] * 4,
            out_specs=VMEM,
            compiler_params=params(4),
            name="last_dual",
        )(dual1, bounds_rhs, made["image"], made["image2"])
        return ((True, made["out"]), (True, made["dual"]))

    got2 = exchange(send2, last_image_work, bulk_work, rest_work)
    out, dual2 = made["out"], made["dual"]
    ml2, sums2 = pl.pallas_call(
        functools.partial(last_kernel, S, J, HB, devices),
        out_shape=[near(HB * Q, BLK), near(8, BLK)],
        in_specs=[VMEM] * 7,
        out_specs=[VMEM] * 2,
        compiler_params=params(8),
        name="last",
    )(got2, ids, ent1, mu2, h2, ml1, pen1)
    ml2 = pl.pallas_call(
        functools.partial(order_kernel, S, J, HB),
        out_shape=shape(S * HB * J, BLK),
        in_specs=[VMEM],
        out_specs=VMEM,
        compiler_params=params(4),
        name="order",
    )(ml2)
    pen2 = pl.pallas_call(
        penalty_kernel,
        out_shape=shape(1, 1),
        in_specs=[VMEM] * 3,
        out_specs=VMEM,
        compiler_params=params(4),
        name="penalty",
    )(pen1, sums2, from_section(sums2))

    return (
        uninterleave(out),
        dual2,
        uninterleave(ml2.reshape(S, HB * J, BLK)),
        pen2.reshape(()),
    )


def solution(mesh):
    sizes = tuple(mesh.shape[a] for a in ("scen", "rows", "section"))
    in_specs = (
        P("scen", "rows", "section", None, None, None),
        P("scen", None, "section", None),
        P(None, "scen"),
        P("scen"),
        P("scen", "section", None),
        P("scen", "rows"),
        P("scen", "section", None),
        P("scen", "rows"),
        P("scen", "section", None),
        P(),
    )
    out_specs = (P("scen", "section", None), P("scen", "rows"), P("scen", "section", None), P())
    return jax.shard_map(
        functools.partial(local, sizes),
        mesh=mesh,
        in_specs=in_specs,
        out_specs=out_specs,
        check_vma=False,
    )
```

```python
import functools

import jax
import jax.numpy as jnp
from jax import lax
from jax.experimental import pallas as pl
from jax.experimental.pallas import tpu as pltpu
from jax.sharding import PartitionSpec as P

BLK = 128
N1 = 8
N2 = 64
SWEEPS = 2
TAU_STEP = 0.4
SIGMA_STEP = 0.4
RHO_START = 1.0
EPSILON = 1e-06
F32 = jnp.float32
BF16 = jnp.bfloat16
HIGHEST = lax.Precision.HIGHEST

VMEM = pl.BlockSpec(memory_space=pltpu.VMEM)
SMEM = pl.BlockSpec(memory_space=pltpu.SMEM)
HBM = pl.BlockSpec(memory_space=pltpu.HBM)


def params(mib=16):
    return pltpu.CompilerParams(vmem_limit_bytes=mib << 20)


def in_vmem(x):
    return pltpu.with_memory_space_constraint(x, pltpu.VMEM)


def in_hbm(x):
    return pltpu.with_memory_space_constraint(x, pltpu.HBM)


def shape(*dims):
    return jax.ShapeDtypeStruct(dims, F32)


def near(*dims):
    return pltpu.VMEM(dims, F32)


def cut(src_ref, dst_ref, sems, parts):
    step = src_ref.shape[0] // parts
    at = [pl.ds(i * step, step) for i in range(parts)]
    return [
        pltpu.make_async_copy(src_ref.at[a], dst_ref.at[a], sems.at[i]) for i, a in enumerate(at)
    ]


def write_pieces(lp_ref, dual, out_ref, S, J, NZ, before=lambda s: None):
    for s in range(S):
        before(s)
        row = dual[s : s + 1, :].astype(BF16)
        for j in range(J):
            for n in range(NZ):
                y = jnp.dot(row, lp_ref[s, j * NZ + n], preferred_element_type=F32)
                out_ref[pl.ds((n * J + j) * S + s, 1), :] = y


def image_kernel(S, J, NZ, lp_ref, step_ref, image_ref):
    for s in range(S):
        total = None
        for j in range(J):
            for n in range(NZ):
                x = step_ref[pl.ds((n * J + j) * S + s, 1), :].astype(BF16)
                y = lax.dot_general(
                    x,
                    lp_ref[s, j * NZ + n],
                    (((1,), (1,)), ((), ())),
                    preferred_element_type=F32,
                )
                total = y if total is None else total + y
        image_ref[pl.ds(s, 1), :] = total


def pieces_kernel(
    S, J, NZ, lp_hbm, dual_hbm, primal_hbm, out_ref, lp_ref, primal_ref, sems, dual_ref, sem, primal_sem
):
    parts = sems.shape[0]
    dual_copy = pltpu.make_async_copy(dual_hbm, dual_ref, sem)
    dual_copy.start()
    copies = cut(lp_hbm, lp_ref, sems, parts)
    for copy in copies:
        copy.start()
    primal_copy = pltpu.make_async_copy(primal_hbm, primal_ref, primal_sem)
    primal_copy.start()
    dual_copy.wait()

    def before(s):
        if s % (S // parts) == 0:
            copies[s // (S // parts)].wait()

    write_pieces(lp_ref, dual_ref[...], out_ref, S, J, NZ, before)
    primal_copy.wait()


def dual_kernel(S, J, NZ, lp_ref, dual_ref, rhs_ref, image_ref, image2_ref, next_ref, out_ref):
    image = image_ref[...] + image2_ref[...]
    dual = jnp.maximum(dual_ref[...] + SIGMA_STEP * (image - rhs_ref[...]), 0.0)
    next_ref[...] = dual
    write_pieces(lp_ref, dual, out_ref, S, J, NZ)


def setup_kernel(
    S,
    J,
    R,
    NZ,
    HB,
    cols_ref,
    nodes_ref,
    weights_ref,
    primal_ref,
    cost_ref,
    mult_ref,
    table_hbm,
    pp_ref,
    pc_ref,
    hp_ref,
    hc_ref,
    cb_ref,
    ml_ref,
    an_ref,
    id_ref,
    wb_ref,
    idx_sc,
    pp_sc,
    pc_sc,
    hp_sc,
    hc_sc,
    table_ref,
    table_sem,
):
    K, Q = R * NZ, J * S
    table_copy = pltpu.make_async_copy(table_hbm, table_ref, table_sem)
    table_copy.start()
    section = lax.axis_index("section")
    rows = primal_ref.shape[1]
    for s in range(S):
        for j in range(J):
            for k in range(K):
                c = cols_ref[k // NZ, j, k % NZ, s]
                idx_sc[pl.ds((s * K + k) * J + j, 1), :] = jnp.full(
                    (1, BLK), c * J + j, jnp.int32
                )
    nodes_of = []
    for j in range(J):
        g = section * J + j
        level = jnp.maximum(g - 1, 0)
        off = jnp.where(g == 0, 0, jnp.where(g == 1, 1, jnp.where(g == 2, 1 + N1, 1 + N1 + N2)))
        keep = jnp.where(g == 0, 0, 1)
        for s in range(S):
            node = nodes_ref[level, s] * keep + off
            q = j * S + s
            id_ref[pl.ds(q, 1), :] = jnp.full((1, BLK), node, jnp.int32).astype(F32)
            wb_ref[pl.ds(q, 1), :] = jnp.full((1, BLK), weights_ref[s], F32)
            nodes_of.append(node)
    tiles = -(-rows // BLK)
    lane = lax.broadcasted_iota(jnp.int32, (K * J, BLK), 1)

    def gather(source_ref, placed_ref, hedged_ref):
        for s in range(S):
            want = idx_sc[pl.ds(s * K * J, K * J), :]
            pick = jnp.concatenate(
                [(want == lane + t * BLK).astype(F32).astype(BF16) for t in range(tiles)], axis=1
            )[:, :rows]
            placed_ref[pl.ds(s * K * J, K * J), :] = jnp.dot(
                pick, source_ref[s], preferred_element_type=F32
            )
            hedged_ref[pl.ds(s * HB * J, HB * J), :] = source_ref[s, : HB * J, :].astype(F32)

    gather(primal_ref, pp_sc, hp_sc)
    for j in range(J):
        for k in range(K):
            src, dst = pl.ds(k * J + j, S, stride=K * J), pl.ds(k * Q + j * S, S)
            pp_ref[dst, :] = pp_sc[src, :]
            cb_ref[dst, :] = (idx_sc[src, :] - j).astype(F32)
        for h in range(HB):
            src, dst = pl.ds(h * J + j, S, stride=HB * J), pl.ds(h * Q + j * S, S)
            hp_ref[dst, :] = hp_sc[src, :]
            ml_ref[dst, :] = mult_ref[src, :]
    gather(cost_ref, pc_sc, hc_sc)
    for j in range(J):
        for k in range(K):
            src, dst = pl.ds(k * J + j, S, stride=K * J), pl.ds(k * Q + j * S, S)
            pc_ref[dst, :] = pc_sc[src, :]
        for h in range(HB):
            src, dst = pl.ds(h * J + j, S, stride=HB * J), pl.ds(h * Q + j * S, S)
            hc_ref[dst, :] = hc_sc[src, :]
    table_copy.wait()
    for q, node in enumerate(nodes_of):
        line = table_ref[pl.ds(node, 1), :]
        for h in range(HB):
            an_ref[pl.ds(h * Q + q, 1), :] = line[:, h * BLK : (h + 1) * BLK]


def total(x):
    return jnp.sum(x, axis=(0, 1), keepdims=True)


def primal_step(
    S, J, R, NZ, HB, own, pieces_ref, other_refs, p_ref, pc_ref, h_ref, hc_ref, cb_ref, hedge, all_sc
):
    K, Q = R * NZ, J * S
    for shift in range(R):
        src = pieces_ref if shift == 0 else other_refs[shift - 1]
        at = lax.rem(own + shift, R) * (NZ * Q)
        all_sc[pl.ds(pl.multiple_of(at, 8), NZ * Q), :] = src[...]
    slot = lambda ref, k: ref[k * Q : (k + 1) * Q, :]
    cols = [slot(cb_ref, k) for k in range(K)]
    parts = [slot(all_sc, k) for k in range(K)]
    placed, hedged = [], []
    for k in range(K):
        add = None
        for m in range(K):
            term = parts[m] if m == k else jnp.where(cols[m] == cols[k], parts[m], 0.0)
            add = term if add is None else add + term
        for h in range(HB):
            add = add + jnp.where(cols[k] == float(h * J), hedge[h], 0.0)
        placed.append(
            jnp.maximum(slot(p_ref, k) - TAU_STEP * (slot(pc_ref, k) + add), 0.0)
        )
    for h in range(HB):
        add = None
        for m in range(K):
            term = jnp.where(cols[m] == float(h * J), parts[m], 0.0)
            add = term if add is None else add + term
        add = add + hedge[h]
        hedged.append(jnp.maximum(slot(h_ref, h) - TAU_STEP * (slot(hc_ref, h) + add), 0.0))
    return placed, hedged


def finish_step(
    S, J, R, NZ, HB, own, p_ref, placed, hedged, anchors, with_anchors, ids, wb, p_out, h_out, mu_ref, send_ref, step_ref
):
    K, Q = R * NZ, J * S
    for k in range(K):
        p_out[k * Q : (k + 1) * Q, :] = placed[k]
    mine = pl.ds(pl.multiple_of(own * (NZ * Q), 8), NZ * Q)
    step_ref[...] = 2.0 * p_out[mine, :] - p_ref[mine, :]
    for h in range(HB):
        h_out[h * Q : (h + 1) * Q, :] = hedged[h]
    across = jnp.transpose(ids)[0:1, :Q]
    same = (jnp.broadcast_to(ids[:, :1], (Q, Q)) == across).astype(F32)
    sums = jnp.dot(
        same,
        jnp.concatenate([wb * x for x in hedged] + [wb], axis=1),
        precision=HIGHEST,
        preferred_element_type=F32,
    )
    mass = sums[:, HB * BLK :]
    inner = []
    for j in range(J):
        mine = ids[j * S : (j + 1) * S]
        inner.append((mine != mine[:1]) & (mine != mine[S - 1 :]))
    inner = jnp.concatenate([x.astype(F32) for x in inner], axis=0)
    gap, drift = jnp.zeros((Q, BLK), F32), jnp.zeros((Q, BLK), F32)
    for h in range(HB):
        mu = sums[:, h * BLK : (h + 1) * BLK] / mass
        mu_ref[h * Q : (h + 1) * Q, :] = mu
        gap = gap + wb * (hedged[h] - mu) ** 2
        drift = drift + (wb * inner) * (mu - anchors[h]) ** 2
    lane = lax.broadcasted_iota(jnp.int32, (1, BLK), 1)
    note = jnp.zeros((1, BLK), F32)
    for j in range(J):
        a, b = j * S, j * S + S - 1
        fresh = ids[b : b + 1] != ids[a : a + 1]
        for f in range(2):
            e = f * J + j
            at = b if f else a
            for h in range(HB):
                line = sums[at : at + 1, h * BLK : (h + 1) * BLK]
                send_ref[pl.ds(e * HB + h, 1), :] = jnp.where(fresh, line, 0.0) if f else line
            name, weight = ids[at : at + 1], mass[at : at + 1]
            if f:
                name, weight = jnp.where(fresh, name, -1.0), jnp.where(fresh, weight, 0.0)
            note = jnp.where(lane == e, name, note)
            note = jnp.where(lane == 2 * J + e, weight, note)
    note = jnp.where(lane == 4 * J, total(gap), note)
    note = jnp.where(lane == 4 * J + 1, total(drift), note)
    if with_anchors:
        for j in range(J):
            for f in range(2):
                at = j * S + (S - 1) * f
                for h in range(HB):
                    send_ref[pl.ds(2 * J * HB + 1 + (f * J + j) * HB + h, 1), :] = anchors[h][at : at + 1]
    at = 2 * J * HB * (2 if with_anchors else 1)
    send_ref[pl.ds(2 * J * HB, 1), :] = note
    send_ref[pl.ds(at + 1, send_ref.shape[0] - at - 1), :] = jnp.zeros(
        (send_ref.shape[0] - at - 1, BLK), F32
    )


def first_kernel(
    S, J, R, NZ, HB, pp_ref, pc_ref, hp_ref, hc_ref, cb_ref, ml_ref, an_ref, id_ref, wb_ref, pieces_ref, *rest
):
    other_refs = rest[: R - 1]
    p_out, h_out, mu_ref, send_ref, step_ref, all_sc = rest[R - 1 :]
    Q = J * S
    own = lax.axis_index("rows")
    slot = lambda ref, k: ref[k * Q : (k + 1) * Q, :]
    anchors = [slot(an_ref, h) for h in range(HB)]
    hedge = [
        slot(ml_ref, h) + RHO_START * (slot(hp_ref, h) - anchors[h]) for h in range(HB)
    ]
    placed, hedged = primal_step(
        S, J, R, NZ, HB, own, pieces_ref, other_refs, pp_ref, pc_ref, hp_ref, hc_ref, cb_ref, hedge, all_sc
    )
    finish_step(
        S, J, R, NZ, HB, own, pp_ref, placed, hedged, anchors, True, id_ref[...], wb_ref[...], p_out, h_out, mu_ref, send_ref, step_ref
    )


def read_nodes(J, HB, got_ref, ids, devices):
    step = got_ref.shape[0] // devices
    E = 2 * J
    sums = [
        jnp.concatenate(
            [got_ref[pl.ds(e * HB + h, devices, stride=step), :] for e in range(E)], axis=0
        )
        for h in range(HB)
    ]
    notes = got_ref[pl.ds(E * HB, devices, stride=step), :]
    wide = lambda at: jnp.broadcast_to(notes[:, at : at + 1], (devices, BLK))
    names = jnp.concatenate([wide(e) for e in range(E)], axis=0)
    weight = jnp.concatenate([wide(E + e) for e in range(E)], axis=0)
    every = jnp.concatenate([ids, names], axis=0)
    across = jnp.transpose(names)[0:1, :]
    count = E * devices
    same = (jnp.broadcast_to(every[:, :1], (every.shape[0], count)) == across).astype(F32)
    totals = jnp.dot(
        same,
        jnp.concatenate(sums + [weight], axis=1),
        precision=HIGHEST,
        preferred_element_type=F32,
    )
    mass = totals[:, HB * BLK :]
    positive = mass > 0
    safe = jnp.where(positive, mass, 1.0)
    means = [
        jnp.where(positive, totals[:, h * BLK : (h + 1) * BLK] / safe, 0.0) for h in range(HB)
    ]
    own_safe = jnp.where(weight > 0, weight, 1.0)
    gap = total(notes[:, 2 * E : 2 * E + 1])
    drift = total(notes[:, 2 * E + 1 : 2 * E + 2])
    before = [
        jnp.concatenate(
            [
                got_ref[pl.ds(E * HB + 1 + e * HB + h, devices, stride=step), :]
                for e in range(E)
            ],
            axis=0,
        )
        for h in range(HB)
    ] if step > 2 * E * HB else None
    rows = ids.shape[0]
    spread = jnp.zeros((count, BLK), F32)
    for h in range(HB):
        spread = spread + weight * (sums[h] / own_safe - means[h][rows:]) ** 2
    gap = gap + total(spread)
    return positive[:rows], [m[:rows] for m in means], [m[rows:] for m in means], before, weight, gap, drift


def moved(weight, means, before):
    change = jnp.zeros_like(weight)
    for mean, old in zip(means, before):
        change = change + weight * (mean - old) ** 2
    return total(change)


def put_sums(gap, drift, out_ref):
    lane = lax.broadcasted_iota(jnp.int32, out_ref.shape, 1)
    out_ref[...] = jnp.where(lane == 0, gap, drift)


def scaled(penalty, own_ref, other_refs):
    sums = own_ref[...]
    for ref in other_refs:
        sums = sums + ref[...]
    return penalty * jnp.sqrt(sums[0:1, 0:1] / (sums[0:1, 1:2] + EPSILON))


def nodes_kernel(
    S, J, HB, devices, got_ref, id_ref, mu_ref, h_ref, ml_ref, an_out, ml_out, ent_ref, sums_ref
):
    Q = J * S
    shared, means, entry_means, before, weight, gap, drift = read_nodes(
        J, HB, got_ref, id_ref[...], devices
    )
    put_sums(gap, drift + moved(weight, entry_means, before), sums_ref)
    for h in range(HB):
        at = pl.ds(h * Q, Q)
        ent_ref[h] = entry_means[h]
        anchor = jnp.where(shared, means[h], mu_ref[at, :])
        an_out[at, :] = anchor
        ml_out[at, :] = ml_ref[at, :] + RHO_START * (h_ref[at, :] - anchor)


def second_kernel(
    S, J, R, NZ, HB, pp_ref, pc_ref, hp_ref, hc_ref, cb_ref, ml_ref, an_ref, id_ref, wb_ref, sums_ref, sums2_ref, pieces_ref, *rest
):
    other_refs = rest[: R - 1]
    p_out, h_out, mu_out, send_ref, step_ref, pen_ref, all_sc = rest[R - 1 :]
    Q = J * S
    own = lax.axis_index("rows")
    slot = lambda ref, k: ref[k * Q : (k + 1) * Q, :]
    penalty = scaled(RHO_START, sums_ref, [sums2_ref])
    pen_ref[...] = jnp.broadcast_to(penalty, pen_ref.shape)
    anchors = [slot(an_ref, h) for h in range(HB)]
    hedge = [slot(ml_ref, h) + penalty * (slot(hp_ref, h) - anchors[h]) for h in range(HB)]
    placed, hedged = primal_step(
        S, J, R, NZ, HB, own, pieces_ref, other_refs, pp_ref, pc_ref, hp_ref, hc_ref, cb_ref, hedge, all_sc
    )
    finish_step(
        S, J, R, NZ, HB, own, pp_ref, placed, hedged, anchors, False, id_ref[...], wb_ref[...], p_out, h_out, mu_out, send_ref, step_ref
    )


def last_kernel(
    S, J, HB, devices, got_ref, id_ref, ent_ref, mu_ref, h_ref, ml_ref, pen_ref, ml_out, sums_ref
):
    Q = J * S
    shared, means, entry_means, before, weight, gap, drift = read_nodes(
        J, HB, got_ref, id_ref[...], devices
    )
    drift = drift + moved(weight, entry_means, [ent_ref[h] for h in range(HB)])
    put_sums(gap, drift, sums_ref)
    penalty = pen_ref[0:1, 0:1]
    for h in range(HB):
        at = pl.ds(h * Q, Q)
        anchor = jnp.where(shared, means[h], mu_ref[at, :])
        ml_out[at, :] = ml_ref[at, :] + penalty * (h_ref[at, :] - anchor)


def finish_kernel(
    S, J, HB, ml_ref, dual_ref, rhs_ref, image_ref, image2_ref, ml_out, dual_out
):
    for h in range(HB):
        for j in range(J):
            src = pl.ds(h * J * S + j * S, S)
            ml_out[pl.ds(h * J + j, S, stride=HB * J), :] = ml_ref[src, :]
    image = image_ref[...] + image2_ref[...]
    dual_out[...] = jnp.maximum(dual_ref[...] + SIGMA_STEP * (image - rhs_ref[...]), 0.0)


def penalty_kernel(pen_ref, sums_ref, sums2_ref, out_ref):
    out_ref[...] = scaled(pen_ref[0:1, 0:1], sums_ref, [sums2_ref])


def bulk_kernel(S, primal_ref, cost_ref, out_ref):
    for s in range(S):
        move = TAU_STEP * cost_ref[s].astype(F32)
        x = primal_ref[s].astype(F32)
        for _ in range(SWEEPS):
            x = jnp.maximum(x - move, 0.0)
        out_ref[s] = x


def place_kernel(S, J, R, NZ, HB, first, count, parts, cols_ref, bulk_ref, p_ref, h_ref, *rest):
    near_ref, out_hbm, sems = rest[-3:]
    K, Q = R * NZ, J * S
    step = count // parts
    copies = []
    for i in range(count):
        s = first + i
        for j in range(J):
            for k in range(K):
                c = cols_ref[k // NZ, j, k % NZ, s]
                near_ref[s, pl.ds(c * J + j, 1), :] = p_ref[pl.ds(k * Q + j * S + s, 1), :]
            for h in range(HB):
                near_ref[s, pl.ds(h * J + j, 1), :] = h_ref[pl.ds(h * Q + j * S + s, 1), :]
        if (i + 1) % step == 0:
            at = pl.ds(s + 1 - step, step)
            copies.append(
                pltpu.make_async_copy(near_ref.at[at], out_hbm.at[at], sems.at[i // step])
            )
            copies[-1].start()
    for copy in copies:
        copy.wait()


def merge_kernel(apart, x_ref, y_ref, *rest):
    out_ref = rest[-1]
    rows = x_ref.shape[0]
    high = lax.rem(lax.axis_index("scen") // apart, 2)
    out_ref[pl.ds(pl.multiple_of(high * rows, 8), rows), :] = x_ref[...]
    out_ref[pl.ds(pl.multiple_of((1 - high) * rows, 8), rows), :] = y_ref[...]


def local(
    sizes,
    lp_blocks,
    block_columns,
    scenario_nodes,
    scenario_weights,
    cost,
    bounds_rhs,
    primal_start,
    dual_start,
    multiplier_start,
    consensus_start,
):
    scens, R, sections = sizes
    S, J, columns = cost.shape
    NZ = lp_blocks.shape[3]
    hedged = multiplier_start.shape[2]
    HB, C = hedged // BLK, columns // BLK
    K, Q = R * NZ, J * S
    devices = scens
    message = -(-(2 * J * HB + 1) // 8) * 8
    message1 = -(-(4 * J * HB + 1) // 8) * 8
    static = (S, J, R, NZ, HB)

    def interleave(x):
        return x.reshape(S, J, -1, BLK).transpose(0, 2, 1, 3).reshape(S, -1, BLK)

    def uninterleave(x):
        return x.reshape(S, -1, J, BLK).transpose(0, 2, 1, 3).reshape(S, J, -1)

    columns_of = block_columns.transpose(1, 2, 3, 0)
    lp = in_hbm(lp_blocks.reshape(S, J * NZ, BLK, BLK))
    primal, price = in_hbm(interleave(primal_start)), in_vmem(interleave(cost))
    mult = interleave(multiplier_start).reshape(S * HB * J, BLK)

    def from_rows(x):
        return [
            lax.ppermute(x, "rows", [((i + q) % R, i) for i in range(R)]) for q in range(1, R)
        ]

    def from_section(x):
        return lax.ppermute(x, "section", [(i, (i + 1) % sections) for i in range(sections)])

    def partner(x, apart):
        return lax.ppermute(x, "scen", [(i, i ^ apart) for i in range(scens)])

    def merge(x, y, apart, *after):
        return pl.pallas_call(
            functools.partial(merge_kernel, apart),
            out_shape=near(2 * x.shape[0], BLK),
            in_specs=[VMEM] * 2 + [HBM if far else VMEM for far, _ in after],
            out_specs=VMEM,
            compiler_params=params(4),
            name="merge",
        )(x, y, *[in_hbm(z) if far else z for far, z in after])

    def exchange(x, *work):
        if scens & (scens - 1):
            return lax.all_gather(x, "scen", axis=0, tiled=True)
        apart, turn = scens // 2, 0
        while apart:
            y = partner(x, apart)
            x = merge(x, y, apart, *(work[turn]() if turn < len(work) else ()))
            apart, turn = apart // 2, turn + 1
        return x

    def near_like(x):
        return pltpu.VMEM(x.shape, x.dtype)

    parts = max(p for p in (4, 3, 2, 1) if S % p == 0)
    pieces, lp, primal = pl.pallas_call(
        functools.partial(pieces_kernel, S, J, NZ),
        out_shape=[near(NZ * Q, BLK), near_like(lp), near_like(primal)],
        in_specs=[HBM] * 3,
        out_specs=[VMEM] * 3,
        scratch_shapes=[
            pltpu.SemaphoreType.DMA((parts,)),
            pltpu.VMEM(dual_start.shape, F32),
            pltpu.SemaphoreType.DMA,
            pltpu.SemaphoreType.DMA,
        ],
        compiler_params=params(16),
        name="pieces",
    )(lp, in_hbm(dual_start), primal)
    others = from_rows(pieces)

    pp, pc, hp, hc, cb, ml, an, ids, wb = pl.pallas_call(
        functools.partial(setup_kernel, *static),
        out_shape=[near(K * Q, BLK)] * 2
        + [near(HB * Q, BLK)] * 2
        + [near(K * Q, BLK)]
        + [near(HB * Q, BLK)] * 2
        + [near(Q, BLK)] * 2,
        in_specs=[SMEM] * 3 + [VMEM] * 3 + [HBM],
        out_specs=[VMEM] * 9,
        scratch_shapes=[pltpu.VMEM((S * K * J, BLK), jnp.int32)]
        + [pltpu.VMEM((S * K * J, BLK), F32)] * 2
        + [pltpu.VMEM((S * HB * J, BLK), F32)] * 2
        + [pltpu.VMEM(consensus_start.shape, F32)]
        + [pltpu.SemaphoreType.DMA],
        compiler_params=params(16),
        name="setup",
    )(columns_of, scenario_nodes, scenario_weights, in_vmem(primal), price, mult, in_hbm(consensus_start))
    primal = in_vmem(primal)

    def step_out(rows):
        return [
            near(K * Q, BLK),
            near(HB * Q, BLK),
            near(HB * Q, BLK),
            near(rows, BLK),
            near(NZ * Q, BLK),
        ]

    def image_of(step):
        return pl.pallas_call(
            functools.partial(image_kernel, S, J, NZ),
            out_shape=near(S, BLK),
            in_specs=[VMEM] * 2,
            out_specs=VMEM,
            compiler_params=params(8),
            name="image",
        )(lp, step)

    scratch = [pltpu.VMEM((K * Q, BLK), F32)]
    p1, h1, mu1, send1, step1 = pl.pallas_call(
        functools.partial(first_kernel, *static),
        out_shape=step_out(message1),
        in_specs=[VMEM] * (10 + R - 1),
        out_specs=[VMEM] * 5,
        scratch_shapes=scratch,
        compiler_params=params(8),
        name="first",
    )(pp, pc, hp, hc, cb, ml, an, ids, wb, pieces, *others)
    made = {}

    def image_work():
        made["image"] = image_of(step1)
        return ((False, made["image"]),)

    def dual_work():
        made["dual"], made["pieces"] = pl.pallas_call(
            functools.partial(dual_kernel, S, J, NZ),
            out_shape=[near(S, BLK), near(NZ * Q, BLK)],
            in_specs=[VMEM] * 5,
            out_specs=[VMEM] * 2,
            compiler_params=params(8),
            name="dual",
        )(lp, dual_start, bounds_rhs, made["image"], from_section(made["image"]))
        return ((False, made["pieces"]),)

    def bulk_work():
        made["bulk"] = pl.pallas_call(
            functools.partial(bulk_kernel, S),
            out_shape=near(S, C * J, BLK),
            in_specs=[VMEM] * 2,
            out_specs=VMEM,
            compiler_params=params(8),
            name="bulk",
        )(primal, price)
        return ((False, made["bulk"]),)

    got1 = exchange(send1, image_work, dual_work, bulk_work)
    dual1, pieces2 = made["dual"], made["pieces"]
    others2 = from_rows(pieces2)

    an1, ml1, ent1, sums1 = pl.pallas_call(
        functools.partial(nodes_kernel, S, J, HB, devices),
        out_shape=[near(HB * Q, BLK)] * 2 + [near(HB, 2 * J * devices, BLK), near(8, BLK)],
        in_specs=[VMEM] * 5,
        out_specs=[VMEM] * 4,
        compiler_params=params(8),
        name="nodes",
    )(got1, ids, mu1, h1, ml)
    sums1b = from_section(sums1)

    p2, h2, mu2, send2, step2, pen1 = pl.pallas_call(
        functools.partial(second_kernel, *static),
        out_shape=step_out(message) + [near(8, BLK)],
        in_specs=[VMEM] * (12 + R - 1),
        out_specs=[VMEM] * 6,
        scratch_shapes=scratch,
        compiler_params=params(8),
        name="second",
    )(p1, pc, h1, hc, cb, ml1, an1, ids, wb, sums1, sums1b, pieces2, *others2)
    half = S // 2

    def place(first, count, whole, *into):
        cuts = max(p for p in (2, 1) if count % p == 0)
        return pl.pallas_call(
            functools.partial(place_kernel, *static, first, count, cuts),
            out_shape=[near(S, C * J, BLK), shape(S, C * J, BLK)],
            in_specs=[SMEM] + [VMEM] * 3 + [HBM] * len(into),
            out_specs=[VMEM, HBM],
            scratch_shapes=[pltpu.SemaphoreType.DMA((cuts,))],
            input_output_aliases={1: 0, 4: 1} if into else {1: 0},
            compiler_params=params(4),
            name="place",
        )(columns_of, whole, p2, h2, *into)

    def last_image_work():
        made["image"] = image_of(step2)
        return ((False, made["image"]),)

    def place_work():
        made["bulk"], made["out"] = place(0, half, made["bulk"])
        return ((True, made["out"]),)

    def rest_work():
        made["bulk"], made["out"] = place(half, S - half, made["bulk"], made["out"])
        return ((True, made["out"]),)

    got2 = exchange(send2, last_image_work, place_work, rest_work)
    out, image2 = made["out"], made["image"]
    ml2, sums2 = pl.pallas_call(
        functools.partial(last_kernel, S, J, HB, devices),
        out_shape=[near(HB * Q, BLK), near(8, BLK)],
        in_specs=[VMEM] * 7,
        out_specs=[VMEM] * 2,
        compiler_params=params(8),
        name="last",
    )(got2, ids, ent1, mu2, h2, ml1, pen1)
    ml2, dual2 = pl.pallas_call(
        functools.partial(finish_kernel, S, J, HB),
        out_shape=[shape(S * HB * J, BLK), shape(S, BLK)],
        in_specs=[VMEM] * 5,
        out_specs=[VMEM] * 2,
        compiler_params=params(4),
        name="finish",
    )(ml2, dual1, bounds_rhs, image2, from_section(image2))
    pen2 = pl.pallas_call(
        penalty_kernel,
        out_shape=shape(1, 1),
        in_specs=[VMEM] * 3,
        out_specs=VMEM,
        compiler_params=params(4),
        name="penalty",
    )(pen1, sums2, from_section(sums2))

    return (
        uninterleave(out),
        dual2,
        uninterleave(ml2.reshape(S, HB * J, BLK)),
        pen2.reshape(()),
    )


def solution(mesh):
    sizes = tuple(mesh.shape[a] for a in ("scen", "rows", "section"))
    in_specs = (
        P("scen", "rows", "section", None, None, None),
        P("scen", None, "section", None),
        P(None, "scen"),
        P("scen"),
        P("scen", "section", None),
        P("scen", "rows"),
        P("scen", "section", None),
        P("scen", "rows"),
        P("scen", "section", None),
        P(),
    )
    out_specs = (P("scen", "section", None), P("scen", "rows"), P("scen", "section", None), P())
    return jax.shard_map(
        functools.partial(local, sizes),
        mesh=mesh,
        in_specs=in_specs,
        out_specs=out_specs,
        check_vma=False,
    )
```

```python
import functools

import jax
import jax.numpy as jnp
from jax import lax
from jax.experimental import pallas as pl
from jax.experimental.pallas import tpu as pltpu
from jax.sharding import PartitionSpec as P

BLK = 128
N1 = 8
N2 = 64
SWEEPS = 2
TAU_STEP = 0.4
SIGMA_STEP = 0.4
RHO_START = 1.0
EPSILON = 1e-06
F32 = jnp.float32
BF16 = jnp.bfloat16
HIGHEST = lax.Precision.HIGHEST

VMEM = pl.BlockSpec(memory_space=pltpu.VMEM)
SMEM = pl.BlockSpec(memory_space=pltpu.SMEM)
HBM = pl.BlockSpec(memory_space=pltpu.HBM)


def params(mib=16):
    return pltpu.CompilerParams(vmem_limit_bytes=mib << 20)


def in_vmem(x):
    return pltpu.with_memory_space_constraint(x, pltpu.VMEM)


def in_hbm(x):
    return pltpu.with_memory_space_constraint(x, pltpu.HBM)


def shape(*dims):
    return jax.ShapeDtypeStruct(dims, F32)


def near(*dims):
    return pltpu.VMEM(dims, F32)


def cut(src_ref, dst_ref, sems, parts):
    step = src_ref.shape[0] // parts
    at = [pl.ds(i * step, step) for i in range(parts)]
    return [
        pltpu.make_async_copy(src_ref.at[a], dst_ref.at[a], sems.at[i]) for i, a in enumerate(at)
    ]


def write_pieces(lp_ref, dual, out_ref, S, J, NZ, before=lambda s: None):
    for s in range(S):
        before(s)
        row = dual[s : s + 1, :].astype(BF16)
        for j in range(J):
            for n in range(NZ):
                y = jnp.dot(row, lp_ref[s, j * NZ + n], preferred_element_type=F32)
                out_ref[pl.ds((n * J + j) * S + s, 1), :] = y


def image_kernel(S, J, NZ, lp_ref, step_ref, image_ref):
    for s in range(S):
        total = None
        for j in range(J):
            for n in range(NZ):
                x = step_ref[pl.ds((n * J + j) * S + s, 1), :].astype(BF16)
                y = lax.dot_general(
                    x,
                    lp_ref[s, j * NZ + n],
                    (((1,), (1,)), ((), ())),
                    preferred_element_type=F32,
                )
                total = y if total is None else total + y
        image_ref[pl.ds(s, 1), :] = total


def pieces_kernel(
    S, J, NZ, lp_hbm, dual_hbm, primal_hbm, out_ref, lp_ref, primal_ref, sems, dual_ref, sem, primal_sem
):
    parts = sems.shape[0]
    dual_copy = pltpu.make_async_copy(dual_hbm, dual_ref, sem)
    dual_copy.start()
    copies = cut(lp_hbm, lp_ref, sems, parts)
    for copy in copies:
        copy.start()
    primal_copy = pltpu.make_async_copy(primal_hbm, primal_ref, primal_sem)
    primal_copy.start()
    dual_copy.wait()

    def before(s):
        if s % (S // parts) == 0:
            copies[s // (S // parts)].wait()

    write_pieces(lp_ref, dual_ref[...], out_ref, S, J, NZ, before)
    primal_copy.wait()


def dual_kernel(S, J, NZ, lp_ref, dual_ref, rhs_ref, image_ref, image2_ref, next_ref, out_ref):
    image = image_ref[...] + image2_ref[...]
    dual = jnp.maximum(dual_ref[...] + SIGMA_STEP * (image - rhs_ref[...]), 0.0)
    next_ref[...] = dual
    write_pieces(lp_ref, dual, out_ref, S, J, NZ)


def down(row, count):
    return jnp.transpose(jnp.broadcast_to(row, (BLK, row.shape[1])))[:count]


def setup_kernel(
    S,
    J,
    R,
    NZ,
    HB,
    nodes_ref,
    weights_ref,
    cols_ref,
    primal_ref,
    cost_ref,
    mult_ref,
    table_hbm,
    pp_ref,
    pc_ref,
    hp_ref,
    hc_ref,
    cb_ref,
    ml_ref,
    an_ref,
    id_ref,
    wb_ref,
    same_ref,
    table_ref,
    idx_sc,
    pp_sc,
    pc_sc,
    hp_sc,
    hc_sc,
    table_sem,
):
    K, Q = R * NZ, J * S
    table_copy = pltpu.make_async_copy(table_hbm, table_ref, table_sem)
    table_copy.start()
    section = lax.axis_index("section")
    rows = primal_ref.shape[1]

    cols = cols_ref[...]
    section_of = lax.rem(lax.broadcasted_iota(jnp.int32, (K * J, BLK), 0) // NZ, J)
    tiles = -(-rows // BLK)
    lane = lax.broadcasted_iota(jnp.int32, (K * J, BLK), 1)
    picks = []
    for s in range(S):
        want = jnp.broadcast_to(cols[:, s : s + 1], (K * J, BLK))
        idx_sc[pl.ds(s * K * J, K * J), :] = want.astype(F32)
        want = want * J + section_of
        picks.append(
            jnp.concatenate(
                [(want == lane + t * BLK).astype(F32).astype(BF16) for t in range(tiles)], axis=1
            )[:, :rows]
        )

    def gather(source_ref, placed_ref, hedged_ref):
        for s in range(S):
            placed_ref[pl.ds(s * K * J, K * J), :] = jnp.dot(
                picks[s], source_ref[s], preferred_element_type=F32
            )
            hedged_ref[pl.ds(s * HB * J, HB * J), :] = source_ref[s, : HB * J, :].astype(F32)

    def placed_rows(k, j):
        return pl.ds(((k // NZ) * J + j) * NZ + k % NZ, S, stride=K * J), pl.ds(k * Q + j * S, S)

    def hedged_rows(h, j):
        return pl.ds(h * J + j, S, stride=HB * J), pl.ds(h * Q + j * S, S)

    gather(primal_ref, pp_sc, hp_sc)
    gather(cost_ref, pc_sc, hc_sc)
    weights = down(weights_ref[...], S)
    ids, picked = [], []
    for j in range(J):
        g = section * J + j
        own = jnp.zeros((1, nodes_ref.shape[1]), jnp.int32)
        for level, off in enumerate((1, 1 + N1, 1 + N1 + N2)):
            own = jnp.where(g == level + 1, nodes_ref[level : level + 1, :] + off, own)
        ids.append(down(own.astype(F32), S))
        picked.append(own)
        wb_ref[pl.ds(j * S, S), :] = weights
    ids = jnp.concatenate(ids, axis=0)
    id_ref[...] = ids
    across = jnp.transpose(ids)[0:1, :Q]
    same_ref[:, :Q] = (jnp.broadcast_to(ids[:, :1], (Q, Q)) == across).astype(F32)
    for j in range(J):
        for k in range(K):
            src, dst = placed_rows(k, j)
            pp_ref[dst, :] = pp_sc[src, :]
            pc_ref[dst, :] = pc_sc[src, :]
            cb_ref[dst, :] = idx_sc[src, :]
        for h in range(HB):
            src, dst = hedged_rows(h, j)
            hp_ref[dst, :] = hp_sc[src, :]
            hc_ref[dst, :] = hc_sc[src, :]
            ml_ref[dst, :] = mult_ref[src, :]
    table_copy.wait()
    for j in range(J):
        for s in range(S):
            line = table_ref[pl.ds(picked[j][0, s], 1), :]
            for h in range(HB):
                an_ref[pl.ds(h * Q + j * S + s, 1), :] = line[:, h * BLK : (h + 1) * BLK]


def total(x):
    return jnp.sum(x, axis=(0, 1), keepdims=True)


def primal_step(
    S, J, R, NZ, HB, own, pieces_ref, other_refs, p_ref, pc_ref, h_ref, hc_ref, cb_ref, hedge, all_sc
):
    K, Q = R * NZ, J * S
    for shift in range(R):
        src = pieces_ref if shift == 0 else other_refs[shift - 1]
        at = lax.rem(own + shift, R) * (NZ * Q)
        all_sc[pl.ds(pl.multiple_of(at, 8), NZ * Q), :] = src[...]
    slot = lambda ref, k: ref[k * Q : (k + 1) * Q, :]
    cols = [slot(cb_ref, k) for k in range(K)]
    parts = [slot(all_sc, k) for k in range(K)]
    placed, hedged = [], []
    for k in range(K):
        add = None
        for m in range(K):
            term = parts[m] if m == k else jnp.where(cols[m] == cols[k], parts[m], 0.0)
            add = term if add is None else add + term
        for h in range(HB):
            add = add + jnp.where(cols[k] == float(h), hedge[h], 0.0)
        placed.append(
            jnp.maximum(slot(p_ref, k) - TAU_STEP * (slot(pc_ref, k) + add), 0.0)
        )
    for h in range(HB):
        add = None
        for m in range(K):
            term = jnp.where(cols[m] == float(h), parts[m], 0.0)
            add = term if add is None else add + term
        add = add + hedge[h]
        hedged.append(jnp.maximum(slot(h_ref, h) - TAU_STEP * (slot(hc_ref, h) + add), 0.0))
    return placed, hedged


def finish_step(
    S, J, R, NZ, HB, own, p_ref, placed, hedged, anchors, ids, wb, same, p_out, h_out, mu_ref, send_ref, step_ref
):
    K, Q = R * NZ, J * S
    for k in range(K):
        p_out[k * Q : (k + 1) * Q, :] = placed[k]
    mine = pl.ds(pl.multiple_of(own * (NZ * Q), 8), NZ * Q)
    step_ref[...] = 2.0 * p_out[mine, :] - p_ref[mine, :]
    for h in range(HB):
        h_out[h * Q : (h + 1) * Q, :] = hedged[h]
    sums = jnp.dot(
        same[:, :Q],
        jnp.concatenate([wb * x for x in hedged] + [wb], axis=1),
        precision=HIGHEST,
        preferred_element_type=F32,
    )
    mass = sums[:, HB * BLK :]
    inner = []
    for j in range(J):
        mine = ids[j * S : (j + 1) * S]
        inner.append((mine != mine[:1]) & (mine != mine[S - 1 :]))
    inner = jnp.concatenate([x.astype(F32) for x in inner], axis=0)
    gap, drift = jnp.zeros((Q, BLK), F32), jnp.zeros((Q, BLK), F32)
    for h in range(HB):
        mu = sums[:, h * BLK : (h + 1) * BLK] / mass
        mu_ref[h * Q : (h + 1) * Q, :] = mu
        gap = gap + wb * (hedged[h] - mu) ** 2
        drift = drift + (wb * inner) * (mu - anchors[h]) ** 2
    lane = lax.broadcasted_iota(jnp.int32, (1, BLK), 1)
    note = jnp.zeros((1, BLK), F32)
    for j in range(J):
        a, b = j * S, j * S + S - 1
        fresh = ids[b : b + 1] != ids[a : a + 1]
        for f in range(2):
            e = f * J + j
            at = b if f else a
            for h in range(HB):
                line = sums[at : at + 1, h * BLK : (h + 1) * BLK]
                send_ref[pl.ds(e * HB + h, 1), :] = jnp.where(fresh, line, 0.0) if f else line
            name, weight = ids[at : at + 1], mass[at : at + 1]
            if f:
                name, weight = jnp.where(fresh, name, -1.0), jnp.where(fresh, weight, 0.0)
            note = jnp.where(lane == e, name, note)
            note = jnp.where(lane == 2 * J + e, weight, note)
    note = jnp.where(lane == 4 * J, total(gap), note)
    note = jnp.where(lane == 4 * J + 1, total(drift), note)
    at = 2 * J * HB
    send_ref[pl.ds(2 * J * HB, 1), :] = note
    send_ref[pl.ds(at + 1, send_ref.shape[0] - at - 1), :] = jnp.zeros(
        (send_ref.shape[0] - at - 1, BLK), F32
    )


def first_kernel(
    S, J, R, NZ, HB, pp_ref, pc_ref, hp_ref, hc_ref, cb_ref, ml_ref, an_ref, id_ref, wb_ref, same_ref, pieces_ref, *rest
):
    other_refs = rest[: R - 1]
    p_out, h_out, mu_ref, send_ref, step_ref, all_sc = rest[R - 1 :]
    Q = J * S
    own = lax.axis_index("rows")
    slot = lambda ref, k: ref[k * Q : (k + 1) * Q, :]
    anchors = [slot(an_ref, h) for h in range(HB)]
    hedge = [
        slot(ml_ref, h) + RHO_START * (slot(hp_ref, h) - anchors[h]) for h in range(HB)
    ]
    placed, hedged = primal_step(
        S, J, R, NZ, HB, own, pieces_ref, other_refs, pp_ref, pc_ref, hp_ref, hc_ref, cb_ref, hedge, all_sc
    )
    finish_step(
        S, J, R, NZ, HB, own, pp_ref, placed, hedged, anchors, id_ref[...], wb_ref[...], same_ref[...], p_out, h_out, mu_ref, send_ref, step_ref
    )


def read_nodes(J, HB, got_ref, ids, devices):
    E = 2 * J
    sums = [
        jnp.concatenate(
            [got_ref[pl.ds(e * HB + h, devices, stride=E * HB), :] for e in range(E)], axis=0
        )
        for h in range(HB)
    ]
    notes = got_ref[pl.ds(E * HB * devices, devices), :]
    wide = lambda at: jnp.broadcast_to(notes[:, at : at + 1], (devices, BLK))
    names = jnp.concatenate([wide(e) for e in range(E)], axis=0)
    weight = jnp.concatenate([wide(E + e) for e in range(E)], axis=0)
    every = jnp.concatenate([ids, names], axis=0)
    across = jnp.transpose(names)[0:1, :]
    count = E * devices
    same = (jnp.broadcast_to(every[:, :1], (every.shape[0], count)) == across).astype(F32)
    totals = jnp.dot(
        same,
        jnp.concatenate(sums + [weight], axis=1),
        precision=HIGHEST,
        preferred_element_type=F32,
    )
    mass = totals[:, HB * BLK :]
    positive = mass > 0
    safe = jnp.where(positive, mass, 1.0)
    means = [
        jnp.where(positive, totals[:, h * BLK : (h + 1) * BLK] / safe, 0.0) for h in range(HB)
    ]
    own_safe = jnp.where(weight > 0, weight, 1.0)
    gap = total(notes[:, 2 * E : 2 * E + 1])
    drift = total(notes[:, 2 * E + 1 : 2 * E + 2])
    rows = ids.shape[0]
    spread = jnp.zeros((count, BLK), F32)
    for h in range(HB):
        spread = spread + weight * (sums[h] / own_safe - means[h][rows:]) ** 2
    gap = gap + total(spread)
    return positive[:rows], [m[:rows] for m in means], [m[rows:] for m in means], weight, gap, drift


def moved(weight, means, before):
    change = jnp.zeros_like(weight)
    for mean, old in zip(means, before):
        change = change + weight * (mean - old) ** 2
    return total(change)


def put_sums(gap, drift, out_ref):
    lane = lax.broadcasted_iota(jnp.int32, out_ref.shape, 1)
    out_ref[...] = jnp.where(lane == 0, gap, drift)


def scaled(penalty, own_ref, other_refs):
    sums = own_ref[...]
    for ref in other_refs:
        sums = sums + ref[...]
    return penalty * jnp.sqrt(sums[0:1, 0:1] / (sums[0:1, 1:2] + EPSILON))


def nodes_kernel(
    S, J, HB, devices, got_ref, id_ref, mu_ref, h_ref, ml_ref, table_ref, an_out, ml_out, ent_ref, sums_ref, old_sc
):
    Q, E = J * S, 2 * J
    names = jnp.maximum(got_ref[pl.ds(E * HB * devices, devices), :], 0.0).astype(jnp.int32)
    shared, means, entry_means, weight, gap, drift = read_nodes(
        J, HB, got_ref, id_ref[...], devices
    )
    for h in range(HB):
        at = pl.ds(h * Q, Q)
        ent_ref[h] = entry_means[h]
        anchor = jnp.where(shared, means[h], mu_ref[at, :])
        an_out[at, :] = anchor
        ml_out[at, :] = ml_ref[at, :] + RHO_START * (h_ref[at, :] - anchor)
    for e in range(E):
        for d in range(devices):
            old_sc[pl.ds(e * devices + d, 1), :] = table_ref[pl.ds(names[d, e], 1), :]
    before = [old_sc[:, h * BLK : (h + 1) * BLK] for h in range(HB)]
    put_sums(gap, drift + moved(weight, entry_means, before), sums_ref)


def second_kernel(
    S, J, R, NZ, HB, pp_ref, pc_ref, hp_ref, hc_ref, cb_ref, ml_ref, an_ref, id_ref, wb_ref, same_ref, sums_ref, sums2_ref, pieces_ref, *rest
):
    other_refs = rest[: R - 1]
    p_out, h_out, mu_out, send_ref, step_ref, pen_ref, all_sc = rest[R - 1 :]
    Q = J * S
    own = lax.axis_index("rows")
    slot = lambda ref, k: ref[k * Q : (k + 1) * Q, :]
    penalty = scaled(RHO_START, sums_ref, [sums2_ref])
    pen_ref[...] = jnp.broadcast_to(penalty, pen_ref.shape)
    anchors = [slot(an_ref, h) for h in range(HB)]
    hedge = [slot(ml_ref, h) + penalty * (slot(hp_ref, h) - anchors[h]) for h in range(HB)]
    placed, hedged = primal_step(
        S, J, R, NZ, HB, own, pieces_ref, other_refs, pp_ref, pc_ref, hp_ref, hc_ref, cb_ref, hedge, all_sc
    )
    finish_step(
        S, J, R, NZ, HB, own, pp_ref, placed, hedged, anchors, id_ref[...], wb_ref[...], same_ref[...], p_out, h_out, mu_out, send_ref, step_ref
    )


def last_kernel(
    S, J, HB, devices, got_ref, id_ref, ent_ref, mu_ref, h_ref, ml_ref, pen_ref, ml_out, sums_ref
):
    Q = J * S
    shared, means, entry_means, weight, gap, drift = read_nodes(
        J, HB, got_ref, id_ref[...], devices
    )
    drift = drift + moved(weight, entry_means, [ent_ref[h] for h in range(HB)])
    put_sums(gap, drift, sums_ref)
    penalty = pen_ref[0:1, 0:1]
    for h in range(HB):
        at = pl.ds(h * Q, Q)
        anchor = jnp.where(shared, means[h], mu_ref[at, :])
        ml_out[at, :] = ml_ref[at, :] + penalty * (h_ref[at, :] - anchor)


def finish_kernel(
    S, J, HB, ml_ref, dual_ref, rhs_ref, image_ref, image2_ref, ml_out, dual_out
):
    for h in range(HB):
        for j in range(J):
            src = pl.ds(h * J * S + j * S, S)
            ml_out[pl.ds(h * J + j, S, stride=HB * J), :] = ml_ref[src, :]
    image = image_ref[...] + image2_ref[...]
    dual_out[...] = jnp.maximum(dual_ref[...] + SIGMA_STEP * (image - rhs_ref[...]), 0.0)


def penalty_kernel(pen_ref, sums_ref, sums2_ref, out_ref):
    out_ref[...] = scaled(pen_ref[0:1, 0:1], sums_ref, [sums2_ref])


def bulk_kernel(S, primal_ref, cost_ref, out_ref):
    for s in range(S):
        move = TAU_STEP * cost_ref[s].astype(F32)
        x = primal_ref[s].astype(F32)
        for _ in range(SWEEPS):
            x = jnp.maximum(x - move, 0.0)
        out_ref[s] = x


def place_kernel(S, J, R, NZ, HB, first, count, parts, cols_ref, bulk_ref, p_ref, h_ref, *rest):
    near_ref, out_hbm, sems = rest[-3:]
    K, Q = R * NZ, J * S
    step = count // parts
    copies = []
    for i in range(count):
        s = first + i
        for j in range(J):
            for k in range(K):
                c = cols_ref[k // NZ, j, k % NZ, s]
                near_ref[s, pl.ds(c * J + j, 1), :] = p_ref[pl.ds(k * Q + j * S + s, 1), :]
            for h in range(HB):
                near_ref[s, pl.ds(h * J + j, 1), :] = h_ref[pl.ds(h * Q + j * S + s, 1), :]
        if (i + 1) % step == 0:
            at = pl.ds(s + 1 - step, step)
            copies.append(
                pltpu.make_async_copy(near_ref.at[at], out_hbm.at[at], sems.at[i // step])
            )
            copies[-1].start()
    for copy in copies:
        copy.wait()


def merge_kernel(apart, count, sums, x_ref, y_ref, *rest):
    out_ref = rest[-1]
    rows = count * sums
    high = lax.rem(lax.axis_index("scen") // apart, 2)
    for place, ref in ((high, x_ref), (1 - high, y_ref)):
        out_ref[pl.ds(pl.multiple_of(place * rows, 8), rows), :] = ref[:rows, :]
        for i in range(count):
            out_ref[pl.ds(2 * rows + place * count + i, 1), :] = ref[rows + i : rows + i + 1, :]
    used = 2 * rows + 2 * count
    if out_ref.shape[0] > used:
        out_ref[used:, :] = jnp.zeros((out_ref.shape[0] - used, BLK), F32)


def local(
    sizes,
    lp_blocks,
    block_columns,
    scenario_nodes,
    scenario_weights,
    cost,
    bounds_rhs,
    primal_start,
    dual_start,
    multiplier_start,
    consensus_start,
):
    scens, R, sections = sizes
    S, J, columns = cost.shape
    NZ = lp_blocks.shape[3]
    hedged = multiplier_start.shape[2]
    HB, C = hedged // BLK, columns // BLK
    K, Q = R * NZ, J * S
    devices = scens
    message = -(-(2 * J * HB + 1) // 8) * 8
    static = (S, J, R, NZ, HB)

    def interleave(x):
        return x.reshape(S, J, -1, BLK).transpose(0, 2, 1, 3).reshape(S, -1, BLK)

    def uninterleave(x):
        return x.reshape(S, -1, J, BLK).transpose(0, 2, 1, 3).reshape(S, J, -1)

    columns_of = block_columns.transpose(1, 2, 3, 0)
    lp = in_hbm(lp_blocks.reshape(S, J * NZ, BLK, BLK))
    primal, price = in_hbm(interleave(primal_start)), in_vmem(interleave(cost))
    mult = interleave(multiplier_start).reshape(S * HB * J, BLK)

    def from_rows(x):
        return [
            lax.ppermute(x, "rows", [((i + q) % R, i) for i in range(R)]) for q in range(1, R)
        ]

    def from_section(x):
        return lax.ppermute(x, "section", [(i, (i + 1) % sections) for i in range(sections)])

    def partner(x, apart):
        return lax.ppermute(x, "scen", [(i, i ^ apart) for i in range(scens)])

    def merge(x, y, apart, count, least, *after):
        rows = max(least, 2 * count * (2 * J * HB) + -(-2 * count // 8) * 8)
        return pl.pallas_call(
            functools.partial(merge_kernel, apart, count, 2 * J * HB),
            out_shape=near(rows, BLK),
            in_specs=[VMEM] * 2 + [HBM if far else VMEM for far, _ in after],
            out_specs=VMEM,
            compiler_params=params(4),
            name="merge",
        )(x, y, *[in_hbm(z) if far else z for far, z in after])

    def exchange(x, least, *work):
        assert scens & (scens - 1) == 0
        apart, turn = scens // 2, 0
        while apart:
            y = partner(x, apart)
            x = merge(x, y, apart, 1 << turn, least if apart == 2 else 0, *(work[turn]() if turn < len(work) else ()))
            apart, turn = apart // 2, turn + 1
        return x

    def near_like(x):
        return pltpu.VMEM(x.shape, x.dtype)

    parts = max(p for p in (4, 3, 2, 1) if S % p == 0)
    pieces, lp, primal = pl.pallas_call(
        functools.partial(pieces_kernel, S, J, NZ),
        out_shape=[near(NZ * Q, BLK), near_like(lp), near_like(primal)],
        in_specs=[HBM] * 3,
        out_specs=[VMEM] * 3,
        scratch_shapes=[
            pltpu.SemaphoreType.DMA((parts,)),
            pltpu.VMEM(dual_start.shape, F32),
            pltpu.SemaphoreType.DMA,
            pltpu.SemaphoreType.DMA,
        ],
        compiler_params=params(16),
        name="pieces",
    )(lp, in_hbm(dual_start), primal)
    others = from_rows(pieces)

    pp, pc, hp, hc, cb, ml, an, ids, wb, same, table = pl.pallas_call(
        functools.partial(setup_kernel, *static),
        out_shape=[near(K * Q, BLK)] * 2
        + [near(HB * Q, BLK)] * 2
        + [near(K * Q, BLK)]
        + [near(HB * Q, BLK)] * 2
        + [near(Q, BLK)] * 3
        + [near_like(consensus_start)],
        in_specs=[VMEM] * 6 + [HBM],
        out_specs=[VMEM] * 11,
        scratch_shapes=[pltpu.VMEM((S * K * J, BLK), F32)] * 3
        + [pltpu.VMEM((S * HB * J, BLK), F32)] * 2
        + [pltpu.SemaphoreType.DMA],
        compiler_params=params(16),
        name="setup",
    )(
        scenario_nodes,
        scenario_weights.reshape(1, S),
        columns_of.reshape(K * J, S),
        in_vmem(primal),
        price,
        mult,
        in_hbm(consensus_start),
    )
    primal = in_vmem(primal)

    def step_out(rows):
        return [
            near(K * Q, BLK),
            near(HB * Q, BLK),
            near(HB * Q, BLK),
            near(rows, BLK),
            near(NZ * Q, BLK),
        ]

    def image_of(step):
        return pl.pallas_call(
            functools.partial(image_kernel, S, J, NZ),
            out_shape=near(S, BLK),
            in_specs=[VMEM] * 2,
            out_specs=VMEM,
            compiler_params=params(8),
            name="image",
        )(lp, step)

    scratch = [pltpu.VMEM((K * Q, BLK), F32)]
    p1, h1, mu1, send1, step1 = pl.pallas_call(
        functools.partial(first_kernel, *static),
        out_shape=step_out(message),
        in_specs=[VMEM] * (11 + R - 1),
        out_specs=[VMEM] * 5,
        scratch_shapes=scratch,
        compiler_params=params(8),
        name="first",
    )(pp, pc, hp, hc, cb, ml, an, ids, wb, same, pieces, *others)
    made = {}

    def image_work():
        made["image"] = image_of(step1)
        return ((False, made["image"]),)

    def dual_work():
        made["bulk"] = pl.pallas_call(
            functools.partial(bulk_kernel, S),
            out_shape=near(S, C * J, BLK),
            in_specs=[VMEM] * 2,
            out_specs=VMEM,
            compiler_params=params(8),
            name="bulk",
        )(primal, price)
        made["dual"], made["pieces"] = pl.pallas_call(
            functools.partial(dual_kernel, S, J, NZ),
            out_shape=[near(S, BLK), near(NZ * Q, BLK)],
            in_specs=[VMEM] * 5,
            out_specs=[VMEM] * 2,
            compiler_params=params(8),
            name="dual",
        )(lp, dual_start, bounds_rhs, made["image"], from_section(made["image"]))
        return ((False, made["pieces"]), (False, made["bulk"]))

    got1 = exchange(send1, NZ * Q, image_work, dual_work)
    dual1, pieces2 = made["dual"], made["pieces"]
    others2 = from_rows(pieces2)

    an1, ml1, ent1, sums1 = pl.pallas_call(
        functools.partial(nodes_kernel, S, J, HB, devices),
        out_shape=[near(HB * Q, BLK)] * 2 + [near(HB, 2 * J * devices, BLK), near(8, BLK)],
        in_specs=[VMEM] * 6,
        out_specs=[VMEM] * 4,
        scratch_shapes=[
            pltpu.VMEM((2 * J * devices, hedged), F32),
        ],
        compiler_params=params(8),
        name="nodes",
    )(got1, ids, mu1, h1, ml, table)
    sums1b = from_section(sums1)

    p2, h2, mu2, send2, step2, pen1 = pl.pallas_call(
        functools.partial(second_kernel, *static),
        out_shape=step_out(message) + [near(8, BLK)],
        in_specs=[VMEM] * (13 + R - 1),
        out_specs=[VMEM] * 6,
        scratch_shapes=scratch,
        compiler_params=params(8),
        name="second",
    )(p1, pc, h1, hc, cb, ml1, an1, ids, wb, same, sums1, sums1b, pieces2, *others2)
    half = S // 2

    def place(first, count, whole, *into):
        cuts = max(p for p in (2, 1) if count % p == 0)
        return pl.pallas_call(
            functools.partial(place_kernel, *static, first, count, cuts),
            out_shape=[near(S, C * J, BLK), shape(S, C * J, BLK)],
            in_specs=[SMEM] + [VMEM] * 3 + [HBM] * len(into),
            out_specs=[VMEM, HBM],
            scratch_shapes=[pltpu.SemaphoreType.DMA((cuts,))],
            input_output_aliases={1: 0, 4: 1} if into else {1: 0},
            compiler_params=params(4),
            name="place",
        )(columns_of, whole, p2, h2, *into)

    def last_image_work():
        made["image"] = image_of(step2)
        return ((False, made["image"]),)

    def place_work():
        made["bulk"], made["out"] = place(0, half, made["bulk"])
        return ((True, made["out"]),)

    def rest_work():
        made["bulk"], made["out"] = place(half, S - half, made["bulk"], made["out"])
        return ((True, made["out"]),)

    got2 = exchange(send2, 0, last_image_work, place_work, rest_work)
    out, image2 = made["out"], made["image"]
    ml2, sums2 = pl.pallas_call(
        functools.partial(last_kernel, S, J, HB, devices),
        out_shape=[near(HB * Q, BLK), near(8, BLK)],
        in_specs=[VMEM] * 7,
        out_specs=[VMEM] * 2,
        compiler_params=params(8),
        name="last",
    )(got2, ids, ent1, mu2, h2, ml1, pen1)
    ml2, dual2 = pl.pallas_call(
        functools.partial(finish_kernel, S, J, HB),
        out_shape=[shape(S * HB * J, BLK), shape(S, BLK)],
        in_specs=[VMEM] * 5,
        out_specs=[VMEM] * 2,
        compiler_params=params(4),
        name="finish",
    )(ml2, dual1, bounds_rhs, image2, from_section(image2))
    pen2 = pl.pallas_call(
        penalty_kernel,
        out_shape=shape(1, 1),
        in_specs=[VMEM] * 3,
        out_specs=VMEM,
        compiler_params=params(4),
        name="penalty",
    )(pen1, sums2, from_section(sums2))

    return (
        uninterleave(out),
        dual2,
        uninterleave(ml2.reshape(S, HB * J, BLK)),
        pen2.reshape(()),
    )


def solution(mesh):
    sizes = tuple(mesh.shape[a] for a in ("scen", "rows", "section"))
    in_specs = (
        P("scen", "rows", "section", None, None, None),
        P("scen", None, "section", None),
        P(None, "scen"),
        P("scen"),
        P("scen", "section", None),
        P("scen", "rows"),
        P("scen", "section", None),
        P("scen", "rows"),
        P("scen", "section", None),
        P(),
    )
    out_specs = (P("scen", "section", None), P("scen", "rows"), P("scen", "section", None), P())
    return jax.shard_map(
        functools.partial(local, sizes),
        mesh=mesh,
        in_specs=in_specs,
        out_specs=out_specs,
        check_vma=False,
    )
```

```python
import functools

import jax
import jax.numpy as jnp
from jax import lax
from jax.experimental import pallas as pl
from jax.experimental.pallas import tpu as pltpu
from jax.sharding import PartitionSpec as P

BLK = 128
N1 = 8
N2 = 64
SWEEPS = 2
TAU_STEP = 0.4
SIGMA_STEP = 0.4
RHO_START = 1.0
EPSILON = 1e-06
F32 = jnp.float32
BF16 = jnp.bfloat16
NOTES = 3

VMEM = pl.BlockSpec(memory_space=pltpu.VMEM)
SMEM = pl.BlockSpec(memory_space=pltpu.SMEM)
HBM = pl.BlockSpec(memory_space=pltpu.HBM)


def params(mib=16):
    return pltpu.CompilerParams(vmem_limit_bytes=mib << 20)


def in_vmem(x):
    return pltpu.with_memory_space_constraint(x, pltpu.VMEM)


def in_hbm(x):
    return pltpu.with_memory_space_constraint(x, pltpu.HBM)


def shape(*dims):
    return jax.ShapeDtypeStruct(dims, F32)


def near(*dims):
    return pltpu.VMEM(dims, F32)


def cut(src_ref, dst_ref, sems, parts):
    step = src_ref.shape[0] // parts
    at = [pl.ds(i * step, step) for i in range(parts)]
    return [
        pltpu.make_async_copy(src_ref.at[a], dst_ref.at[a], sems.at[i]) for i, a in enumerate(at)
    ]


def write_pieces(lp_ref, dual, out_ref, S, J, NZ, before=lambda s: None):
    for s in range(S):
        before(s)
        row = dual[s : s + 1, :].astype(BF16)
        for j in range(J):
            for n in range(NZ):
                y = jnp.dot(row, lp_ref[s, j * NZ + n], preferred_element_type=F32)
                out_ref[pl.ds((n * J + j) * S + s, 1), :] = y


def image_kernel(S, J, NZ, lp_ref, step_ref, image_ref):
    for s in range(S):
        total = None
        for j in range(J):
            for n in range(NZ):
                x = step_ref[pl.ds((n * J + j) * S + s, 1), :].astype(BF16)
                y = lax.dot_general(
                    x,
                    lp_ref[s, j * NZ + n],
                    (((1,), (1,)), ((), ())),
                    preferred_element_type=F32,
                )
                total = y if total is None else total + y
        image_ref[pl.ds(s, 1), :] = total


def pieces_kernel(
    S, J, NZ, lp_hbm, dual_hbm, primal_hbm, out_ref, lp_ref, primal_ref, sems, dual_ref, sem, primal_sem
):
    parts = sems.shape[0]
    dual_copy = pltpu.make_async_copy(dual_hbm, dual_ref, sem)
    dual_copy.start()
    copies = cut(lp_hbm, lp_ref, sems, parts)
    for copy in copies:
        copy.start()
    primal_copy = pltpu.make_async_copy(primal_hbm, primal_ref, primal_sem)
    primal_copy.start()
    dual_copy.wait()

    def before(s):
        if s % (S // parts) == 0:
            copies[s // (S // parts)].wait()

    write_pieces(lp_ref, dual_ref[...], out_ref, S, J, NZ, before)
    primal_copy.wait()


def dual_kernel(S, J, NZ, lp_ref, dual_ref, rhs_ref, image_ref, image2_ref, next_ref, out_ref):
    image = image_ref[...] + image2_ref[...]
    dual = jnp.maximum(dual_ref[...] + SIGMA_STEP * (image - rhs_ref[...]), 0.0)
    next_ref[...] = dual
    write_pieces(lp_ref, dual, out_ref, S, J, NZ)


def down(row, count):
    return jnp.transpose(jnp.broadcast_to(row, (BLK, row.shape[1])))[:count]


def setup_kernel(
    S,
    J,
    R,
    NZ,
    HB,
    nodes_ref,
    weights_ref,
    cols_ref,
    primal_ref,
    cost_ref,
    mult_ref,
    table_hbm,
    pp_ref,
    pc_ref,
    hp_ref,
    hc_ref,
    cb_ref,
    ml_ref,
    an_ref,
    id_ref,
    wb_ref,
    same_ref,
    table_ref,
    idx_sc,
    pp_sc,
    pc_sc,
    hp_sc,
    hc_sc,
    table_sem,
):
    K, Q = R * NZ, J * S
    table_copy = pltpu.make_async_copy(table_hbm, table_ref, table_sem)
    table_copy.start()
    section = lax.axis_index("section")
    rows = primal_ref.shape[1]

    cols = cols_ref[...]
    section_of = lax.rem(lax.broadcasted_iota(jnp.int32, (K * J, BLK), 0) // NZ, J)
    tiles = -(-rows // BLK)
    lane = lax.broadcasted_iota(jnp.int32, (K * J, BLK), 1)
    picks = []
    for s in range(S):
        want = jnp.broadcast_to(cols[:, s : s + 1], (K * J, BLK))
        idx_sc[pl.ds(s * K * J, K * J), :] = want.astype(F32)
        want = want * J + section_of
        picks.append(
            jnp.concatenate(
                [(want == lane + t * BLK).astype(F32).astype(BF16) for t in range(tiles)], axis=1
            )[:, :rows]
        )

    def gather(source_ref, placed_ref, hedged_ref):
        for s in range(S):
            placed_ref[pl.ds(s * K * J, K * J), :] = jnp.dot(
                picks[s], source_ref[s], preferred_element_type=F32
            )
            hedged_ref[pl.ds(s * HB * J, HB * J), :] = source_ref[s, : HB * J, :].astype(F32)

    def placed_rows(k, j):
        return pl.ds(((k // NZ) * J + j) * NZ + k % NZ, S, stride=K * J), pl.ds(k * Q + j * S, S)

    def hedged_rows(h, j):
        return pl.ds(h * J + j, S, stride=HB * J), pl.ds(h * Q + j * S, S)

    gather(primal_ref, pp_sc, hp_sc)
    gather(cost_ref, pc_sc, hc_sc)
    weights = down(weights_ref[...], S)
    ids, picked = [], []
    for j in range(J):
        g = section * J + j
        own = jnp.zeros((1, nodes_ref.shape[1]), jnp.int32)
        for level, off in enumerate((1, 1 + N1, 1 + N1 + N2)):
            own = jnp.where(g == level + 1, nodes_ref[level : level + 1, :] + off, own)
        ids.append(down(own.astype(F32), S))
        picked.append(own)
        wb_ref[pl.ds(j * S, S), :] = weights
    ids = jnp.concatenate(ids, axis=0)
    id_ref[...] = ids
    across = jnp.transpose(ids)[0:1, :Q]
    same_ref[:, :Q] = (jnp.broadcast_to(ids[:, :1], (Q, Q)) == across).astype(F32)
    for j in range(J):
        for k in range(K):
            src, dst = placed_rows(k, j)
            pp_ref[dst, :] = pp_sc[src, :]
            pc_ref[dst, :] = pc_sc[src, :]
            cb_ref[dst, :] = idx_sc[src, :]
        for h in range(HB):
            src, dst = hedged_rows(h, j)
            hp_ref[dst, :] = hp_sc[src, :]
            hc_ref[dst, :] = hc_sc[src, :]
            ml_ref[dst, :] = mult_ref[src, :]
    table_copy.wait()
    for j in range(J):
        for s in range(S):
            line = table_ref[pl.ds(picked[j][0, s], 1), :]
            for h in range(HB):
                an_ref[pl.ds(h * Q + j * S + s, 1), :] = line[:, h * BLK : (h + 1) * BLK]


def added(x):
    return jnp.sum(x, axis=0, keepdims=True)


def chosen_sums(same, x):
    same, sums = same.astype(BF16), None
    for _ in range(3):
        part = x.astype(BF16)
        y = jnp.dot(same, part, preferred_element_type=F32)
        sums = y if sums is None else sums + y
        x = x - part.astype(F32)
    return sums


def primal_step(
    S, J, R, NZ, HB, own, pieces_ref, other_refs, p_ref, pc_ref, h_ref, hc_ref, cb_ref, hedge, all_sc
):
    K, Q = R * NZ, J * S
    for shift in range(R):
        src = pieces_ref if shift == 0 else other_refs[shift - 1]
        at = lax.rem(own + shift, R) * (NZ * Q)
        all_sc[pl.ds(pl.multiple_of(at, 8), NZ * Q), :] = src[...]
    slot = lambda ref, k: ref[k * Q : (k + 1) * Q, :]
    cols = [slot(cb_ref, k) for k in range(K)]
    parts = [slot(all_sc, k) for k in range(K)]
    placed, hedged = [], []
    for k in range(K):
        add = None
        for m in range(K):
            term = parts[m] if m == k else jnp.where(cols[m] == cols[k], parts[m], 0.0)
            add = term if add is None else add + term
        for h in range(HB):
            add = add + jnp.where(cols[k] == float(h), hedge[h], 0.0)
        placed.append(
            jnp.maximum(slot(p_ref, k) - TAU_STEP * (slot(pc_ref, k) + add), 0.0)
        )
    for h in range(HB):
        add = None
        for m in range(K):
            term = jnp.where(cols[m] == float(h), parts[m], 0.0)
            add = term if add is None else add + term
        add = add + hedge[h]
        hedged.append(jnp.maximum(slot(h_ref, h) - TAU_STEP * (slot(hc_ref, h) + add), 0.0))
    return placed, hedged


def finish_step(
    S, J, R, NZ, HB, own, p_ref, placed, hedged, anchors, ids, wb, same, p_out, h_out, mu_ref, send_ref, step_ref
):
    K, Q = R * NZ, J * S
    for k in range(K):
        p_out[k * Q : (k + 1) * Q, :] = placed[k]
    mine = pl.ds(pl.multiple_of(own * (NZ * Q), 8), NZ * Q)
    step_ref[...] = 2.0 * p_out[mine, :] - p_ref[mine, :]
    for h in range(HB):
        h_out[h * Q : (h + 1) * Q, :] = hedged[h]
    sums = chosen_sums(same[:, :Q], jnp.concatenate([wb * x for x in hedged] + [wb], axis=1))
    mass = sums[:, HB * BLK :]
    inner = []
    for j in range(J):
        mine = ids[j * S : (j + 1) * S]
        inner.append((mine != mine[:1]) & (mine != mine[S - 1 :]))
    inner = jnp.concatenate([x.astype(F32) for x in inner], axis=0)
    gap, drift = jnp.zeros((Q, BLK), F32), jnp.zeros((Q, BLK), F32)
    for h in range(HB):
        mu = sums[:, h * BLK : (h + 1) * BLK] / mass
        mu_ref[h * Q : (h + 1) * Q, :] = mu
        gap = gap + wb * (hedged[h] - mu) ** 2
        drift = drift + (wb * inner) * (mu - anchors[h]) ** 2
    lane = lax.broadcasted_iota(jnp.int32, (1, BLK), 1)
    note = jnp.zeros((1, BLK), F32)
    for j in range(J):
        a, b = j * S, j * S + S - 1
        fresh = ids[b : b + 1] != ids[a : a + 1]
        for f in range(2):
            e = f * J + j
            at = b if f else a
            for h in range(HB):
                line = sums[at : at + 1, h * BLK : (h + 1) * BLK]
                send_ref[pl.ds(e * HB + h, 1), :] = jnp.where(fresh, line, 0.0) if f else line
            name, weight = ids[at : at + 1], mass[at : at + 1]
            if f:
                name, weight = jnp.where(fresh, name, -1.0), jnp.where(fresh, weight, 0.0)
            note = jnp.where(lane == e, name, note)
            note = jnp.where(lane == 2 * J + e, weight, note)
    at = 2 * J * HB
    for i, row in enumerate((note, added(gap), added(drift))):
        send_ref[pl.ds(at + i, 1), :] = row
    rest = send_ref.shape[0] - at - NOTES
    send_ref[pl.ds(at + NOTES, rest), :] = jnp.zeros((rest, BLK), F32)


def first_kernel(
    S, J, R, NZ, HB, pp_ref, pc_ref, hp_ref, hc_ref, cb_ref, ml_ref, an_ref, id_ref, wb_ref, same_ref, pieces_ref, *rest
):
    other_refs = rest[: R - 1]
    p_out, h_out, mu_ref, send_ref, step_ref, all_sc = rest[R - 1 :]
    Q = J * S
    own = lax.axis_index("rows")
    slot = lambda ref, k: ref[k * Q : (k + 1) * Q, :]
    anchors = [slot(an_ref, h) for h in range(HB)]
    hedge = [
        slot(ml_ref, h) + RHO_START * (slot(hp_ref, h) - anchors[h]) for h in range(HB)
    ]
    placed, hedged = primal_step(
        S, J, R, NZ, HB, own, pieces_ref, other_refs, pp_ref, pc_ref, hp_ref, hc_ref, cb_ref, hedge, all_sc
    )
    finish_step(
        S, J, R, NZ, HB, own, pp_ref, placed, hedged, anchors, id_ref[...], wb_ref[...], same_ref[...], p_out, h_out, mu_ref, send_ref, step_ref
    )


def read_nodes(J, HB, got_ref, ids, devices):
    E = 2 * J
    sums = [
        jnp.concatenate(
            [got_ref[pl.ds(e * HB + h, devices, stride=E * HB), :] for e in range(E)], axis=0
        )
        for h in range(HB)
    ]
    notes, gaps, drifts = (
        got_ref[pl.ds(E * HB * devices + i, devices, stride=NOTES), :] for i in range(NOTES)
    )
    wide = lambda at: jnp.broadcast_to(notes[:, at : at + 1], (devices, BLK))
    names = jnp.concatenate([wide(e) for e in range(E)], axis=0)
    weight = jnp.concatenate([wide(E + e) for e in range(E)], axis=0)
    every = jnp.concatenate([ids, names], axis=0)
    across = jnp.transpose(names)[0:1, :]
    count = E * devices
    same = (jnp.broadcast_to(every[:, :1], (every.shape[0], count)) == across).astype(F32)
    totals = chosen_sums(same, jnp.concatenate(sums + [weight], axis=1))
    mass = totals[:, HB * BLK :]
    positive = mass > 0
    safe = jnp.where(positive, mass, 1.0)
    means = [
        jnp.where(positive, totals[:, h * BLK : (h + 1) * BLK] / safe, 0.0) for h in range(HB)
    ]
    own_safe = jnp.where(weight > 0, weight, 1.0)
    rows = ids.shape[0]
    spread = jnp.zeros((count, BLK), F32)
    for h in range(HB):
        spread = spread + weight * (sums[h] / own_safe - means[h][rows:]) ** 2
    gap, drift = added(gaps) + added(spread), added(drifts)
    return positive[:rows], [m[:rows] for m in means], [m[rows:] for m in means], weight, gap, drift


def moved(weight, means, before):
    change = jnp.zeros_like(weight)
    for mean, old in zip(means, before):
        change = change + weight * (mean - old) ** 2
    return added(change)


def put_sums(gap, drift, out_ref):
    out_ref[...] = jnp.concatenate(
        [gap, drift, jnp.zeros((out_ref.shape[0] - 2, BLK), F32)], axis=0
    )


def scaled(penalty, own_ref, other_refs):
    sums = own_ref[...]
    for ref in other_refs:
        sums = sums + ref[...]
    sums = jnp.sum(sums, axis=1, keepdims=True)
    return penalty * jnp.sqrt(sums[0:1] / (sums[1:2] + EPSILON))


def nodes_kernel(
    S, J, HB, devices, got_ref, id_ref, mu_ref, h_ref, ml_ref, table_ref, an_out, ml_out, ent_ref, sums_ref, old_sc
):
    Q, E = J * S, 2 * J
    names = got_ref[pl.ds(E * HB * devices, devices, stride=NOTES), :]
    names = jnp.maximum(names, 0.0).astype(jnp.int32)
    shared, means, entry_means, weight, gap, drift = read_nodes(
        J, HB, got_ref, id_ref[...], devices
    )
    for h in range(HB):
        at = pl.ds(h * Q, Q)
        ent_ref[h] = entry_means[h]
        anchor = jnp.where(shared, means[h], mu_ref[at, :])
        an_out[at, :] = anchor
        ml_out[at, :] = ml_ref[at, :] + RHO_START * (h_ref[at, :] - anchor)
    for e in range(E):
        for d in range(devices):
            old_sc[pl.ds(e * devices + d, 1), :] = table_ref[pl.ds(names[d, e], 1), :]
    before = [old_sc[:, h * BLK : (h + 1) * BLK] for h in range(HB)]
    put_sums(gap, drift + moved(weight, entry_means, before), sums_ref)


def second_kernel(
    S, J, R, NZ, HB, pp_ref, pc_ref, hp_ref, hc_ref, cb_ref, ml_ref, an_ref, id_ref, wb_ref, same_ref, sums_ref, sums2_ref, pieces_ref, *rest
):
    other_refs = rest[: R - 1]
    p_out, h_out, mu_out, send_ref, step_ref, pen_ref, all_sc = rest[R - 1 :]
    Q = J * S
    own = lax.axis_index("rows")
    slot = lambda ref, k: ref[k * Q : (k + 1) * Q, :]
    penalty = scaled(RHO_START, sums_ref, [sums2_ref])
    pen_ref[...] = jnp.broadcast_to(penalty, pen_ref.shape)
    anchors = [slot(an_ref, h) for h in range(HB)]
    hedge = [slot(ml_ref, h) + penalty * (slot(hp_ref, h) - anchors[h]) for h in range(HB)]
    placed, hedged = primal_step(
        S, J, R, NZ, HB, own, pieces_ref, other_refs, pp_ref, pc_ref, hp_ref, hc_ref, cb_ref, hedge, all_sc
    )
    finish_step(
        S, J, R, NZ, HB, own, pp_ref, placed, hedged, anchors, id_ref[...], wb_ref[...], same_ref[...], p_out, h_out, mu_out, send_ref, step_ref
    )


def last_kernel(
    S, J, HB, devices, got_ref, id_ref, ent_ref, mu_ref, h_ref, ml_ref, pen_ref, ml_out, sums_ref
):
    Q = J * S
    shared, means, entry_means, weight, gap, drift = read_nodes(
        J, HB, got_ref, id_ref[...], devices
    )
    drift = drift + moved(weight, entry_means, [ent_ref[h] for h in range(HB)])
    put_sums(gap, drift, sums_ref)
    penalty = pen_ref[0:1, 0:1]
    for h in range(HB):
        at = pl.ds(h * Q, Q)
        anchor = jnp.where(shared, means[h], mu_ref[at, :])
        ml_out[at, :] = ml_ref[at, :] + penalty * (h_ref[at, :] - anchor)


def finish_kernel(
    S, J, HB, ml_ref, dual_ref, rhs_ref, image_ref, image2_ref, ml_out, dual_out
):
    for h in range(HB):
        for j in range(J):
            src = pl.ds(h * J * S + j * S, S)
            ml_out[pl.ds(h * J + j, S, stride=HB * J), :] = ml_ref[src, :]
    image = image_ref[...] + image2_ref[...]
    dual_out[...] = jnp.maximum(dual_ref[...] + SIGMA_STEP * (image - rhs_ref[...]), 0.0)


def penalty_kernel(pen_ref, sums_ref, sums2_ref, out_ref):
    out_ref[...] = scaled(pen_ref[0:1, 0:1], sums_ref, [sums2_ref])


def bulk_kernel(S, primal_ref, cost_ref, out_ref):
    for s in range(S):
        move = TAU_STEP * cost_ref[s].astype(F32)
        x = primal_ref[s].astype(F32)
        for _ in range(SWEEPS):
            x = jnp.maximum(x - move, 0.0)
        out_ref[s] = x


def place_kernel(S, J, R, NZ, HB, first, count, parts, cols_ref, bulk_ref, p_ref, h_ref, *rest):
    near_ref, out_hbm, sems = rest[-3:]
    K, Q = R * NZ, J * S
    step = count // parts
    copies = []
    for i in range(count):
        s = first + i
        for j in range(J):
            for k in range(K):
                c = cols_ref[k // NZ, j, k % NZ, s]
                near_ref[s, pl.ds(c * J + j, 1), :] = p_ref[pl.ds(k * Q + j * S + s, 1), :]
            for h in range(HB):
                near_ref[s, pl.ds(h * J + j, 1), :] = h_ref[pl.ds(h * Q + j * S + s, 1), :]
        if (i + 1) % step == 0:
            at = pl.ds(s + 1 - step, step)
            copies.append(
                pltpu.make_async_copy(near_ref.at[at], out_hbm.at[at], sems.at[i // step])
            )
            copies[-1].start()
    for copy in copies:
        copy.wait()


def merge_kernel(apart, count, sums, x_ref, y_ref, *rest):
    out_ref = rest[-1]
    rows = count * sums
    high = lax.rem(lax.axis_index("scen") // apart, 2)
    for place, ref in ((high, x_ref), (1 - high, y_ref)):
        out_ref[pl.ds(pl.multiple_of(place * rows, 8), rows), :] = ref[:rows, :]
        for i in range(NOTES * count):
            at = 2 * rows + place * (NOTES * count) + i
            out_ref[pl.ds(at, 1), :] = ref[rows + i : rows + i + 1, :]
    used = 2 * rows + 2 * NOTES * count
    if out_ref.shape[0] > used:
        out_ref[used:, :] = jnp.zeros((out_ref.shape[0] - used, BLK), F32)


def local(
    sizes,
    lp_blocks,
    block_columns,
    scenario_nodes,
    scenario_weights,
    cost,
    bounds_rhs,
    primal_start,
    dual_start,
    multiplier_start,
    consensus_start,
):
    scens, R, sections = sizes
    S, J, columns = cost.shape
    NZ = lp_blocks.shape[3]
    hedged = multiplier_start.shape[2]
    HB, C = hedged // BLK, columns // BLK
    K, Q = R * NZ, J * S
    devices = scens
    message = -(-(2 * J * HB + NOTES) // 8) * 8
    static = (S, J, R, NZ, HB)

    def interleave(x):
        return x.reshape(S, J, -1, BLK).transpose(0, 2, 1, 3).reshape(S, -1, BLK)

    def uninterleave(x):
        return x.reshape(S, -1, J, BLK).transpose(0, 2, 1, 3).reshape(S, J, -1)

    columns_of = block_columns.transpose(1, 2, 3, 0)
    lp = in_hbm(lp_blocks.reshape(S, J * NZ, BLK, BLK))
    primal, price = in_hbm(interleave(primal_start)), in_vmem(interleave(cost))
    mult = interleave(multiplier_start).reshape(S * HB * J, BLK)

    def from_rows(x):
        return [
            lax.ppermute(x, "rows", [((i + q) % R, i) for i in range(R)]) for q in range(1, R)
        ]

    def from_section(x):
        return lax.ppermute(x, "section", [(i, (i + 1) % sections) for i in range(sections)])

    def partner(x, apart):
        return lax.ppermute(x, "scen", [(i, i ^ apart) for i in range(scens)])

    def merge(x, y, apart, count, least, *after):
        rows = max(least, 2 * count * (2 * J * HB) + -(-2 * NOTES * count // 8) * 8)
        return pl.pallas_call(
            functools.partial(merge_kernel, apart, count, 2 * J * HB),
            out_shape=near(rows, BLK),
            in_specs=[VMEM] * 2 + [HBM if far else VMEM for far, _ in after],
            out_specs=VMEM,
            compiler_params=params(4),
            name="merge",
        )(x, y, *[in_hbm(z) if far else z for far, z in after])

    def exchange(x, least, *work):
        assert scens & (scens - 1) == 0
        apart, turn = scens // 2, 0
        while apart:
            y = partner(x, apart)
            x = merge(x, y, apart, 1 << turn, least if apart == 2 else 0, *(work[turn]() if turn < len(work) else ()))
            apart, turn = apart // 2, turn + 1
        return x

    def near_like(x):
        return pltpu.VMEM(x.shape, x.dtype)

    parts = max(p for p in (4, 3, 2, 1) if S % p == 0)
    pieces, lp, primal = pl.pallas_call(
        functools.partial(pieces_kernel, S, J, NZ),
        out_shape=[near(NZ * Q, BLK), near_like(lp), near_like(primal)],
        in_specs=[HBM] * 3,
        out_specs=[VMEM] * 3,
        scratch_shapes=[
            pltpu.SemaphoreType.DMA((parts,)),
            pltpu.VMEM(dual_start.shape, F32),
            pltpu.SemaphoreType.DMA,
            pltpu.SemaphoreType.DMA,
        ],
        compiler_params=params(16),
        name="pieces",
    )(lp, in_hbm(dual_start), primal)
    others = from_rows(pieces)

    pp, pc, hp, hc, cb, ml, an, ids, wb, same, table = pl.pallas_call(
        functools.partial(setup_kernel, *static),
        out_shape=[near(K * Q, BLK)] * 2
        + [near(HB * Q, BLK)] * 2
        + [near(K * Q, BLK)]
        + [near(HB * Q, BLK)] * 2
        + [near(Q, BLK)] * 3
        + [near_like(consensus_start)],
        in_specs=[VMEM] * 6 + [HBM],
        out_specs=[VMEM] * 11,
        scratch_shapes=[pltpu.VMEM((S * K * J, BLK), F32)] * 3
        + [pltpu.VMEM((S * HB * J, BLK), F32)] * 2
        + [pltpu.SemaphoreType.DMA],
        compiler_params=params(16),
        name="setup",
    )(
        scenario_nodes,
        scenario_weights.reshape(1, S),
        columns_of.reshape(K * J, S),
        in_vmem(primal),
        price,
        mult,
        in_hbm(consensus_start),
    )
    primal = in_vmem(primal)

    def step_out(rows):
        return [
            near(K * Q, BLK),
            near(HB * Q, BLK),
            near(HB * Q, BLK),
            near(rows, BLK),
            near(NZ * Q, BLK),
        ]

    def image_of(step):
        return pl.pallas_call(
            functools.partial(image_kernel, S, J, NZ),
            out_shape=near(S, BLK),
            in_specs=[VMEM] * 2,
            out_specs=VMEM,
            compiler_params=params(8),
            name="image",
        )(lp, step)

    scratch = [pltpu.VMEM((K * Q, BLK), F32)]
    p1, h1, mu1, send1, step1 = pl.pallas_call(
        functools.partial(first_kernel, *static),
        out_shape=step_out(message),
        in_specs=[VMEM] * (11 + R - 1),
        out_specs=[VMEM] * 5,
        scratch_shapes=scratch,
        compiler_params=params(8),
        name="first",
    )(pp, pc, hp, hc, cb, ml, an, ids, wb, same, pieces, *others)
    made = {}

    def image_work():
        made["image"] = image_of(step1)
        return ((False, made["image"]),)

    def dual_work():
        made["bulk"] = pl.pallas_call(
            functools.partial(bulk_kernel, S),
            out_shape=near(S, C * J, BLK),
            in_specs=[VMEM] * 2,
            out_specs=VMEM,
            compiler_params=params(8),
            name="bulk",
        )(primal, price)
        made["dual"], made["pieces"] = pl.pallas_call(
            functools.partial(dual_kernel, S, J, NZ),
            out_shape=[near(S, BLK), near(NZ * Q, BLK)],
            in_specs=[VMEM] * 5,
            out_specs=[VMEM] * 2,
            compiler_params=params(8),
            name="dual",
        )(lp, dual_start, bounds_rhs, made["image"], from_section(made["image"]))
        return ((False, made["pieces"]), (False, made["bulk"]))

    got1 = exchange(send1, NZ * Q, image_work, dual_work)
    dual1, pieces2 = made["dual"], made["pieces"]
    others2 = from_rows(pieces2)

    an1, ml1, ent1, sums1 = pl.pallas_call(
        functools.partial(nodes_kernel, S, J, HB, devices),
        out_shape=[near(HB * Q, BLK)] * 2 + [near(HB, 2 * J * devices, BLK), near(8, BLK)],
        in_specs=[VMEM] * 6,
        out_specs=[VMEM] * 4,
        scratch_shapes=[
            pltpu.VMEM((2 * J * devices, hedged), F32),
        ],
        compiler_params=params(8),
        name="nodes",
    )(got1, ids, mu1, h1, ml, table)
    sums1b = from_section(sums1)

    p2, h2, mu2, send2, step2, pen1 = pl.pallas_call(
        functools.partial(second_kernel, *static),
        out_shape=step_out(message) + [near(8, BLK)],
        in_specs=[VMEM] * (13 + R - 1),
        out_specs=[VMEM] * 6,
        scratch_shapes=scratch,
        compiler_params=params(8),
        name="second",
    )(p1, pc, h1, hc, cb, ml1, an1, ids, wb, same, sums1, sums1b, pieces2, *others2)
    half = S // 2

    def place(first, count, whole, *into):
        cuts = max(p for p in (2, 1) if count % p == 0)
        return pl.pallas_call(
            functools.partial(place_kernel, *static, first, count, cuts),
            out_shape=[near(S, C * J, BLK), shape(S, C * J, BLK)],
            in_specs=[SMEM] + [VMEM] * 3 + [HBM] * len(into),
            out_specs=[VMEM, HBM],
            scratch_shapes=[pltpu.SemaphoreType.DMA((cuts,))],
            input_output_aliases={1: 0, 4: 1} if into else {1: 0},
            compiler_params=params(4),
            name="place",
        )(columns_of, whole, p2, h2, *into)

    def last_image_work():
        made["image"] = image_of(step2)
        return ((False, made["image"]),)

    def place_work():
        made["bulk"], made["out"] = place(0, half, made["bulk"])
        return ((True, made["out"]),)

    def rest_work():
        made["bulk"], made["out"] = place(half, S - half, made["bulk"], made["out"])
        return ((True, made["out"]),)

    got2 = exchange(send2, 0, last_image_work, place_work, rest_work)
    out, image2 = made["out"], made["image"]
    ml2, sums2 = pl.pallas_call(
        functools.partial(last_kernel, S, J, HB, devices),
        out_shape=[near(HB * Q, BLK), near(8, BLK)],
        in_specs=[VMEM] * 7,
        out_specs=[VMEM] * 2,
        compiler_params=params(8),
        name="last",
    )(got2, ids, ent1, mu2, h2, ml1, pen1)
    ml2, dual2 = pl.pallas_call(
        functools.partial(finish_kernel, S, J, HB),
        out_shape=[shape(S * HB * J, BLK), shape(S, BLK)],
        in_specs=[VMEM] * 5,
        out_specs=[VMEM] * 2,
        compiler_params=params(4),
        name="finish",
    )(ml2, dual1, bounds_rhs, image2, from_section(image2))
    pen2 = pl.pallas_call(
        penalty_kernel,
        out_shape=shape(1, 1),
        in_specs=[VMEM] * 3,
        out_specs=VMEM,
        compiler_params=params(4),
        name="penalty",
    )(pen1, sums2, from_section(sums2))

    return (
        uninterleave(out),
        dual2,
        uninterleave(ml2.reshape(S, HB * J, BLK)),
        pen2.reshape(()),
    )


def solution(mesh):
    sizes = tuple(mesh.shape[a] for a in ("scen", "rows", "section"))
    in_specs = (
        P("scen", "rows", "section", None, None, None),
        P("scen", None, "section", None),
        P(None, "scen"),
        P("scen"),
        P("scen", "section", None),
        P("scen", "rows"),
        P("scen", "section", None),
        P("scen", "rows"),
        P("scen", "section", None),
        P(),
    )
    out_specs = (P("scen", "section", None), P("scen", "rows"), P("scen", "section", None), P())
    return jax.shard_map(
        functools.partial(local, sizes),
        mesh=mesh,
        in_specs=in_specs,
        out_specs=out_specs,
        check_vma=False,
    )
```

```python
import functools

import jax
import jax.numpy as jnp
from jax import lax
from jax.experimental import pallas as pl
from jax.experimental.pallas import tpu as pltpu
from jax.sharding import PartitionSpec as P

BLK = 128
N1 = 8
N2 = 64
SWEEPS = 2
TAU_STEP = 0.4
SIGMA_STEP = 0.4
RHO_START = 1.0
EPSILON = 1e-06
F32 = jnp.float32
BF16 = jnp.bfloat16
NOTES = 3

VMEM = pl.BlockSpec(memory_space=pltpu.VMEM)
SMEM = pl.BlockSpec(memory_space=pltpu.SMEM)
HBM = pl.BlockSpec(memory_space=pltpu.HBM)


def params(mib=16):
    return pltpu.CompilerParams(vmem_limit_bytes=mib << 20)


def in_vmem(x):
    return pltpu.with_memory_space_constraint(x, pltpu.VMEM)


def in_hbm(x):
    return pltpu.with_memory_space_constraint(x, pltpu.HBM)


def shape(*dims):
    return jax.ShapeDtypeStruct(dims, F32)


def near(*dims):
    return pltpu.VMEM(dims, F32)


def cut(src_ref, dst_ref, sems, parts):
    step = src_ref.shape[0] // parts
    at = [pl.ds(i * step, step) for i in range(parts)]
    return [
        pltpu.make_async_copy(src_ref.at[a], dst_ref.at[a], sems.at[i]) for i, a in enumerate(at)
    ]


def write_pieces(lp_ref, dual, out_ref, S, J, NZ, before=lambda s: None):
    for s in range(S):
        before(s)
        row = dual[s : s + 1, :].astype(BF16)
        for j in range(J):
            for n in range(NZ):
                y = jnp.dot(row, lp_ref[s, j * NZ + n], preferred_element_type=F32)
                out_ref[pl.ds((n * J + j) * S + s, 1), :] = y


def image_kernel(S, J, NZ, lp_ref, step_ref, image_ref):
    for s in range(S):
        total = None
        for j in range(J):
            for n in range(NZ):
                x = step_ref[pl.ds((n * J + j) * S + s, 1), :].astype(BF16)
                y = lax.dot_general(
                    x,
                    lp_ref[s, j * NZ + n],
                    (((1,), (1,)), ((), ())),
                    preferred_element_type=F32,
                )
                total = y if total is None else total + y
        image_ref[pl.ds(s, 1), :] = total


def pieces_kernel(
    S, J, NZ, lp_hbm, dual_hbm, primal_hbm, out_ref, lp_ref, primal_ref, sems, dual_ref, sem, primal_sem
):
    parts = sems.shape[0]
    dual_copy = pltpu.make_async_copy(dual_hbm, dual_ref, sem)
    dual_copy.start()
    copies = cut(lp_hbm, lp_ref, sems, parts)
    for copy in copies:
        copy.start()
    primal_copy = pltpu.make_async_copy(primal_hbm, primal_ref, primal_sem)
    primal_copy.start()
    dual_copy.wait()

    def before(s):
        if s % (S // parts) == 0:
            copies[s // (S // parts)].wait()

    write_pieces(lp_ref, dual_ref[...], out_ref, S, J, NZ, before)
    primal_copy.wait()


def dual_kernel(S, J, NZ, lp_ref, dual_ref, rhs_ref, image_ref, image2_ref, next_ref, out_ref):
    image = image_ref[...] + image2_ref[...]
    dual = jnp.maximum(dual_ref[...] + SIGMA_STEP * (image - rhs_ref[...]), 0.0)
    next_ref[...] = dual
    write_pieces(lp_ref, dual, out_ref, S, J, NZ)


def down(row, count):
    return jnp.transpose(jnp.broadcast_to(row, (BLK, row.shape[1])))[:count]


def setup_kernel(
    S,
    J,
    R,
    NZ,
    HB,
    nodes_ref,
    weights_ref,
    cols_ref,
    primal_ref,
    cost_ref,
    mult_ref,
    table_hbm,
    pp_ref,
    pc_ref,
    hp_ref,
    hc_ref,
    cb_ref,
    ml_ref,
    an_ref,
    id_ref,
    wb_ref,
    same_ref,
    table_ref,
    idx_sc,
    pp_sc,
    pc_sc,
    hp_sc,
    hc_sc,
    table_sem,
):
    K, Q = R * NZ, J * S
    table_copy = pltpu.make_async_copy(table_hbm, table_ref, table_sem)
    table_copy.start()
    section = lax.axis_index("section")
    rows = primal_ref.shape[1]

    cols = cols_ref[...]
    section_of = lax.rem(lax.broadcasted_iota(jnp.int32, (K * J, BLK), 0) // NZ, J)
    tiles = -(-rows // BLK)
    lane = lax.broadcasted_iota(jnp.int32, (K * J, BLK), 1)
    picks = []
    for s in range(S):
        want = jnp.broadcast_to(cols[:, s : s + 1], (K * J, BLK))
        idx_sc[pl.ds(s * K * J, K * J), :] = want.astype(F32)
        want = want * J + section_of
        picks.append(
            jnp.concatenate(
                [(want == lane + t * BLK).astype(F32).astype(BF16) for t in range(tiles)], axis=1
            )[:, :rows]
        )

    def gather(source_ref, placed_ref, hedged_ref):
        for s in range(S):
            placed_ref[pl.ds(s * K * J, K * J), :] = jnp.dot(
                picks[s], source_ref[s], preferred_element_type=F32
            )
            hedged_ref[pl.ds(s * HB * J, HB * J), :] = source_ref[s, : HB * J, :].astype(F32)

    def placed_rows(k, j):
        return pl.ds(((k // NZ) * J + j) * NZ + k % NZ, S, stride=K * J), pl.ds(k * Q + j * S, S)

    def hedged_rows(h, j):
        return pl.ds(h * J + j, S, stride=HB * J), pl.ds(h * Q + j * S, S)

    gather(primal_ref, pp_sc, hp_sc)
    gather(cost_ref, pc_sc, hc_sc)
    weights = down(weights_ref[...], S)
    ids, picked = [], []
    for j in range(J):
        g = section * J + j
        own = jnp.zeros((1, nodes_ref.shape[1]), jnp.int32)
        for level, off in enumerate((1, 1 + N1, 1 + N1 + N2)):
            own = jnp.where(g == level + 1, nodes_ref[level : level + 1, :] + off, own)
        ids.append(down(own.astype(F32), S))
        picked.append(own)
        wb_ref[pl.ds(j * S, S), :] = weights
    ids = jnp.concatenate(ids, axis=0)
    id_ref[...] = ids
    across = jnp.transpose(ids)[0:1, :Q]
    same_ref[:, :Q] = (jnp.broadcast_to(ids[:, :1], (Q, Q)) == across).astype(F32)
    for j in range(J):
        for k in range(K):
            src, dst = placed_rows(k, j)
            pp_ref[dst, :] = pp_sc[src, :]
            pc_ref[dst, :] = pc_sc[src, :]
            cb_ref[dst, :] = idx_sc[src, :]
        for h in range(HB):
            src, dst = hedged_rows(h, j)
            hp_ref[dst, :] = hp_sc[src, :]
            hc_ref[dst, :] = hc_sc[src, :]
            ml_ref[dst, :] = mult_ref[src, :]
    table_copy.wait()
    for j in range(J):
        for s in range(S):
            line = table_ref[pl.ds(picked[j][0, s], 1), :]
            for h in range(HB):
                an_ref[pl.ds(h * Q + j * S + s, 1), :] = line[:, h * BLK : (h + 1) * BLK]


def added(x):
    return jnp.sum(x, axis=0, keepdims=True)


def chosen_sums(same, x):
    same, sums = same.astype(BF16), None
    for _ in range(3):
        part = x.astype(BF16)
        y = jnp.dot(same, part, preferred_element_type=F32)
        sums = y if sums is None else sums + y
        x = x - part.astype(F32)
    return sums


def primal_step(
    S, J, R, NZ, HB, own, pieces_ref, other_refs, p_ref, pc_ref, h_ref, hc_ref, cb_ref, hedge, all_sc
):
    K, Q = R * NZ, J * S
    for shift in range(R):
        src = pieces_ref if shift == 0 else other_refs[shift - 1]
        at = lax.rem(own + shift, R) * (NZ * Q)
        all_sc[pl.ds(pl.multiple_of(at, 8), NZ * Q), :] = src[...]
    slot = lambda ref, k: ref[k * Q : (k + 1) * Q, :]
    cols = [slot(cb_ref, k) for k in range(K)]
    parts = [slot(all_sc, k) for k in range(K)]
    placed, hedged = [], []
    for k in range(K):
        add = None
        for m in range(K):
            term = parts[m] if m == k else jnp.where(cols[m] == cols[k], parts[m], 0.0)
            add = term if add is None else add + term
        for h in range(HB):
            add = add + jnp.where(cols[k] == float(h), hedge[h], 0.0)
        placed.append(
            jnp.maximum(slot(p_ref, k) - TAU_STEP * (slot(pc_ref, k) + add), 0.0)
        )
    for h in range(HB):
        add = None
        for m in range(K):
            term = jnp.where(cols[m] == float(h), parts[m], 0.0)
            add = term if add is None else add + term
        add = add + hedge[h]
        hedged.append(jnp.maximum(slot(h_ref, h) - TAU_STEP * (slot(hc_ref, h) + add), 0.0))
    return placed, hedged


def finish_step(
    S, J, R, NZ, HB, own, p_ref, placed, hedged, anchors, ids, wb, same, p_out, h_out, mu_ref, send_ref, step_ref
):
    K, Q = R * NZ, J * S
    for k in range(K):
        p_out[k * Q : (k + 1) * Q, :] = placed[k]
    mine = pl.ds(pl.multiple_of(own * (NZ * Q), 8), NZ * Q)
    step_ref[...] = 2.0 * p_out[mine, :] - p_ref[mine, :]
    for h in range(HB):
        h_out[h * Q : (h + 1) * Q, :] = hedged[h]
    sums = chosen_sums(same[:, :Q], jnp.concatenate([wb * x for x in hedged] + [wb], axis=1))
    mass = sums[:, HB * BLK :]
    inner = []
    for j in range(J):
        mine = ids[j * S : (j + 1) * S]
        inner.append((mine != mine[:1]) & (mine != mine[S - 1 :]))
    inner = jnp.concatenate([x.astype(F32) for x in inner], axis=0)
    gap, drift = jnp.zeros((Q, BLK), F32), jnp.zeros((Q, BLK), F32)
    for h in range(HB):
        mu = sums[:, h * BLK : (h + 1) * BLK] / mass
        mu_ref[h * Q : (h + 1) * Q, :] = mu
        gap = gap + wb * (hedged[h] - mu) ** 2
        drift = drift + (wb * inner) * (mu - anchors[h]) ** 2
    lane = lax.broadcasted_iota(jnp.int32, (1, BLK), 1)
    note = jnp.zeros((1, BLK), F32)
    for j in range(J):
        a, b = j * S, j * S + S - 1
        fresh = ids[b : b + 1] != ids[a : a + 1]
        for f in range(2):
            e = f * J + j
            at = b if f else a
            for h in range(HB):
                line = sums[at : at + 1, h * BLK : (h + 1) * BLK]
                send_ref[pl.ds(e * HB + h, 1), :] = jnp.where(fresh, line, 0.0) if f else line
            name, weight = ids[at : at + 1], mass[at : at + 1]
            if f:
                name, weight = jnp.where(fresh, name, -1.0), jnp.where(fresh, weight, 0.0)
            note = jnp.where(lane == e, name, note)
            note = jnp.where(lane == 2 * J + e, weight, note)
    at = 2 * J * HB
    for i, row in enumerate((note, added(gap), added(drift))):
        send_ref[pl.ds(at + i, 1), :] = row
    rest = send_ref.shape[0] - at - NOTES
    send_ref[pl.ds(at + NOTES, rest), :] = jnp.zeros((rest, BLK), F32)


def first_kernel(
    S, J, R, NZ, HB, pp_ref, pc_ref, hp_ref, hc_ref, cb_ref, ml_ref, an_ref, id_ref, wb_ref, same_ref, pieces_ref, *rest
):
    other_refs = rest[: R - 1]
    p_out, h_out, mu_ref, send_ref, step_ref, all_sc = rest[R - 1 :]
    Q = J * S
    own = lax.axis_index("rows")
    slot = lambda ref, k: ref[k * Q : (k + 1) * Q, :]
    anchors = [slot(an_ref, h) for h in range(HB)]
    hedge = [
        slot(ml_ref, h) + RHO_START * (slot(hp_ref, h) - anchors[h]) for h in range(HB)
    ]
    placed, hedged = primal_step(
        S, J, R, NZ, HB, own, pieces_ref, other_refs, pp_ref, pc_ref, hp_ref, hc_ref, cb_ref, hedge, all_sc
    )
    finish_step(
        S, J, R, NZ, HB, own, pp_ref, placed, hedged, anchors, id_ref[...], wb_ref[...], same_ref[...], p_out, h_out, mu_ref, send_ref, step_ref
    )


def read_nodes(J, HB, got_ref, ids, devices):
    E = 2 * J
    sums = [
        jnp.concatenate(
            [got_ref[pl.ds(e * HB + h, devices, stride=E * HB), :] for e in range(E)], axis=0
        )
        for h in range(HB)
    ]
    notes, gaps, drifts = (
        got_ref[pl.ds(E * HB * devices + i, devices, stride=NOTES), :] for i in range(NOTES)
    )
    wide = lambda at: jnp.broadcast_to(notes[:, at : at + 1], (devices, BLK))
    names = jnp.concatenate([wide(e) for e in range(E)], axis=0)
    weight = jnp.concatenate([wide(E + e) for e in range(E)], axis=0)
    every = jnp.concatenate([ids, names], axis=0)
    across = jnp.transpose(names)[0:1, :]
    count = E * devices
    same = (jnp.broadcast_to(every[:, :1], (every.shape[0], count)) == across).astype(F32)
    totals = chosen_sums(same, jnp.concatenate(sums + [weight], axis=1))
    mass = totals[:, HB * BLK :]
    positive = mass > 0
    safe = jnp.where(positive, mass, 1.0)
    means = [
        jnp.where(positive, totals[:, h * BLK : (h + 1) * BLK] / safe, 0.0) for h in range(HB)
    ]
    own_safe = jnp.where(weight > 0, weight, 1.0)
    rows = ids.shape[0]
    spread = jnp.zeros((count, BLK), F32)
    for h in range(HB):
        spread = spread + weight * (sums[h] / own_safe - means[h][rows:]) ** 2
    gap, drift = added(gaps) + added(spread), added(drifts)
    return positive[:rows], [m[:rows] for m in means], [m[rows:] for m in means], weight, gap, drift


def moved(weight, means, before):
    change = jnp.zeros_like(weight)
    for mean, old in zip(means, before):
        change = change + weight * (mean - old) ** 2
    return added(change)


def put_sums(gap, drift, out_ref):
    out_ref[...] = jnp.concatenate(
        [gap, drift, jnp.zeros((out_ref.shape[0] - 2, BLK), F32)], axis=0
    )


def scaled(penalty, own_ref, other_refs):
    sums = own_ref[...]
    for ref in other_refs:
        sums = sums + ref[...]
    sums = jnp.sum(sums, axis=1, keepdims=True)
    return penalty * jnp.sqrt(sums[0:1] / (sums[1:2] + EPSILON))


def nodes_kernel(
    S, J, HB, devices, got_ref, id_ref, mu_ref, h_ref, ml_ref, table_ref, an_out, ml_out, ent_ref, sums_ref, old_sc
):
    Q, E = J * S, 2 * J
    names = got_ref[pl.ds(E * HB * devices, devices, stride=NOTES), :]
    names = jnp.maximum(names, 0.0).astype(jnp.int32)
    shared, means, entry_means, weight, gap, drift = read_nodes(
        J, HB, got_ref, id_ref[...], devices
    )
    for h in range(HB):
        at = pl.ds(h * Q, Q)
        ent_ref[h] = entry_means[h]
        anchor = jnp.where(shared, means[h], mu_ref[at, :])
        an_out[at, :] = anchor
        ml_out[at, :] = ml_ref[at, :] + RHO_START * (h_ref[at, :] - anchor)
    for e in range(E):
        for d in range(devices):
            old_sc[pl.ds(e * devices + d, 1), :] = table_ref[pl.ds(names[d, e], 1), :]
    before = [old_sc[:, h * BLK : (h + 1) * BLK] for h in range(HB)]
    put_sums(gap, drift + moved(weight, entry_means, before), sums_ref)


def second_kernel(
    S, J, R, NZ, HB, pp_ref, pc_ref, hp_ref, hc_ref, cb_ref, ml_ref, an_ref, id_ref, wb_ref, same_ref, sums_ref, sums2_ref, pieces_ref, *rest
):
    other_refs = rest[: R - 1]
    p_out, h_out, mu_out, send_ref, step_ref, pen_ref, all_sc = rest[R - 1 :]
    Q = J * S
    own = lax.axis_index("rows")
    slot = lambda ref, k: ref[k * Q : (k + 1) * Q, :]
    penalty = scaled(RHO_START, sums_ref, [sums2_ref])
    pen_ref[...] = jnp.broadcast_to(penalty, pen_ref.shape)
    anchors = [slot(an_ref, h) for h in range(HB)]
    hedge = [slot(ml_ref, h) + penalty * (slot(hp_ref, h) - anchors[h]) for h in range(HB)]
    placed, hedged = primal_step(
        S, J, R, NZ, HB, own, pieces_ref, other_refs, pp_ref, pc_ref, hp_ref, hc_ref, cb_ref, hedge, all_sc
    )
    finish_step(
        S, J, R, NZ, HB, own, pp_ref, placed, hedged, anchors, id_ref[...], wb_ref[...], same_ref[...], p_out, h_out, mu_out, send_ref, step_ref
    )


def last_kernel(
    S, J, HB, devices, got_ref, id_ref, ent_ref, mu_ref, h_ref, ml_ref, pen_ref, ml_out, sums_ref
):
    Q = J * S
    shared, means, entry_means, weight, gap, drift = read_nodes(
        J, HB, got_ref, id_ref[...], devices
    )
    drift = drift + moved(weight, entry_means, [ent_ref[h] for h in range(HB)])
    put_sums(gap, drift, sums_ref)
    penalty = pen_ref[0:1, 0:1]
    for h in range(HB):
        at = pl.ds(h * Q, Q)
        anchor = jnp.where(shared, means[h], mu_ref[at, :])
        ml_out[at, :] = ml_ref[at, :] + penalty * (h_ref[at, :] - anchor)


def finish_kernel(
    S, J, HB, ml_ref, dual_ref, rhs_ref, image_ref, image2_ref, ml_out, dual_out
):
    for h in range(HB):
        for j in range(J):
            src = pl.ds(h * J * S + j * S, S)
            ml_out[pl.ds(h * J + j, S, stride=HB * J), :] = ml_ref[src, :]
    image = image_ref[...] + image2_ref[...]
    dual_out[...] = jnp.maximum(dual_ref[...] + SIGMA_STEP * (image - rhs_ref[...]), 0.0)


def penalty_kernel(pen_ref, sums_ref, sums2_ref, out_ref):
    out_ref[...] = scaled(pen_ref[0:1, 0:1], sums_ref, [sums2_ref])


def bulk_kernel(S, primal_ref, cost_ref, out_ref):
    for s in range(S):
        move = TAU_STEP * cost_ref[s].astype(F32)
        x = primal_ref[s].astype(F32)
        for _ in range(SWEEPS):
            x = jnp.maximum(x - move, 0.0)
        out_ref[s] = x


def place_kernel(S, J, R, NZ, HB, first, count, parts, cols_ref, bulk_ref, p_ref, h_ref, *rest):
    near_ref, out_hbm, sems = rest[-3:]
    K, Q = R * NZ, J * S
    step = count // parts
    copies = []
    for i in range(count):
        s = first + i
        for j in range(J):
            for k in range(K):
                c = cols_ref[k // NZ, j, k % NZ, s]
                near_ref[s, pl.ds(c * J + j, 1), :] = p_ref[pl.ds(k * Q + j * S + s, 1), :]
            for h in range(HB):
                near_ref[s, pl.ds(h * J + j, 1), :] = h_ref[pl.ds(h * Q + j * S + s, 1), :]
        if (i + 1) % step == 0:
            at = pl.ds(s + 1 - step, step)
            copies.append(
                pltpu.make_async_copy(near_ref.at[at], out_hbm.at[at], sems.at[i // step])
            )
            copies[-1].start()
    for copy in copies:
        copy.wait()


def merge_kernel(apart, count, sums, x_ref, y_ref, *rest):
    out_ref = rest[-1]
    rows = count * sums
    high = lax.rem(lax.axis_index("scen") // apart, 2)
    for place, ref in ((high, x_ref), (1 - high, y_ref)):
        out_ref[pl.ds(pl.multiple_of(place * rows, 8), rows), :] = ref[:rows, :]
        for i in range(NOTES * count):
            at = 2 * rows + place * (NOTES * count) + i
            out_ref[pl.ds(at, 1), :] = ref[rows + i : rows + i + 1, :]
    used = 2 * rows + 2 * NOTES * count
    if out_ref.shape[0] > used:
        out_ref[used:, :] = jnp.zeros((out_ref.shape[0] - used, BLK), F32)


def local(
    sizes,
    lp_blocks,
    block_columns,
    scenario_nodes,
    scenario_weights,
    cost,
    bounds_rhs,
    primal_start,
    dual_start,
    multiplier_start,
    consensus_start,
):
    scens, R, sections = sizes
    S, J, columns = cost.shape
    NZ = lp_blocks.shape[3]
    hedged = multiplier_start.shape[2]
    HB, C = hedged // BLK, columns // BLK
    K, Q = R * NZ, J * S
    devices = scens
    message = -(-(2 * J * HB + NOTES) // 8) * 8
    static = (S, J, R, NZ, HB)

    def interleave(x):
        return x.reshape(S, J, -1, BLK).transpose(0, 2, 1, 3).reshape(S, -1, BLK)

    def uninterleave(x):
        return x.reshape(S, -1, J, BLK).transpose(0, 2, 1, 3).reshape(S, J, -1)

    columns_of = block_columns.transpose(1, 2, 3, 0)
    lp = in_hbm(lp_blocks.reshape(S, J * NZ, BLK, BLK))
    primal, price = in_hbm(interleave(primal_start)), in_vmem(interleave(cost))
    mult = interleave(multiplier_start).reshape(S * HB * J, BLK)

    def from_rows(x):
        return [
            lax.ppermute(x, "rows", [((i + q) % R, i) for i in range(R)]) for q in range(1, R)
        ]

    def from_section(x):
        return lax.ppermute(x, "section", [(i, (i + 1) % sections) for i in range(sections)])

    def partner(x, apart):
        return lax.ppermute(x, "scen", [(i, i ^ apart) for i in range(scens)])

    def merge(x, y, apart, count, least, *after):
        rows = max(least, 2 * count * (2 * J * HB) + -(-2 * NOTES * count // 8) * 8)
        return pl.pallas_call(
            functools.partial(merge_kernel, apart, count, 2 * J * HB),
            out_shape=near(rows, BLK),
            in_specs=[VMEM] * 2 + [HBM if far else VMEM for far, _ in after],
            out_specs=VMEM,
            compiler_params=params(4),
            name="merge",
        )(x, y, *[in_hbm(z) if far else z for far, z in after])

    def exchange(x, least, *work):
        assert scens & (scens - 1) == 0
        apart, turn = scens // 2, 0
        while apart:
            y = partner(x, apart)
            x = merge(x, y, apart, 1 << turn, least if apart == 2 else 0, *(work[turn]() if turn < len(work) else ()))
            apart, turn = apart // 2, turn + 1
        return x

    def near_like(x):
        return pltpu.VMEM(x.shape, x.dtype)

    parts = max(p for p in (3, 2, 1) if S % p == 0)
    pieces, lp, primal = pl.pallas_call(
        functools.partial(pieces_kernel, S, J, NZ),
        out_shape=[near(NZ * Q, BLK), near_like(lp), near_like(primal)],
        in_specs=[HBM] * 3,
        out_specs=[VMEM] * 3,
        scratch_shapes=[
            pltpu.SemaphoreType.DMA((parts,)),
            pltpu.VMEM(dual_start.shape, F32),
            pltpu.SemaphoreType.DMA,
            pltpu.SemaphoreType.DMA,
        ],
        compiler_params=params(16),
        name="pieces",
    )(lp, in_hbm(dual_start), primal)
    others = from_rows(pieces)

    pp, pc, hp, hc, cb, ml, an, ids, wb, same, table = pl.pallas_call(
        functools.partial(setup_kernel, *static),
        out_shape=[near(K * Q, BLK)] * 2
        + [near(HB * Q, BLK)] * 2
        + [near(K * Q, BLK)]
        + [near(HB * Q, BLK)] * 2
        + [near(Q, BLK)] * 3
        + [near_like(consensus_start)],
        in_specs=[VMEM] * 6 + [HBM],
        out_specs=[VMEM] * 11,
        scratch_shapes=[pltpu.VMEM((S * K * J, BLK), F32)] * 3
        + [pltpu.VMEM((S * HB * J, BLK), F32)] * 2
        + [pltpu.SemaphoreType.DMA],
        compiler_params=params(16),
        name="setup",
    )(
        scenario_nodes,
        scenario_weights.reshape(1, S),
        columns_of.reshape(K * J, S),
        in_vmem(primal),
        price,
        mult,
        in_hbm(consensus_start),
    )
    primal = in_vmem(primal)

    def step_out(rows):
        return [
            near(K * Q, BLK),
            near(HB * Q, BLK),
            near(HB * Q, BLK),
            near(rows, BLK),
            near(NZ * Q, BLK),
        ]

    def image_of(step):
        return pl.pallas_call(
            functools.partial(image_kernel, S, J, NZ),
            out_shape=near(S, BLK),
            in_specs=[VMEM] * 2,
            out_specs=VMEM,
            compiler_params=params(8),
            name="image",
        )(lp, step)

    scratch = [pltpu.VMEM((K * Q, BLK), F32)]
    p1, h1, mu1, send1, step1 = pl.pallas_call(
        functools.partial(first_kernel, *static),
        out_shape=step_out(message),
        in_specs=[VMEM] * (11 + R - 1),
        out_specs=[VMEM] * 5,
        scratch_shapes=scratch,
        compiler_params=params(8),
        name="first",
    )(pp, pc, hp, hc, cb, ml, an, ids, wb, same, pieces, *others)
    made = {}

    def image_work():
        made["image"] = image_of(step1)
        return ((False, made["image"]),)

    def dual_work():
        made["bulk"] = pl.pallas_call(
            functools.partial(bulk_kernel, S),
            out_shape=near(S, C * J, BLK),
            in_specs=[VMEM] * 2,
            out_specs=VMEM,
            compiler_params=params(8),
            name="bulk",
        )(primal, price)
        made["dual"], made["pieces"] = pl.pallas_call(
            functools.partial(dual_kernel, S, J, NZ),
            out_shape=[near(S, BLK), near(NZ * Q, BLK)],
            in_specs=[VMEM] * 5,
            out_specs=[VMEM] * 2,
            compiler_params=params(8),
            name="dual",
        )(lp, dual_start, bounds_rhs, made["image"], from_section(made["image"]))
        return ((False, made["pieces"]), (False, made["bulk"]))

    got1 = exchange(send1, 88, image_work, dual_work)
    dual1, pieces2 = made["dual"], made["pieces"]
    others2 = from_rows(pieces2)

    an1, ml1, ent1, sums1 = pl.pallas_call(
        functools.partial(nodes_kernel, S, J, HB, devices),
        out_shape=[near(HB * Q, BLK)] * 2 + [near(HB, 2 * J * devices, BLK), near(8, BLK)],
        in_specs=[VMEM] * 6,
        out_specs=[VMEM] * 4,
        scratch_shapes=[
            pltpu.VMEM((2 * J * devices, hedged), F32),
        ],
        compiler_params=params(8),
        name="nodes",
    )(got1, ids, mu1, h1, ml, table)
    sums1b = from_section(sums1)

    p2, h2, mu2, send2, step2, pen1 = pl.pallas_call(
        functools.partial(second_kernel, *static),
        out_shape=step_out(message) + [near(8, BLK)],
        in_specs=[VMEM] * (13 + R - 1),
        out_specs=[VMEM] * 6,
        scratch_shapes=scratch,
        compiler_params=params(8),
        name="second",
    )(p1, pc, h1, hc, cb, ml1, an1, ids, wb, same, sums1, sums1b, pieces2, *others2)
    half = S // 2

    def place(first, count, whole, *into):
        cuts = max(p for p in (2, 1) if count % p == 0)
        return pl.pallas_call(
            functools.partial(place_kernel, *static, first, count, cuts),
            out_shape=[near(S, C * J, BLK), shape(S, C * J, BLK)],
            in_specs=[SMEM] + [VMEM] * 3 + [HBM] * len(into),
            out_specs=[VMEM, HBM],
            scratch_shapes=[pltpu.SemaphoreType.DMA((cuts,))],
            input_output_aliases={1: 0, 4: 1} if into else {1: 0},
            compiler_params=params(4),
            name="place",
        )(columns_of, whole, p2, h2, *into)

    def last_image_work():
        made["image"] = image_of(step2)
        return ((False, made["image"]),)

    def place_work():
        made["bulk"], made["out"] = place(0, half, made["bulk"])
        return ((True, made["out"]),)

    def rest_work():
        made["bulk"], made["out"] = place(half, S - half, made["bulk"], made["out"])
        return ((True, made["out"]),)

    got2 = exchange(send2, 0, last_image_work, place_work, rest_work)
    out, image2 = made["out"], made["image"]
    ml2, sums2 = pl.pallas_call(
        functools.partial(last_kernel, S, J, HB, devices),
        out_shape=[near(HB * Q, BLK), near(8, BLK)],
        in_specs=[VMEM] * 7,
        out_specs=[VMEM] * 2,
        compiler_params=params(8),
        name="last",
    )(got2, ids, ent1, mu2, h2, ml1, pen1)
    ml2, dual2 = pl.pallas_call(
        functools.partial(finish_kernel, S, J, HB),
        out_shape=[shape(S * HB * J, BLK), shape(S, BLK)],
        in_specs=[VMEM] * 5,
        out_specs=[VMEM] * 2,
        compiler_params=params(4),
        name="finish",
    )(ml2, dual1, bounds_rhs, image2, from_section(image2))
    pen2 = pl.pallas_call(
        penalty_kernel,
        out_shape=shape(1, 1),
        in_specs=[VMEM] * 3,
        out_specs=VMEM,
        compiler_params=params(4),
        name="penalty",
    )(pen1, sums2, from_section(sums2))

    return (
        uninterleave(out),
        dual2,
        uninterleave(ml2.reshape(S, HB * J, BLK)),
        pen2.reshape(()),
    )


def solution(mesh):
    sizes = tuple(mesh.shape[a] for a in ("scen", "rows", "section"))
    in_specs = (
        P("scen", "rows", "section", None, None, None),
        P("scen", None, "section", None),
        P(None, "scen"),
        P("scen"),
        P("scen", "section", None),
        P("scen", "rows"),
        P("scen", "section", None),
        P("scen", "rows"),
        P("scen", "section", None),
        P(),
    )
    out_specs = (P("scen", "section", None), P("scen", "rows"), P("scen", "section", None), P())
    return jax.shard_map(
        functools.partial(local, sizes),
        mesh=mesh,
        in_specs=in_specs,
        out_specs=out_specs,
        check_vma=False,
    )
```

```python
import functools

import jax
import jax.numpy as jnp
from jax import lax
from jax.experimental import pallas as pl
from jax.experimental.pallas import tpu as pltpu
from jax.sharding import PartitionSpec as P

BLK = 128
N1 = 8
N2 = 64
SWEEPS = 2
TAU_STEP = 0.4
SIGMA_STEP = 0.4
RHO_START = 1.0
EPSILON = 1e-06
F32 = jnp.float32
BF16 = jnp.bfloat16
NOTES = 3

VMEM = pl.BlockSpec(memory_space=pltpu.VMEM)
SMEM = pl.BlockSpec(memory_space=pltpu.SMEM)
HBM = pl.BlockSpec(memory_space=pltpu.HBM)


def params(mib=16):
    return pltpu.CompilerParams(vmem_limit_bytes=mib << 20)


def in_vmem(x):
    return pltpu.with_memory_space_constraint(x, pltpu.VMEM)


def in_hbm(x):
    return pltpu.with_memory_space_constraint(x, pltpu.HBM)


def shape(*dims):
    return jax.ShapeDtypeStruct(dims, F32)


def near(*dims):
    return pltpu.VMEM(dims, F32)


def cut(src_ref, dst_ref, sems, parts):
    step = src_ref.shape[0] // parts
    at = [pl.ds(i * step, step) for i in range(parts)]
    return [
        pltpu.make_async_copy(src_ref.at[a], dst_ref.at[a], sems.at[i]) for i, a in enumerate(at)
    ]


def write_pieces(lp_ref, dual, out_ref, S, J, NZ, before=lambda s: None):
    for s in range(S):
        before(s)
        row = dual[s : s + 1, :].astype(BF16)
        for j in range(J):
            for n in range(NZ):
                y = jnp.dot(row, lp_ref[s, j * NZ + n], preferred_element_type=F32)
                out_ref[pl.ds((n * J + j) * S + s, 1), :] = y


def image_kernel(S, J, NZ, lp_ref, step_ref, image_ref):
    for s in range(S):
        total = None
        for j in range(J):
            for n in range(NZ):
                x = step_ref[pl.ds((n * J + j) * S + s, 1), :].astype(BF16)
                y = lax.dot_general(
                    x,
                    lp_ref[s, j * NZ + n],
                    (((1,), (1,)), ((), ())),
                    preferred_element_type=F32,
                )
                total = y if total is None else total + y
        image_ref[pl.ds(s, 1), :] = total


def pieces_kernel(
    S, J, NZ, lp_hbm, dual_hbm, primal_hbm, out_ref, lp_ref, primal_ref, sems, dual_ref, sem, primal_sem
):
    parts = sems.shape[0]
    dual_copy = pltpu.make_async_copy(dual_hbm, dual_ref, sem)
    dual_copy.start()
    copies = cut(lp_hbm, lp_ref, sems, parts)
    for copy in copies:
        copy.start()
    primal_copy = pltpu.make_async_copy(primal_hbm, primal_ref, primal_sem)
    primal_copy.start()
    dual_copy.wait()

    def before(s):
        if s % (S // parts) == 0:
            copies[s // (S // parts)].wait()

    write_pieces(lp_ref, dual_ref[...], out_ref, S, J, NZ, before)
    primal_copy.wait()


def dual_kernel(S, J, NZ, lp_ref, dual_ref, rhs_ref, image_ref, image2_ref, next_ref, out_ref):
    image = image_ref[...] + image2_ref[...]
    dual = jnp.maximum(dual_ref[...] + SIGMA_STEP * (image - rhs_ref[...]), 0.0)
    next_ref[...] = dual
    write_pieces(lp_ref, dual, out_ref, S, J, NZ)


def down(row, count):
    return jnp.transpose(jnp.broadcast_to(row, (BLK, row.shape[1])))[:count]


def setup_kernel(
    S,
    J,
    R,
    NZ,
    HB,
    nodes_ref,
    weights_ref,
    cols_ref,
    primal_ref,
    cost_ref,
    mult_ref,
    table_hbm,
    pp_ref,
    pc_ref,
    hp_ref,
    hc_ref,
    cb_ref,
    ml_ref,
    an_ref,
    id_ref,
    wb_ref,
    same_ref,
    table_ref,
    idx_sc,
    pp_sc,
    pc_sc,
    hp_sc,
    hc_sc,
    table_sem,
):
    K, Q = R * NZ, J * S
    table_copy = pltpu.make_async_copy(table_hbm, table_ref, table_sem)
    table_copy.start()
    section = lax.axis_index("section")
    rows = primal_ref.shape[1]

    cols = cols_ref[...]
    section_of = lax.rem(lax.broadcasted_iota(jnp.int32, (K * J, BLK), 0) // NZ, J)
    tiles = -(-rows // BLK)
    lane = lax.broadcasted_iota(jnp.int32, (K * J, BLK), 1)
    picks = []
    for s in range(S):
        want = jnp.broadcast_to(cols[:, s : s + 1], (K * J, BLK))
        idx_sc[pl.ds(s * K * J, K * J), :] = want.astype(F32)
        want = want * J + section_of
        picks.append(
            jnp.concatenate(
                [(want == lane + t * BLK).astype(F32).astype(BF16) for t in range(tiles)], axis=1
            )[:, :rows]
        )

    def gather(source_ref, placed_ref, hedged_ref):
        for s in range(S):
            placed_ref[pl.ds(s * K * J, K * J), :] = jnp.dot(
                picks[s], source_ref[s], preferred_element_type=F32
            )
            hedged_ref[pl.ds(s * HB * J, HB * J), :] = source_ref[s, : HB * J, :].astype(F32)

    def placed_rows(k, j):
        return pl.ds(((k // NZ) * J + j) * NZ + k % NZ, S, stride=K * J), pl.ds(k * Q + j * S, S)

    def hedged_rows(h, j):
        return pl.ds(h * J + j, S, stride=HB * J), pl.ds(h * Q + j * S, S)

    gather(primal_ref, pp_sc, hp_sc)
    gather(cost_ref, pc_sc, hc_sc)
    weights = down(weights_ref[...], S)
    ids, picked = [], []
    for j in range(J):
        g = section * J + j
        own = jnp.zeros((1, nodes_ref.shape[1]), jnp.int32)
        for level, off in enumerate((1, 1 + N1, 1 + N1 + N2)):
            own = jnp.where(g == level + 1, nodes_ref[level : level + 1, :] + off, own)
        ids.append(down(own.astype(F32), S))
        picked.append(own)
        wb_ref[pl.ds(j * S, S), :] = weights
    ids = jnp.concatenate(ids, axis=0)
    id_ref[...] = ids
    across = jnp.transpose(ids)[0:1, :Q]
    same_ref[:, :Q] = (jnp.broadcast_to(ids[:, :1], (Q, Q)) == across).astype(F32)
    for j in range(J):
        for k in range(K):
            src, dst = placed_rows(k, j)
            pp_ref[dst, :] = pp_sc[src, :]
            pc_ref[dst, :] = pc_sc[src, :]
            cb_ref[dst, :] = idx_sc[src, :]
        for h in range(HB):
            src, dst = hedged_rows(h, j)
            hp_ref[dst, :] = hp_sc[src, :]
            hc_ref[dst, :] = hc_sc[src, :]
            ml_ref[dst, :] = mult_ref[src, :]
    table_copy.wait()
    for j in range(J):
        for s in range(S):
            line = table_ref[pl.ds(picked[j][0, s], 1), :]
            for h in range(HB):
                an_ref[pl.ds(h * Q + j * S + s, 1), :] = line[:, h * BLK : (h + 1) * BLK]


def added(x):
    return jnp.sum(x, axis=0, keepdims=True)


def chosen_sums(same, x):
    same, sums = same.astype(BF16), None
    for _ in range(3):
        part = x.astype(BF16)
        y = jnp.dot(same, part, preferred_element_type=F32)
        sums = y if sums is None else sums + y
        x = x - part.astype(F32)
    return sums


def primal_step(
    S, J, R, NZ, HB, own, pieces_ref, other_refs, p_ref, pc_ref, h_ref, hc_ref, cb_ref, hedge, all_sc
):
    K, Q = R * NZ, J * S
    for shift in range(R):
        src = pieces_ref if shift == 0 else other_refs[shift - 1]
        at = lax.rem(own + shift, R) * (NZ * Q)
        all_sc[pl.ds(pl.multiple_of(at, 8), NZ * Q), :] = src[...]
    slot = lambda ref, k: ref[k * Q : (k + 1) * Q, :]
    cols = [slot(cb_ref, k) for k in range(K)]
    parts = [slot(all_sc, k) for k in range(K)]
    placed, hedged = [], []
    for k in range(K):
        add = None
        for m in range(K):
            term = parts[m] if m == k else jnp.where(cols[m] == cols[k], parts[m], 0.0)
            add = term if add is None else add + term
        for h in range(HB):
            add = add + jnp.where(cols[k] == float(h), hedge[h], 0.0)
        placed.append(
            jnp.maximum(slot(p_ref, k) - TAU_STEP * (slot(pc_ref, k) + add), 0.0)
        )
    for h in range(HB):
        add = None
        for m in range(K):
            term = jnp.where(cols[m] == float(h), parts[m], 0.0)
            add = term if add is None else add + term
        add = add + hedge[h]
        hedged.append(jnp.maximum(slot(h_ref, h) - TAU_STEP * (slot(hc_ref, h) + add), 0.0))
    return placed, hedged


def finish_step(
    S, J, R, NZ, HB, own, p_ref, placed, hedged, anchors, ids, wb, same, p_out, h_out, mu_ref, send_ref, step_ref
):
    K, Q = R * NZ, J * S
    for k in range(K):
        p_out[k * Q : (k + 1) * Q, :] = placed[k]
    mine = pl.ds(pl.multiple_of(own * (NZ * Q), 8), NZ * Q)
    step_ref[...] = 2.0 * p_out[mine, :] - p_ref[mine, :]
    for h in range(HB):
        h_out[h * Q : (h + 1) * Q, :] = hedged[h]
    sums = chosen_sums(same[:, :Q], jnp.concatenate([wb * x for x in hedged] + [wb], axis=1))
    mass = sums[:, HB * BLK :]
    inner = []
    for j in range(J):
        mine = ids[j * S : (j + 1) * S]
        inner.append((mine != mine[:1]) & (mine != mine[S - 1 :]))
    inner = jnp.concatenate([x.astype(F32) for x in inner], axis=0)
    gap, drift = jnp.zeros((Q, BLK), F32), jnp.zeros((Q, BLK), F32)
    for h in range(HB):
        mu = sums[:, h * BLK : (h + 1) * BLK] / mass
        mu_ref[h * Q : (h + 1) * Q, :] = mu
        gap = gap + wb * (hedged[h] - mu) ** 2
        drift = drift + (wb * inner) * (mu - anchors[h]) ** 2
    lane = lax.broadcasted_iota(jnp.int32, (1, BLK), 1)
    note = jnp.zeros((1, BLK), F32)
    for j in range(J):
        a, b = j * S, j * S + S - 1
        fresh = ids[b : b + 1] != ids[a : a + 1]
        for f in range(2):
            e = f * J + j
            at = b if f else a
            for h in range(HB):
                line = sums[at : at + 1, h * BLK : (h + 1) * BLK]
                send_ref[pl.ds(e * HB + h, 1), :] = jnp.where(fresh, line, 0.0) if f else line
            name, weight = ids[at : at + 1], mass[at : at + 1]
            if f:
                name, weight = jnp.where(fresh, name, -1.0), jnp.where(fresh, weight, 0.0)
            note = jnp.where(lane == e, name, note)
            note = jnp.where(lane == 2 * J + e, weight, note)
    at = 2 * J * HB
    for i, row in enumerate((note, added(gap), added(drift))):
        send_ref[pl.ds(at + i, 1), :] = row
    rest = send_ref.shape[0] - at - NOTES
    send_ref[pl.ds(at + NOTES, rest), :] = jnp.zeros((rest, BLK), F32)


def first_kernel(
    S, J, R, NZ, HB, pp_ref, pc_ref, hp_ref, hc_ref, cb_ref, ml_ref, an_ref, id_ref, wb_ref, same_ref, pieces_ref, *rest
):
    other_refs = rest[: R - 1]
    p_out, h_out, mu_ref, send_ref, step_ref, all_sc = rest[R - 1 :]
    Q = J * S
    own = lax.axis_index("rows")
    slot = lambda ref, k: ref[k * Q : (k + 1) * Q, :]
    anchors = [slot(an_ref, h) for h in range(HB)]
    hedge = [
        slot(ml_ref, h) + RHO_START * (slot(hp_ref, h) - anchors[h]) for h in range(HB)
    ]
    placed, hedged = primal_step(
        S, J, R, NZ, HB, own, pieces_ref, other_refs, pp_ref, pc_ref, hp_ref, hc_ref, cb_ref, hedge, all_sc
    )
    finish_step(
        S, J, R, NZ, HB, own, pp_ref, placed, hedged, anchors, id_ref[...], wb_ref[...], same_ref[...], p_out, h_out, mu_ref, send_ref, step_ref
    )


def read_nodes(J, HB, got_ref, ids, devices):
    E = 2 * J
    sums = [
        jnp.concatenate(
            [got_ref[pl.ds(e * HB + h, devices, stride=E * HB), :] for e in range(E)], axis=0
        )
        for h in range(HB)
    ]
    notes, gaps, drifts = (
        got_ref[pl.ds(E * HB * devices + i, devices, stride=NOTES), :] for i in range(NOTES)
    )
    wide = lambda at: jnp.broadcast_to(notes[:, at : at + 1], (devices, BLK))
    names = jnp.concatenate([wide(e) for e in range(E)], axis=0)
    weight = jnp.concatenate([wide(E + e) for e in range(E)], axis=0)
    every = jnp.concatenate([ids, names], axis=0)
    across = jnp.transpose(names)[0:1, :]
    count = E * devices
    same = (jnp.broadcast_to(every[:, :1], (every.shape[0], count)) == across).astype(F32)
    totals = chosen_sums(same, jnp.concatenate(sums + [weight], axis=1))
    mass = totals[:, HB * BLK :]
    positive = mass > 0
    safe = jnp.where(positive, mass, 1.0)
    means = [
        jnp.where(positive, totals[:, h * BLK : (h + 1) * BLK] / safe, 0.0) for h in range(HB)
    ]
    own_safe = jnp.where(weight > 0, weight, 1.0)
    rows = ids.shape[0]
    spread = jnp.zeros((count, BLK), F32)
    for h in range(HB):
        spread = spread + weight * (sums[h] / own_safe - means[h][rows:]) ** 2
    gap, drift = added(gaps) + added(spread), added(drifts)
    return positive[:rows], [m[:rows] for m in means], [m[rows:] for m in means], weight, gap, drift


def moved(weight, means, before):
    change = jnp.zeros_like(weight)
    for mean, old in zip(means, before):
        change = change + weight * (mean - old) ** 2
    return added(change)


def put_sums(gap, drift, out_ref):
    out_ref[...] = jnp.concatenate(
        [gap, drift, jnp.zeros((out_ref.shape[0] - 2, BLK), F32)], axis=0
    )


def scaled(penalty, own_ref, other_refs):
    sums = own_ref[...]
    for ref in other_refs:
        sums = sums + ref[...]
    sums = jnp.sum(sums, axis=1, keepdims=True)
    return penalty * jnp.sqrt(sums[0:1] / (sums[1:2] + EPSILON))


def nodes_kernel(
    S, J, HB, devices, got_ref, id_ref, mu_ref, h_ref, ml_ref, table_ref, an_out, ml_out, ent_ref, sums_ref, old_sc
):
    Q, E = J * S, 2 * J
    names = got_ref[pl.ds(E * HB * devices, devices, stride=NOTES), :]
    names = jnp.maximum(names, 0.0).astype(jnp.int32)
    shared, means, entry_means, weight, gap, drift = read_nodes(
        J, HB, got_ref, id_ref[...], devices
    )
    for h in range(HB):
        at = pl.ds(h * Q, Q)
        ent_ref[h] = entry_means[h]
        anchor = jnp.where(shared, means[h], mu_ref[at, :])
        an_out[at, :] = anchor
        ml_out[at, :] = ml_ref[at, :] + RHO_START * (h_ref[at, :] - anchor)
    for e in range(E):
        for d in range(devices):
            old_sc[pl.ds(e * devices + d, 1), :] = table_ref[pl.ds(names[d, e], 1), :]
    before = [old_sc[:, h * BLK : (h + 1) * BLK] for h in range(HB)]
    put_sums(gap, drift + moved(weight, entry_means, before), sums_ref)


def second_kernel(
    S, J, R, NZ, HB, pp_ref, pc_ref, hp_ref, hc_ref, cb_ref, ml_ref, an_ref, id_ref, wb_ref, same_ref, sums_ref, sums2_ref, pieces_ref, *rest
):
    other_refs = rest[: R - 1]
    p_out, h_out, mu_out, send_ref, step_ref, pen_ref, all_sc = rest[R - 1 :]
    Q = J * S
    own = lax.axis_index("rows")
    slot = lambda ref, k: ref[k * Q : (k + 1) * Q, :]
    penalty = scaled(RHO_START, sums_ref, [sums2_ref])
    pen_ref[...] = jnp.broadcast_to(penalty, pen_ref.shape)
    anchors = [slot(an_ref, h) for h in range(HB)]
    hedge = [slot(ml_ref, h) + penalty * (slot(hp_ref, h) - anchors[h]) for h in range(HB)]
    placed, hedged = primal_step(
        S, J, R, NZ, HB, own, pieces_ref, other_refs, pp_ref, pc_ref, hp_ref, hc_ref, cb_ref, hedge, all_sc
    )
    finish_step(
        S, J, R, NZ, HB, own, pp_ref, placed, hedged, anchors, id_ref[...], wb_ref[...], same_ref[...], p_out, h_out, mu_out, send_ref, step_ref
    )


def last_kernel(
    S, J, HB, devices, got_ref, id_ref, ent_ref, mu_ref, h_ref, ml_ref, pen_ref, ml_out, sums_ref
):
    Q = J * S
    shared, means, entry_means, weight, gap, drift = read_nodes(
        J, HB, got_ref, id_ref[...], devices
    )
    drift = drift + moved(weight, entry_means, [ent_ref[h] for h in range(HB)])
    put_sums(gap, drift, sums_ref)
    penalty = pen_ref[0:1, 0:1]
    for h in range(HB):
        at = pl.ds(h * Q, Q)
        anchor = jnp.where(shared, means[h], mu_ref[at, :])
        ml_out[at, :] = ml_ref[at, :] + penalty * (h_ref[at, :] - anchor)


def finish_kernel(
    S, J, HB, ml_ref, dual_ref, rhs_ref, image_ref, image2_ref, ml_out, dual_out
):
    for h in range(HB):
        for j in range(J):
            src = pl.ds(h * J * S + j * S, S)
            ml_out[pl.ds(h * J + j, S, stride=HB * J), :] = ml_ref[src, :]
    image = image_ref[...] + image2_ref[...]
    dual_out[...] = jnp.maximum(dual_ref[...] + SIGMA_STEP * (image - rhs_ref[...]), 0.0)


def penalty_kernel(pen_ref, sums_ref, sums2_ref, out_ref):
    out_ref[...] = scaled(pen_ref[0:1, 0:1], sums_ref, [sums2_ref])


def bulk_kernel(S, primal_ref, cost_ref, out_ref):
    for s in range(S):
        move = TAU_STEP * cost_ref[s].astype(F32)
        x = primal_ref[s].astype(F32)
        for _ in range(SWEEPS):
            x = jnp.maximum(x - move, 0.0)
        out_ref[s] = x


def place_kernel(S, J, R, NZ, HB, first, count, parts, cols_ref, bulk_ref, p_ref, h_ref, *rest):
    near_ref, out_hbm, sems = rest[-3:]
    K, Q = R * NZ, J * S
    step = count // parts
    copies = []
    for i in range(count):
        s = first + i
        for j in range(J):
            for k in range(K):
                c = cols_ref[k // NZ, j, k % NZ, s]
                near_ref[s, pl.ds(c * J + j, 1), :] = p_ref[pl.ds(k * Q + j * S + s, 1), :]
            for h in range(HB):
                near_ref[s, pl.ds(h * J + j, 1), :] = h_ref[pl.ds(h * Q + j * S + s, 1), :]
        if (i + 1) % step == 0:
            at = pl.ds(s + 1 - step, step)
            copies.append(
                pltpu.make_async_copy(near_ref.at[at], out_hbm.at[at], sems.at[i // step])
            )
            copies[-1].start()
    for copy in copies:
        copy.wait()


def merge_kernel(apart, count, sums, x_ref, y_ref, *rest):
    out_ref = rest[-1]
    rows = count * sums
    high = lax.rem(lax.axis_index("scen") // apart, 2)
    for place, ref in ((high, x_ref), (1 - high, y_ref)):
        out_ref[pl.ds(pl.multiple_of(place * rows, 8), rows), :] = ref[:rows, :]
        for i in range(NOTES * count):
            at = 2 * rows + place * (NOTES * count) + i
            out_ref[pl.ds(at, 1), :] = ref[rows + i : rows + i + 1, :]
    used = 2 * rows + 2 * NOTES * count
    if out_ref.shape[0] > used:
        out_ref[used:, :] = jnp.zeros((out_ref.shape[0] - used, BLK), F32)


def local(
    sizes,
    lp_blocks,
    block_columns,
    scenario_nodes,
    scenario_weights,
    cost,
    bounds_rhs,
    primal_start,
    dual_start,
    multiplier_start,
    consensus_start,
):
    scens, R, sections = sizes
    S, J, columns = cost.shape
    NZ = lp_blocks.shape[3]
    hedged = multiplier_start.shape[2]
    HB, C = hedged // BLK, columns // BLK
    K, Q = R * NZ, J * S
    devices = scens
    message = -(-(2 * J * HB + NOTES) // 8) * 8
    static = (S, J, R, NZ, HB)

    def interleave(x):
        return x.reshape(S, J, -1, BLK).transpose(0, 2, 1, 3).reshape(S, -1, BLK)

    def uninterleave(x):
        return x.reshape(S, -1, J, BLK).transpose(0, 2, 1, 3).reshape(S, J, -1)

    columns_of = block_columns.transpose(1, 2, 3, 0)
    lp = in_hbm(lp_blocks.reshape(S, J * NZ, BLK, BLK))
    primal, price = in_hbm(interleave(primal_start)), in_vmem(interleave(cost))
    mult = interleave(multiplier_start).reshape(S * HB * J, BLK)

    def from_rows(x):
        return [
            lax.ppermute(x, "rows", [((i + q) % R, i) for i in range(R)]) for q in range(1, R)
        ]

    def from_section(x):
        return lax.ppermute(x, "section", [(i, (i + 1) % sections) for i in range(sections)])

    def partner(x, apart):
        return lax.ppermute(x, "scen", [(i, i ^ apart) for i in range(scens)])

    def merge(x, y, apart, count, least, *after):
        rows = max(least, 2 * count * (2 * J * HB) + -(-2 * NOTES * count // 8) * 8)
        return pl.pallas_call(
            functools.partial(merge_kernel, apart, count, 2 * J * HB),
            out_shape=near(rows, BLK),
            in_specs=[VMEM] * 2 + [HBM if far else VMEM for far, _ in after],
            out_specs=VMEM,
            compiler_params=params(4),
            name="merge",
        )(x, y, *[in_hbm(z) if far else z for far, z in after])

    def exchange(x, least, *work):
        assert scens & (scens - 1) == 0
        apart, turn = scens // 2, 0
        while apart:
            y = partner(x, apart)
            x = merge(x, y, apart, 1 << turn, least if apart == 2 else 0, *(work[turn]() if turn < len(work) else ()))
            apart, turn = apart // 2, turn + 1
        return x

    def near_like(x):
        return pltpu.VMEM(x.shape, x.dtype)

    parts = max(p for p in (3, 2, 1) if S % p == 0)
    pieces, lp, primal = pl.pallas_call(
        functools.partial(pieces_kernel, S, J, NZ),
        out_shape=[near(NZ * Q, BLK), near_like(lp), near_like(primal)],
        in_specs=[HBM] * 3,
        out_specs=[VMEM] * 3,
        scratch_shapes=[
            pltpu.SemaphoreType.DMA((parts,)),
            pltpu.VMEM(dual_start.shape, F32),
            pltpu.SemaphoreType.DMA,
            pltpu.SemaphoreType.DMA,
        ],
        compiler_params=params(16),
        name="pieces",
    )(lp, in_hbm(dual_start), primal)
    others = from_rows(pieces)

    pp, pc, hp, hc, cb, ml, an, ids, wb, same, table = pl.pallas_call(
        functools.partial(setup_kernel, *static),
        out_shape=[near(K * Q, BLK)] * 2
        + [near(HB * Q, BLK)] * 2
        + [near(K * Q, BLK)]
        + [near(HB * Q, BLK)] * 2
        + [near(Q, BLK)] * 3
        + [near_like(consensus_start)],
        in_specs=[VMEM] * 6 + [HBM],
        out_specs=[VMEM] * 11,
        scratch_shapes=[pltpu.VMEM((S * K * J, BLK), F32)] * 3
        + [pltpu.VMEM((S * HB * J, BLK), F32)] * 2
        + [pltpu.SemaphoreType.DMA],
        compiler_params=params(16),
        name="setup",
    )(
        scenario_nodes,
        scenario_weights.reshape(1, S),
        columns_of.reshape(K * J, S),
        in_vmem(primal),
        price,
        mult,
        in_hbm(consensus_start),
    )
    primal = in_vmem(primal)

    def step_out(rows):
        return [
            near(K * Q, BLK),
            near(HB * Q, BLK),
            near(HB * Q, BLK),
            near(rows, BLK),
            near(NZ * Q, BLK),
        ]

    def image_of(step):
        return pl.pallas_call(
            functools.partial(image_kernel, S, J, NZ),
            out_shape=near(S, BLK),
            in_specs=[VMEM] * 2,
            out_specs=VMEM,
            compiler_params=params(8),
            name="image",
        )(lp, step)

    scratch = [pltpu.VMEM((K * Q, BLK), F32)]
    p1, h1, mu1, send1, step1 = pl.pallas_call(
        functools.partial(first_kernel, *static),
        out_shape=step_out(message),
        in_specs=[VMEM] * (11 + R - 1),
        out_specs=[VMEM] * 5,
        scratch_shapes=scratch,
        compiler_params=params(8),
        name="first",
    )(pp, pc, hp, hc, cb, ml, an, ids, wb, same, pieces, *others)
    made = {}

    def image_work():
        made["image"] = image_of(step1)
        return ((False, made["image"]),)

    def dual_work():
        made["bulk"] = pl.pallas_call(
            functools.partial(bulk_kernel, S),
            out_shape=near(S, C * J, BLK),
            in_specs=[VMEM] * 2,
            out_specs=VMEM,
            compiler_params=params(8),
            name="bulk",
        )(primal, price)
        made["dual"], made["pieces"] = pl.pallas_call(
            functools.partial(dual_kernel, S, J, NZ),
            out_shape=[near(S, BLK), near(NZ * Q, BLK)],
            in_specs=[VMEM] * 5,
            out_specs=[VMEM] * 2,
            compiler_params=params(8),
            name="dual",
        )(lp, dual_start, bounds_rhs, made["image"], from_section(made["image"]))
        return ((False, made["pieces"]), (False, made["bulk"]))

    got1 = exchange(send1, 88, image_work, dual_work)
    dual1, pieces2 = made["dual"], made["pieces"]
    others2 = from_rows(pieces2)

    an1, ml1, ent1, sums1 = pl.pallas_call(
        functools.partial(nodes_kernel, S, J, HB, devices),
        out_shape=[near(HB * Q, BLK)] * 2 + [near(HB, 2 * J * devices, BLK), near(8, BLK)],
        in_specs=[VMEM] * 6,
        out_specs=[VMEM] * 4,
        scratch_shapes=[
            pltpu.VMEM((2 * J * devices, hedged), F32),
        ],
        compiler_params=params(8),
        name="nodes",
    )(got1, ids, mu1, h1, ml, table)
    sums1b = from_section(sums1)

    p2, h2, mu2, send2, step2, pen1 = pl.pallas_call(
        functools.partial(second_kernel, *static),
        out_shape=step_out(message) + [near(8, BLK)],
        in_specs=[VMEM] * (13 + R - 1),
        out_specs=[VMEM] * 6,
        scratch_shapes=scratch,
        compiler_params=params(8),
        name="second",
    )(p1, pc, h1, hc, cb, ml1, an1, ids, wb, same, sums1, sums1b, pieces2, *others2)
    half = S * 5 // 12

    def place(first, count, whole, *into):
        cuts = max(p for p in (2, 1) if count % p == 0)
        return pl.pallas_call(
            functools.partial(place_kernel, *static, first, count, cuts),
            out_shape=[near(S, C * J, BLK), shape(S, C * J, BLK)],
            in_specs=[SMEM] + [VMEM] * 3 + [HBM] * len(into),
            out_specs=[VMEM, HBM],
            scratch_shapes=[pltpu.SemaphoreType.DMA((cuts,))],
            input_output_aliases={1: 0, 4: 1} if into else {1: 0},
            compiler_params=params(4),
            name="place",
        )(columns_of, whole, p2, h2, *into)

    def last_image_work():
        made["image"] = image_of(step2)
        return ((False, made["image"]),)

    def place_work():
        made["bulk"], made["out"] = place(0, half, made["bulk"])
        return ((True, made["out"]),)

    def rest_work():
        made["bulk"], made["out"] = place(half, S - half, made["bulk"], made["out"])
        return ((True, made["out"]),)

    got2 = exchange(send2, 0, last_image_work, place_work, rest_work)
    out, image2 = made["out"], made["image"]
    ml2, sums2 = pl.pallas_call(
        functools.partial(last_kernel, S, J, HB, devices),
        out_shape=[near(HB * Q, BLK), near(8, BLK)],
        in_specs=[VMEM] * 7,
        out_specs=[VMEM] * 2,
        compiler_params=params(8),
        name="last",
    )(got2, ids, ent1, mu2, h2, ml1, pen1)
    ml2, dual2 = pl.pallas_call(
        functools.partial(finish_kernel, S, J, HB),
        out_shape=[shape(S * HB * J, BLK), shape(S, BLK)],
        in_specs=[VMEM] * 5,
        out_specs=[VMEM] * 2,
        compiler_params=params(4),
        name="finish",
    )(ml2, dual1, bounds_rhs, image2, from_section(image2))
    pen2 = pl.pallas_call(
        penalty_kernel,
        out_shape=shape(1, 1),
        in_specs=[VMEM] * 3,
        out_specs=VMEM,
        compiler_params=params(4),
        name="penalty",
    )(pen1, sums2, from_section(sums2))

    return (
        uninterleave(out),
        dual2,
        uninterleave(ml2.reshape(S, HB * J, BLK)),
        pen2.reshape(()),
    )


def solution(mesh):
    sizes = tuple(mesh.shape[a] for a in ("scen", "rows", "section"))
    in_specs = (
        P("scen", "rows", "section", None, None, None),
        P("scen", None, "section", None),
        P(None, "scen"),
        P("scen"),
        P("scen", "section", None),
        P("scen", "rows"),
        P("scen", "section", None),
        P("scen", "rows"),
        P("scen", "section", None),
        P(),
    )
    out_specs = (P("scen", "section", None), P("scen", "rows"), P("scen", "section", None), P())
    return jax.shard_map(
        functools.partial(local, sizes),
        mesh=mesh,
        in_specs=in_specs,
        out_specs=out_specs,
        check_vma=False,
    )
```

```python
import functools

import jax
import jax.numpy as jnp
from jax import lax
from jax.experimental import pallas as pl
from jax.experimental.pallas import tpu as pltpu
from jax.sharding import PartitionSpec as P

BLK = 128
N1 = 8
N2 = 64
SWEEPS = 2
TAU_STEP = 0.4
SIGMA_STEP = 0.4
RHO_START = 1.0
EPSILON = 1e-06
F32 = jnp.float32
BF16 = jnp.bfloat16
NOTES = 3

VMEM = pl.BlockSpec(memory_space=pltpu.VMEM)
SMEM = pl.BlockSpec(memory_space=pltpu.SMEM)
HBM = pl.BlockSpec(memory_space=pltpu.HBM)


def params(mib=16):
    return pltpu.CompilerParams(vmem_limit_bytes=mib << 20)


def in_vmem(x):
    return pltpu.with_memory_space_constraint(x, pltpu.VMEM)


def in_hbm(x):
    return pltpu.with_memory_space_constraint(x, pltpu.HBM)


def shape(*dims):
    return jax.ShapeDtypeStruct(dims, F32)


def near(*dims):
    return pltpu.VMEM(dims, F32)


def cut(src_ref, dst_ref, sems, parts):
    step = src_ref.shape[0] // parts
    at = [pl.ds(i * step, step) for i in range(parts)]
    return [
        pltpu.make_async_copy(src_ref.at[a], dst_ref.at[a], sems.at[i]) for i, a in enumerate(at)
    ]


def write_pieces(lp_ref, dual, out_ref, S, J, NZ, before=lambda s: None):
    for s in range(S):
        before(s)
        row = dual[s : s + 1, :].astype(BF16)
        for j in range(J):
            for n in range(NZ):
                y = jnp.dot(row, lp_ref[s, j * NZ + n], preferred_element_type=F32)
                out_ref[pl.ds((n * J + j) * S + s, 1), :] = y


def image_kernel(S, J, NZ, lp_ref, step_ref, image_ref):
    for s in range(S):
        total = None
        for j in range(J):
            for n in range(NZ):
                x = step_ref[pl.ds((n * J + j) * S + s, 1), :].astype(BF16)
                y = lax.dot_general(
                    x,
                    lp_ref[s, j * NZ + n],
                    (((1,), (1,)), ((), ())),
                    preferred_element_type=F32,
                )
                total = y if total is None else total + y
        image_ref[pl.ds(s, 1), :] = total


def pieces_kernel(
    S, J, NZ, lp_hbm, dual_hbm, primal_hbm, out_ref, lp_ref, primal_ref, sems, dual_ref, sem, primal_sem
):
    parts = sems.shape[0]
    dual_copy = pltpu.make_async_copy(dual_hbm, dual_ref, sem)
    dual_copy.start()
    copies = cut(lp_hbm, lp_ref, sems, parts)
    for copy in copies:
        copy.start()
    primal_copy = pltpu.make_async_copy(primal_hbm, primal_ref, primal_sem)
    primal_copy.start()
    dual_copy.wait()

    def before(s):
        if s % (S // parts) == 0:
            copies[s // (S // parts)].wait()

    write_pieces(lp_ref, dual_ref[...], out_ref, S, J, NZ, before)
    primal_copy.wait()


def dual_kernel(S, J, NZ, lp_ref, dual_ref, rhs_ref, image_ref, image2_ref, next_ref, out_ref):
    image = image_ref[...] + image2_ref[...]
    dual = jnp.maximum(dual_ref[...] + SIGMA_STEP * (image - rhs_ref[...]), 0.0)
    next_ref[...] = dual
    write_pieces(lp_ref, dual, out_ref, S, J, NZ)


def down(row, count):
    return jnp.transpose(jnp.broadcast_to(row, (BLK, row.shape[1])))[:count]


def setup_kernel(
    S,
    J,
    R,
    NZ,
    HB,
    nodes_ref,
    weights_ref,
    cols_ref,
    primal_ref,
    cost_ref,
    mult_ref,
    table_hbm,
    pp_ref,
    pc_ref,
    hp_ref,
    hc_ref,
    cb_ref,
    ml_ref,
    an_ref,
    id_ref,
    wb_ref,
    same_ref,
    table_ref,
    idx_sc,
    pp_sc,
    pc_sc,
    hp_sc,
    hc_sc,
    table_sem,
):
    K, Q = R * NZ, J * S
    table_copy = pltpu.make_async_copy(table_hbm, table_ref, table_sem)
    table_copy.start()
    section = lax.axis_index("section")
    rows = primal_ref.shape[1]

    cols = cols_ref[...]
    section_of = lax.rem(lax.broadcasted_iota(jnp.int32, (K * J, BLK), 0) // NZ, J)
    tiles = -(-rows // BLK)
    lane = lax.broadcasted_iota(jnp.int32, (K * J, BLK), 1)
    picks = []
    for s in range(S):
        want = jnp.broadcast_to(cols[:, s : s + 1], (K * J, BLK))
        idx_sc[pl.ds(s * K * J, K * J), :] = want.astype(F32)
        want = want * J + section_of
        picks.append(
            jnp.concatenate(
                [(want == lane + t * BLK).astype(F32).astype(BF16) for t in range(tiles)], axis=1
            )[:, :rows]
        )

    def gather(source_ref, placed_ref, hedged_ref):
        for s in range(S):
            placed_ref[pl.ds(s * K * J, K * J), :] = jnp.dot(
                picks[s], source_ref[s], preferred_element_type=F32
            )
            hedged_ref[pl.ds(s * HB * J, HB * J), :] = source_ref[s, : HB * J, :].astype(F32)

    def placed_rows(k, j):
        return pl.ds(((k // NZ) * J + j) * NZ + k % NZ, S, stride=K * J), pl.ds(k * Q + j * S, S)

    def hedged_rows(h, j):
        return pl.ds(h * J + j, S, stride=HB * J), pl.ds(h * Q + j * S, S)

    gather(primal_ref, pp_sc, hp_sc)
    gather(cost_ref, pc_sc, hc_sc)
    weights = down(weights_ref[...], S)
    ids, picked = [], []
    for j in range(J):
        g = section * J + j
        own = jnp.zeros((1, nodes_ref.shape[1]), jnp.int32)
        for level, off in enumerate((1, 1 + N1, 1 + N1 + N2)):
            own = jnp.where(g == level + 1, nodes_ref[level : level + 1, :] + off, own)
        ids.append(down(own.astype(F32), S))
        picked.append(own)
        wb_ref[pl.ds(j * S, S), :] = weights
    ids = jnp.concatenate(ids, axis=0)
    id_ref[...] = ids
    across = jnp.transpose(ids)[0:1, :Q]
    same_ref[:, :Q] = (jnp.broadcast_to(ids[:, :1], (Q, Q)) == across).astype(F32)
    for j in range(J):
        for k in range(K):
            src, dst = placed_rows(k, j)
            pp_ref[dst, :] = pp_sc[src, :]
            pc_ref[dst, :] = pc_sc[src, :]
            cb_ref[dst, :] = idx_sc[src, :]
        for h in range(HB):
            src, dst = hedged_rows(h, j)
            hp_ref[dst, :] = hp_sc[src, :]
            hc_ref[dst, :] = hc_sc[src, :]
            ml_ref[dst, :] = mult_ref[src, :]
    table_copy.wait()
    for j in range(J):
        for s in range(S):
            line = table_ref[pl.ds(picked[j][0, s], 1), :]
            for h in range(HB):
                an_ref[pl.ds(h * Q + j * S + s, 1), :] = line[:, h * BLK : (h + 1) * BLK]


def added(x):
    return jnp.sum(x, axis=0, keepdims=True)


def chosen_sums(same, x):
    same, sums = same.astype(BF16), None
    for _ in range(3):
        part = x.astype(BF16)
        y = jnp.dot(same, part, preferred_element_type=F32)
        sums = y if sums is None else sums + y
        x = x - part.astype(F32)
    return sums


def primal_step(
    S, J, R, NZ, HB, own, pieces_ref, other_refs, p_ref, pc_ref, h_ref, hc_ref, cb_ref, hedge, all_sc
):
    K, Q = R * NZ, J * S
    for shift in range(R):
        src = pieces_ref if shift == 0 else other_refs[shift - 1]
        at = lax.rem(own + shift, R) * (NZ * Q)
        all_sc[pl.ds(pl.multiple_of(at, 8), NZ * Q), :] = src[...]
    slot = lambda ref, k: ref[k * Q : (k + 1) * Q, :]
    cols = [slot(cb_ref, k) for k in range(K)]
    parts = [slot(all_sc, k) for k in range(K)]
    placed, hedged = [], []
    for k in range(K):
        add = None
        for m in range(K):
            term = parts[m] if m == k else jnp.where(cols[m] == cols[k], parts[m], 0.0)
            add = term if add is None else add + term
        for h in range(HB):
            add = add + jnp.where(cols[k] == float(h), hedge[h], 0.0)
        placed.append(
            jnp.maximum(slot(p_ref, k) - TAU_STEP * (slot(pc_ref, k) + add), 0.0)
        )
    for h in range(HB):
        add = None
        for m in range(K):
            term = jnp.where(cols[m] == float(h), parts[m], 0.0)
            add = term if add is None else add + term
        add = add + hedge[h]
        hedged.append(jnp.maximum(slot(h_ref, h) - TAU_STEP * (slot(hc_ref, h) + add), 0.0))
    return placed, hedged


def finish_step(
    S, J, R, NZ, HB, own, p_ref, placed, hedged, anchors, ids, wb, same, p_out, h_out, mu_ref, send_ref, step_ref
):
    K, Q = R * NZ, J * S
    for k in range(K):
        p_out[k * Q : (k + 1) * Q, :] = placed[k]
    mine = pl.ds(pl.multiple_of(own * (NZ * Q), 8), NZ * Q)
    step_ref[...] = 2.0 * p_out[mine, :] - p_ref[mine, :]
    for h in range(HB):
        h_out[h * Q : (h + 1) * Q, :] = hedged[h]
    sums = chosen_sums(same[:, :Q], jnp.concatenate([wb * x for x in hedged] + [wb], axis=1))
    mass = sums[:, HB * BLK :]
    inner = []
    for j in range(J):
        mine = ids[j * S : (j + 1) * S]
        inner.append((mine != mine[:1]) & (mine != mine[S - 1 :]))
    inner = jnp.concatenate([x.astype(F32) for x in inner], axis=0)
    gap, drift = jnp.zeros((Q, BLK), F32), jnp.zeros((Q, BLK), F32)
    for h in range(HB):
        mu = sums[:, h * BLK : (h + 1) * BLK] / mass
        mu_ref[h * Q : (h + 1) * Q, :] = mu
        gap = gap + wb * (hedged[h] - mu) ** 2
        drift = drift + (wb * inner) * (mu - anchors[h]) ** 2
    lane = lax.broadcasted_iota(jnp.int32, (1, BLK), 1)
    note = jnp.zeros((1, BLK), F32)
    for j in range(J):
        a, b = j * S, j * S + S - 1
        fresh = ids[b : b + 1] != ids[a : a + 1]
        for f in range(2):
            e = f * J + j
            at = b if f else a
            for h in range(HB):
                line = sums[at : at + 1, h * BLK : (h + 1) * BLK]
                send_ref[pl.ds(e * HB + h, 1), :] = jnp.where(fresh, line, 0.0) if f else line
            name, weight = ids[at : at + 1], mass[at : at + 1]
            if f:
                name, weight = jnp.where(fresh, name, -1.0), jnp.where(fresh, weight, 0.0)
            note = jnp.where(lane == e, name, note)
            note = jnp.where(lane == 2 * J + e, weight, note)
    at = 2 * J * HB
    for i, row in enumerate((note, added(gap), added(drift))):
        send_ref[pl.ds(at + i, 1), :] = row
    rest = send_ref.shape[0] - at - NOTES
    send_ref[pl.ds(at + NOTES, rest), :] = jnp.zeros((rest, BLK), F32)


def first_kernel(
    S, J, R, NZ, HB, pp_ref, pc_ref, hp_ref, hc_ref, cb_ref, ml_ref, an_ref, id_ref, wb_ref, same_ref, pieces_ref, *rest
):
    other_refs = rest[: R - 1]
    p_out, h_out, mu_ref, send_ref, step_ref, all_sc = rest[R - 1 :]
    Q = J * S
    own = lax.axis_index("rows")
    slot = lambda ref, k: ref[k * Q : (k + 1) * Q, :]
    anchors = [slot(an_ref, h) for h in range(HB)]
    hedge = [
        slot(ml_ref, h) + RHO_START * (slot(hp_ref, h) - anchors[h]) for h in range(HB)
    ]
    placed, hedged = primal_step(
        S, J, R, NZ, HB, own, pieces_ref, other_refs, pp_ref, pc_ref, hp_ref, hc_ref, cb_ref, hedge, all_sc
    )
    finish_step(
        S, J, R, NZ, HB, own, pp_ref, placed, hedged, anchors, id_ref[...], wb_ref[...], same_ref[...], p_out, h_out, mu_ref, send_ref, step_ref
    )


def read_nodes(J, HB, got_ref, ids, devices):
    E = 2 * J
    sums = [
        jnp.concatenate(
            [got_ref[pl.ds(e * HB + h, devices, stride=E * HB), :] for e in range(E)], axis=0
        )
        for h in range(HB)
    ]
    notes, gaps, drifts = (
        got_ref[pl.ds(E * HB * devices + i, devices, stride=NOTES), :] for i in range(NOTES)
    )
    wide = lambda at: jnp.broadcast_to(notes[:, at : at + 1], (devices, BLK))
    names = jnp.concatenate([wide(e) for e in range(E)], axis=0)
    weight = jnp.concatenate([wide(E + e) for e in range(E)], axis=0)
    every = jnp.concatenate([ids, names], axis=0)
    across = jnp.transpose(names)[0:1, :]
    count = E * devices
    same = (jnp.broadcast_to(every[:, :1], (every.shape[0], count)) == across).astype(F32)
    totals = chosen_sums(same, jnp.concatenate(sums + [weight], axis=1))
    mass = totals[:, HB * BLK :]
    positive = mass > 0
    safe = jnp.where(positive, mass, 1.0)
    means = [
        jnp.where(positive, totals[:, h * BLK : (h + 1) * BLK] / safe, 0.0) for h in range(HB)
    ]
    own_safe = jnp.where(weight > 0, weight, 1.0)
    rows = ids.shape[0]
    spread = jnp.zeros((count, BLK), F32)
    for h in range(HB):
        spread = spread + weight * (sums[h] / own_safe - means[h][rows:]) ** 2
    gap, drift = added(gaps) + added(spread), added(drifts)
    return positive[:rows], [m[:rows] for m in means], [m[rows:] for m in means], weight, gap, drift


def moved(weight, means, before):
    change = jnp.zeros_like(weight)
    for mean, old in zip(means, before):
        change = change + weight * (mean - old) ** 2
    return added(change)


def put_sums(gap, drift, out_ref):
    out_ref[...] = jnp.concatenate(
        [gap, drift, jnp.zeros((out_ref.shape[0] - 2, BLK), F32)], axis=0
    )


def scaled(penalty, own_ref, other_refs):
    sums = own_ref[...]
    for ref in other_refs:
        sums = sums + ref[...]
    sums = jnp.sum(sums, axis=1, keepdims=True)
    return penalty * jnp.sqrt(sums[0:1] / (sums[1:2] + EPSILON))


def nodes_kernel(
    S, J, HB, devices, got_ref, id_ref, mu_ref, h_ref, ml_ref, table_ref, an_out, ml_out, ent_ref, sums_ref, old_sc
):
    Q, E = J * S, 2 * J
    names = got_ref[pl.ds(E * HB * devices, devices, stride=NOTES), :]
    names = jnp.maximum(names, 0.0).astype(jnp.int32)
    shared, means, entry_means, weight, gap, drift = read_nodes(
        J, HB, got_ref, id_ref[...], devices
    )
    for h in range(HB):
        at = pl.ds(h * Q, Q)
        ent_ref[h] = entry_means[h]
        anchor = jnp.where(shared, means[h], mu_ref[at, :])
        an_out[at, :] = anchor
        ml_out[at, :] = ml_ref[at, :] + RHO_START * (h_ref[at, :] - anchor)
    for e in range(E):
        for d in range(devices):
            old_sc[pl.ds(e * devices + d, 1), :] = table_ref[pl.ds(names[d, e], 1), :]
    before = [old_sc[:, h * BLK : (h + 1) * BLK] for h in range(HB)]
    put_sums(gap, drift + moved(weight, entry_means, before), sums_ref)


def second_kernel(
    S, J, R, NZ, HB, pp_ref, pc_ref, hp_ref, hc_ref, cb_ref, ml_ref, an_ref, id_ref, wb_ref, same_ref, sums_ref, sums2_ref, pieces_ref, *rest
):
    other_refs = rest[: R - 1]
    p_out, h_out, mu_out, send_ref, step_ref, pen_ref, all_sc = rest[R - 1 :]
    Q = J * S
    own = lax.axis_index("rows")
    slot = lambda ref, k: ref[k * Q : (k + 1) * Q, :]
    penalty = scaled(RHO_START, sums_ref, [sums2_ref])
    pen_ref[...] = jnp.broadcast_to(penalty, pen_ref.shape)
    anchors = [slot(an_ref, h) for h in range(HB)]
    hedge = [slot(ml_ref, h) + penalty * (slot(hp_ref, h) - anchors[h]) for h in range(HB)]
    placed, hedged = primal_step(
        S, J, R, NZ, HB, own, pieces_ref, other_refs, pp_ref, pc_ref, hp_ref, hc_ref, cb_ref, hedge, all_sc
    )
    finish_step(
        S, J, R, NZ, HB, own, pp_ref, placed, hedged, anchors, id_ref[...], wb_ref[...], same_ref[...], p_out, h_out, mu_out, send_ref, step_ref
    )


def last_kernel(
    S, J, HB, devices, got_ref, id_ref, ent_ref, mu_ref, h_ref, ml_ref, pen_ref, ml_out, sums_ref
):
    Q = J * S
    shared, means, entry_means, weight, gap, drift = read_nodes(
        J, HB, got_ref, id_ref[...], devices
    )
    drift = drift + moved(weight, entry_means, [ent_ref[h] for h in range(HB)])
    put_sums(gap, drift, sums_ref)
    penalty = pen_ref[0:1, 0:1]
    for h in range(HB):
        at = pl.ds(h * Q, Q)
        anchor = jnp.where(shared, means[h], mu_ref[at, :])
        ml_out[at, :] = ml_ref[at, :] + penalty * (h_ref[at, :] - anchor)


def finish_kernel(
    S, J, HB, ml_ref, dual_ref, rhs_ref, image_ref, image2_ref, ml_out, dual_out
):
    for h in range(HB):
        for j in range(J):
            src = pl.ds(h * J * S + j * S, S)
            ml_out[pl.ds(h * J + j, S, stride=HB * J), :] = ml_ref[src, :]
    image = image_ref[...] + image2_ref[...]
    dual_out[...] = jnp.maximum(dual_ref[...] + SIGMA_STEP * (image - rhs_ref[...]), 0.0)


def penalty_kernel(pen_ref, sums_ref, sums2_ref, out_ref):
    out_ref[0, 0] = scaled(pen_ref[0:1, 0:1], sums_ref, [sums2_ref])[0, 0]


def bulk_kernel(S, primal_ref, cost_ref, out_ref):
    for s in range(S):
        move = TAU_STEP * cost_ref[s].astype(F32)
        x = primal_ref[s].astype(F32)
        for _ in range(SWEEPS):
            x = jnp.maximum(x - move, 0.0)
        out_ref[s] = x


def place_kernel(S, J, R, NZ, HB, first, count, parts, cols_ref, bulk_ref, p_ref, h_ref, *rest):
    near_ref, out_hbm, sems = rest[-3:]
    K, Q = R * NZ, J * S
    step = count // parts
    copies = []
    for i in range(count):
        s = first + i
        for j in range(J):
            for k in range(K):
                c = cols_ref[k // NZ, j, k % NZ, s]
                near_ref[s, pl.ds(c * J + j, 1), :] = p_ref[pl.ds(k * Q + j * S + s, 1), :]
            for h in range(HB):
                near_ref[s, pl.ds(h * J + j, 1), :] = h_ref[pl.ds(h * Q + j * S + s, 1), :]
        if (i + 1) % step == 0:
            at = pl.ds(s + 1 - step, step)
            copies.append(
                pltpu.make_async_copy(near_ref.at[at], out_hbm.at[at], sems.at[i // step])
            )
            copies[-1].start()
    for copy in copies:
        copy.wait()


def merge_kernel(apart, count, sums, x_ref, y_ref, *rest):
    out_ref = rest[-1]
    rows = count * sums
    high = lax.rem(lax.axis_index("scen") // apart, 2)
    for place, ref in ((high, x_ref), (1 - high, y_ref)):
        out_ref[pl.ds(pl.multiple_of(place * rows, 8), rows), :] = ref[:rows, :]
        for i in range(NOTES * count):
            at = 2 * rows + place * (NOTES * count) + i
            out_ref[pl.ds(at, 1), :] = ref[rows + i : rows + i + 1, :]
    used = 2 * rows + 2 * NOTES * count
    if out_ref.shape[0] > used:
        out_ref[used:, :] = jnp.zeros((out_ref.shape[0] - used, BLK), F32)


def local(
    sizes,
    lp_blocks,
    block_columns,
    scenario_nodes,
    scenario_weights,
    cost,
    bounds_rhs,
    primal_start,
    dual_start,
    multiplier_start,
    consensus_start,
):
    scens, R, sections = sizes
    S, J, columns = cost.shape
    NZ = lp_blocks.shape[3]
    hedged = multiplier_start.shape[2]
    HB, C = hedged // BLK, columns // BLK
    K, Q = R * NZ, J * S
    devices = scens
    message = -(-(2 * J * HB + NOTES) // 8) * 8
    static = (S, J, R, NZ, HB)

    def interleave(x):
        return x.reshape(S, J, -1, BLK).transpose(0, 2, 1, 3).reshape(S, -1, BLK)

    def uninterleave(x):
        return x.reshape(S, -1, J, BLK).transpose(0, 2, 1, 3).reshape(S, J, -1)

    columns_of = block_columns.transpose(1, 2, 3, 0)
    lp = in_hbm(lp_blocks.reshape(S, J * NZ, BLK, BLK))
    primal, price = in_hbm(interleave(primal_start)), in_vmem(interleave(cost))
    mult = interleave(multiplier_start).reshape(S * HB * J, BLK)

    def from_rows(x):
        return [
            lax.ppermute(x, "rows", [((i + q) % R, i) for i in range(R)]) for q in range(1, R)
        ]

    def from_section(x):
        return lax.ppermute(x, "section", [(i, (i + 1) % sections) for i in range(sections)])

    def partner(x, apart):
        return lax.ppermute(x, "scen", [(i, i ^ apart) for i in range(scens)])

    def merge(x, y, apart, count, least, *after):
        rows = max(least, 2 * count * (2 * J * HB) + -(-2 * NOTES * count // 8) * 8)
        return pl.pallas_call(
            functools.partial(merge_kernel, apart, count, 2 * J * HB),
            out_shape=near(rows, BLK),
            in_specs=[VMEM] * 2 + [HBM if far else VMEM for far, _ in after],
            out_specs=VMEM,
            compiler_params=params(4),
            name="merge",
        )(x, y, *[in_hbm(z) if far else z for far, z in after])

    def exchange(x, least, *work):
        assert scens & (scens - 1) == 0
        apart, turn = scens // 2, 0
        while apart:
            y = partner(x, apart)
            x = merge(x, y, apart, 1 << turn, least if apart == 2 else 0, *(work[turn]() if turn < len(work) else ()))
            apart, turn = apart // 2, turn + 1
        return x

    def near_like(x):
        return pltpu.VMEM(x.shape, x.dtype)

    parts = max(p for p in (3, 2, 1) if S % p == 0)
    pieces, lp, primal = pl.pallas_call(
        functools.partial(pieces_kernel, S, J, NZ),
        out_shape=[near(NZ * Q, BLK), near_like(lp), near_like(primal)],
        in_specs=[HBM] * 3,
        out_specs=[VMEM] * 3,
        scratch_shapes=[
            pltpu.SemaphoreType.DMA((parts,)),
            pltpu.VMEM(dual_start.shape, F32),
            pltpu.SemaphoreType.DMA,
            pltpu.SemaphoreType.DMA,
        ],
        compiler_params=params(16),
        name="pieces",
    )(lp, in_hbm(dual_start), primal)
    others = from_rows(pieces)

    pp, pc, hp, hc, cb, ml, an, ids, wb, same, table = pl.pallas_call(
        functools.partial(setup_kernel, *static),
        out_shape=[near(K * Q, BLK)] * 2
        + [near(HB * Q, BLK)] * 2
        + [near(K * Q, BLK)]
        + [near(HB * Q, BLK)] * 2
        + [near(Q, BLK)] * 3
        + [near_like(consensus_start)],
        in_specs=[VMEM] * 6 + [HBM],
        out_specs=[VMEM] * 11,
        scratch_shapes=[pltpu.VMEM((S * K * J, BLK), F32)] * 3
        + [pltpu.VMEM((S * HB * J, BLK), F32)] * 2
        + [pltpu.SemaphoreType.DMA],
        compiler_params=params(16),
        name="setup",
    )(
        scenario_nodes,
        scenario_weights.reshape(1, S),
        columns_of.reshape(K * J, S),
        in_vmem(primal),
        price,
        mult,
        in_hbm(consensus_start),
    )
    primal = in_vmem(primal)

    def step_out(rows):
        return [
            near(K * Q, BLK),
            near(HB * Q, BLK),
            near(HB * Q, BLK),
            near(rows, BLK),
            near(NZ * Q, BLK),
        ]

    def image_of(step):
        return pl.pallas_call(
            functools.partial(image_kernel, S, J, NZ),
            out_shape=near(S, BLK),
            in_specs=[VMEM] * 2,
            out_specs=VMEM,
            compiler_params=params(8),
            name="image",
        )(lp, step)

    scratch = [pltpu.VMEM((K * Q, BLK), F32)]
    p1, h1, mu1, send1, step1 = pl.pallas_call(
        functools.partial(first_kernel, *static),
        out_shape=step_out(message),
        in_specs=[VMEM] * (11 + R - 1),
        out_specs=[VMEM] * 5,
        scratch_shapes=scratch,
        compiler_params=params(8),
        name="first",
    )(pp, pc, hp, hc, cb, ml, an, ids, wb, same, pieces, *others)
    made = {}

    def image_work():
        made["image"] = image_of(step1)
        return ((False, made["image"]),)

    def dual_work():
        made["bulk"] = pl.pallas_call(
            functools.partial(bulk_kernel, S),
            out_shape=near(S, C * J, BLK),
            in_specs=[VMEM] * 2,
            out_specs=VMEM,
            compiler_params=params(8),
            name="bulk",
        )(primal, price)
        made["dual"], made["pieces"] = pl.pallas_call(
            functools.partial(dual_kernel, S, J, NZ),
            out_shape=[near(S, BLK), near(NZ * Q, BLK)],
            in_specs=[VMEM] * 5,
            out_specs=[VMEM] * 2,
            compiler_params=params(8),
            name="dual",
        )(lp, dual_start, bounds_rhs, made["image"], from_section(made["image"]))
        return ((False, made["pieces"]), (False, made["bulk"]))

    got1 = exchange(send1, 88, image_work, dual_work)
    dual1, pieces2 = made["dual"], made["pieces"]
    others2 = from_rows(pieces2)

    an1, ml1, ent1, sums1 = pl.pallas_call(
        functools.partial(nodes_kernel, S, J, HB, devices),
        out_shape=[near(HB * Q, BLK)] * 2 + [near(HB, 2 * J * devices, BLK), near(8, BLK)],
        in_specs=[VMEM] * 6,
        out_specs=[VMEM] * 4,
        scratch_shapes=[
            pltpu.VMEM((2 * J * devices, hedged), F32),
        ],
        compiler_params=params(8),
        name="nodes",
    )(got1, ids, mu1, h1, ml, table)
    sums1b = from_section(sums1)

    p2, h2, mu2, send2, step2, pen1 = pl.pallas_call(
        functools.partial(second_kernel, *static),
        out_shape=step_out(message) + [near(8, BLK)],
        in_specs=[VMEM] * (13 + R - 1),
        out_specs=[VMEM] * 6,
        scratch_shapes=scratch,
        compiler_params=params(8),
        name="second",
    )(p1, pc, h1, hc, cb, ml1, an1, ids, wb, same, sums1, sums1b, pieces2, *others2)
    half = S // 2

    def place(first, count, whole, *into):
        cuts = max(p for p in (2, 1) if count % p == 0)
        return pl.pallas_call(
            functools.partial(place_kernel, *static, first, count, cuts),
            out_shape=[near(S, C * J, BLK), shape(S, C * J, BLK)],
            in_specs=[SMEM] + [VMEM] * 3 + [HBM] * len(into),
            out_specs=[VMEM, HBM],
            scratch_shapes=[pltpu.SemaphoreType.DMA((cuts,))],
            input_output_aliases={1: 0, 4: 1} if into else {1: 0},
            compiler_params=params(4),
            name="place",
        )(columns_of, whole, p2, h2, *into)

    def last_image_work():
        made["image"] = image_of(step2)
        return ((False, made["image"]),)

    def place_work():
        made["bulk"], made["out"] = place(0, half, made["bulk"])
        return ((True, made["out"]),)

    def rest_work():
        made["bulk"], made["out"] = place(half, S - half, made["bulk"], made["out"])
        return ((True, made["out"]),)

    got2 = exchange(send2, 0, last_image_work, place_work, rest_work)
    out, image2 = made["out"], made["image"]
    ml2, sums2 = pl.pallas_call(
        functools.partial(last_kernel, S, J, HB, devices),
        out_shape=[near(HB * Q, BLK), near(8, BLK)],
        in_specs=[VMEM] * 7,
        out_specs=[VMEM] * 2,
        compiler_params=params(8),
        name="last",
    )(got2, ids, ent1, mu2, h2, ml1, pen1)
    ml2, dual2 = pl.pallas_call(
        functools.partial(finish_kernel, S, J, HB),
        out_shape=[shape(S * HB * J, BLK), shape(S, BLK)],
        in_specs=[VMEM] * 5,
        out_specs=[VMEM] * 2,
        compiler_params=params(4),
        name="finish",
    )(ml2, dual1, bounds_rhs, image2, from_section(image2))
    pen2 = pl.pallas_call(
        penalty_kernel,
        out_shape=shape(1, 1),
        in_specs=[VMEM] * 3,
        out_specs=SMEM,
        compiler_params=params(4),
        name="penalty",
    )(pen1, sums2, from_section(sums2))

    return (
        uninterleave(out),
        dual2,
        uninterleave(ml2.reshape(S, HB * J, BLK)),
        pen2.reshape(()),
    )


def solution(mesh):
    sizes = tuple(mesh.shape[a] for a in ("scen", "rows", "section"))
    in_specs = (
        P("scen", "rows", "section", None, None, None),
        P("scen", None, "section", None),
        P(None, "scen"),
        P("scen"),
        P("scen", "section", None),
        P("scen", "rows"),
        P("scen", "section", None),
        P("scen", "rows"),
        P("scen", "section", None),
        P(),
    )
    out_specs = (P("scen", "section", None), P("scen", "rows"), P("scen", "section", None), P())
    return jax.shard_map(
        functools.partial(local, sizes),
        mesh=mesh,
        in_specs=in_specs,
        out_specs=out_specs,
        check_vma=False,
    )
```
